32 devices in a mesh: section: 4 (over y, core), batch: 8 (over z, x).
Axes of the slice: x: 2, y: 2, z: 4, core: 2. Of those that a mesh axis runs over, the one named last changes fastest.
Arguments:
- masters: float32 [32, 512, 1024], P('section', 'batch'), may hold values from -0.1875 to 0.1875
- first_moment: float32 [32, 512, 1024], P('section', 'batch')
- second_moment: float32 [32, 512, 1024], P('section', 'batch')
- section_table: float32 [8, 6144], P('section'), may hold values from -1.2 to 1.2
- table_first: float32 [8, 6144], P('section')
- table_second: float32 [8, 6144], P('section')
- owners: int32 [29], replicated, may hold values from 0 to 31, as said below
- step_count: int32 [1], replicated, may hold values from 2 to 20
- phones: int32 [64, 512], P(('section', 'batch')), may hold values from 0 to 511
- codes: int32 [64, 512, 8], P(('section', 'batch')), may hold values from 0 to 1023
- segments: int32 [64, 512], P(('section', 'batch')), may hold values from 0 to 2, never falling along the last dimension, each value on 1 to 384 neighbouring positions
- sections: int32 [64, 1], P(('section', 'batch')), may hold values from 0 to 7
- targets: int32 [64, 512], P(('section', 'batch')), may hold values from 0 to 1023
Outputs:
- new_masters: float32 [32, 512, 1024], P('section', 'batch')
- new_first: float32 [32, 512, 1024], P('section', 'batch')
- new_second: float32 [32, 512, 1024], P('section', 'batch')
- new_table: float32 [8, 6144], P('section')
- new_table_first: float32 [8, 6144], P('section')
- new_table_second: float32 [8, 6144], P('section')
- grad_norm: float32 [], replicated
- loss: float32 [], replicated
The draws below stay inside these ranges and needn't reach their ends.
Inputs may be any that keep to these rules, and one draw needn't show every extreme that they name: `owners`: distinct slot numbers; slot 0 and slot 31 are always among them; a section index of the slots owns a varying number of blocks. `sections`: every section is the section of some row; rows of one section may stand on any device.
All inputs are finite; a program needn't handle non-finite values.
Results may differ from the reference program's by a relative error of at most 0.0067.
Values may be sent and summed in bfloat16 or wider, within the bound.
A program may use at most 320 MiB of HBM per device.

```python
import math
import jax
import jax.numpy as jnp
import numpy as np
from jax import lax

D = 1024
HEADS = 16
HD = 64
FF = 4096
CODES = 1024
LEVELS = 8
PHONES = 512
ROW_LEN = 512
BLOCKS = 29
SECTIONS = 8
BLOCK_ROWS = 512
SLOTS = 32
ROWS = 64


clip_limit = 0.002


def entry_size():
    return clip_limit / math.sqrt(BLOCKS * BLOCK_ROWS * D + SECTIONS * 6 * D)


def first_draw(key, shape, size):
    return jax.random.normal(key, shape, jnp.float32) * (0.111 * size)


def second_draw(key, shape, size, lowest, highest):
    factor = jnp.exp(jax.random.uniform(key, shape, jnp.float32, math.log(lowest), math.log(highest)))
    return factor * (0.0526 * size * size)


def draw_first_moment(key, part):
    return first_draw(key, (SLOTS, BLOCK_ROWS, D), entry_size())


def draw_second_moment(key, part):
    return second_draw(key, (SLOTS, BLOCK_ROWS, D), entry_size(), 0.5, 8.0)


def draw_table_first(key, part):
    return first_draw(key, (SECTIONS, 6 * D), 0.5 * entry_size())


def draw_table_second(key, part):
    return second_draw(key, (SECTIONS, 6 * D), 0.5 * entry_size(), 1.0, 4.0)


def draw_owners(key, part):
    middle = jax.random.permutation(jax.random.fold_in(key, 11), SLOTS - 2)[:BLOCKS - 2].astype(jnp.int32) + 1
    ends = jnp.array([0, SLOTS - 1], dtype=jnp.int32)
    joined = jnp.concatenate([ends, middle])
    order = jax.random.permutation(jax.random.fold_in(key, 23), BLOCKS)
    return joined[order].astype(jnp.int32)


def plant(result, key, least, high):
    spot = [jax.random.randint(jax.random.fold_in(key, axis), (), 0, length) for axis, length in enumerate(result.shape)]
    main_axis = result.shape.index(max(result.shape))
    beside = spot[:main_axis] + [(spot[main_axis] + 1) % result.shape[main_axis]] + spot[main_axis + 1:]
    return result.at[tuple(spot)].set(least).at[tuple(beside)].set(high)


def steps_of(own_key, shape, pieces, low, largest):
    level = 1.0
    for dim, parts in pieces:
        steps = jax.random.uniform(jax.random.fold_in(jax.random.fold_in(own_key, 6), dim), (parts,), jnp.float32, low / len(pieces), largest / len(pieces))
        level = level * jnp.repeat(jnp.exp(steps), shape[dim] // parts).reshape((-1,) + (1,) * (len(shape) - 1 - dim))
    return level


def rank_bounds(amount, lean):
    weights = [(1 << 20) // math.isqrt(grade ** lean) + 1 for grade in range(1, amount + 1)]
    spread = 1 + sum(weights) // (1 << 30)
    return np.cumsum(np.array([max(1, weight // spread) for weight in weights]))


def ranked(rng, extent, amount, skew):
    listing = rank_bounds(amount, skew)
    ticket = jax.random.randint(jax.random.fold_in(rng, 1), extent, 0, int(listing[amount - 1]))
    grade = jnp.searchsorted(jnp.asarray(listing, jnp.int32), ticket, side="right")
    return jax.random.permutation(jax.random.fold_in(rng, 2), amount)[grade].astype(jnp.int32)


def different_ones(stream_key, rows, count, top, lift):
    sequence = jax.random.permutation(jax.random.fold_in(stream_key, 1), count)
    boost = sequence
    for power in range(3):
        boost = boost * boost // count
    boost = boost * lift // count
    chance = jax.random.randint(jax.random.fold_in(stream_key, 2), (rows, count), 0, 4096) + boost
    fixed_rows = jax.random.permutation(jax.random.fold_in(stream_key, 3), rows)[jnp.arange(count) % rows]
    chance = jnp.where(jnp.arange(rows)[:, None] == fixed_rows[None, :], 1 << 14, chance)
    merit = chance * count + jnp.arange(count)
    return lax.top_k(merit.astype(jnp.int32), top)[1].astype(jnp.int32)


def length_profile(count, total, most, lean):
    portions = [(1 << 20) // math.isqrt(grade ** lean) + 1 for grade in range(2, count + 1)]
    spare, holding = total - most - (count - 1), [1] * (count - 1)
    while spare > 0:
        movable = [i for i in range(count - 1) if holding[i] < most]
        whole, left = sum([portions[i] for i in movable]), spare
        for i in movable:
            more = min(most - holding[i], max(1, left * portions[i] // whole), spare)
            holding[i] = holding[i] + more
            spare = spare - more
    return np.array([most] + holding)


def uneven_parts(own_key, amount, total, most, lean):
    if amount == 2:
        one = jax.random.randint(own_key, (), max(1, total - most), min(most, total - 1) + 1)
        return jnp.stack([one, total - one])
    tallies = jnp.asarray(length_profile(amount, total, most, lean), jnp.int32)
    pairs = (amount - 1) // 2
    source_of, sink = tallies[1:1 + 2 * pairs:2], tallies[2:2 + 2 * pairs:2]
    slack = jnp.minimum(source_of - 1, most - sink)
    shifted = jax.random.randint(jax.random.fold_in(own_key, 1), (pairs,), 0, 1 << 20) % (slack + 1)
    tallies = tallies.at[1:1 + 2 * pairs:2].set(source_of - shifted).at[2:2 + 2 * pairs:2].set(sink + shifted)
    return tallies[jax.random.permutation(jax.random.fold_in(own_key, 2), amount)]


def normal_values(stream_key, dims, deviation, most, cuts=(), kind=jnp.bfloat16):
    drawn = deviation * jax.random.normal(stream_key, dims, jnp.float32)
    if cuts:
        drawn = drawn * steps_of(stream_key, dims, cuts, -0.22, 0.18)
    return jnp.clip(drawn, -most, most).astype(kind)


def setup_inputs(seed: int = 0) -> dict:
    key_list = jax.random.split(jax.random.key(seed), 14)
    return {
        "masters": normal_values(key_list[0], (SLOTS, BLOCK_ROWS, D), D ** -0.5, 0.1875, ((0, 4), (1, 8)), jnp.float32),
        "first_moment": draw_first_moment(jax.random.fold_in(key_list[13], 71), 0),
        "second_moment": draw_second_moment(jax.random.fold_in(key_list[13], 71), 0),
        "section_table": normal_values(key_list[3], (SECTIONS, 6 * D), 0.3, 1.2, ((0, 4),), jnp.float32),
        "table_first": draw_table_first(jax.random.fold_in(key_list[13], 71), 0),
        "table_second": draw_table_second(jax.random.fold_in(key_list[13], 71), 0),
        "owners": draw_owners(jax.random.fold_in(key_list[13], 71), 0),
        "step_count": jax.random.randint(key_list[7], (1,), 2, 21).astype(jnp.int32),
        "phones": plant(ranked(key_list[8], (ROWS, ROW_LEN), PHONES, 2), jax.random.fold_in(key_list[8], 3), 0, PHONES - 1).astype(jnp.int32),
        "codes": plant(jax.random.randint(key_list[9], (ROWS, ROW_LEN, LEVELS), 0, CODES), jax.random.fold_in(key_list[9], 1), 0, CODES - 1).astype(jnp.int32),
        "segments": jax.vmap(lambda own: jnp.searchsorted(jnp.cumsum(uneven_parts(own, 3, ROW_LEN, 3 * ROW_LEN // 4, 1)), jnp.arange(ROW_LEN), side="right"))(jax.random.split(key_list[10], ROWS)).reshape((ROWS, ROW_LEN)).astype(jnp.int32),
        "sections": different_ones(key_list[11], ROWS, SECTIONS, 1, 1024),
        "targets": plant(jax.random.randint(key_list[12], (ROWS, ROW_LEN), 0, CODES), jax.random.fold_in(key_list[12], 1), 0, CODES - 1).astype(jnp.int32),
    }


@jax.custom_vjp
def low(v):
    return lax.optimization_barrier(v.astype(jnp.bfloat16)).astype(jnp.float32)

@jax.custom_vjp
def low_back(v):
    return v

def low_keep(v):
    return (low(v), None)

def low_pass(kept, grad):
    return (grad,)

def back_keep(v):
    return (v, None)

def back_low(kept, grad):
    return (low(grad),)
low.defvjp(low_keep, low_pass)
low_back.defvjp(back_keep, back_low)
clip_limit = 0.002
learn_rate = 0.02
table_rate = 0.1
beta_one = 0.9
beta_two = 0.95
adam_eps = 1e-08
decay_rate = 0.1
norm_eps = 1e-05
pos_scale = 0.1
exact = lax.Precision.HIGHEST

def positions(segs):
    index = jnp.broadcast_to(jnp.arange(segs.shape[-1], dtype=jnp.int32), segs.shape)
    first = jnp.ones(segs.shape[:-1] + (1,), dtype=bool)
    change = jnp.concatenate([first, segs[..., 1:] != segs[..., :-1]], axis=-1)
    starts = lax.cummax(jnp.where(change, index, jnp.zeros_like(index)), axis=segs.ndim - 1)
    return (index - starts).astype(jnp.float32)

def sinusoid(place, width):
    column = jnp.arange(width)
    rate = jnp.exp(-(2 * (column // 2)).astype(jnp.float32) * (math.log(10000.0) / width))
    angle = place[..., None] * rate
    return pos_scale * jnp.where(column % 2 == 0, jnp.sin(angle), jnp.cos(angle))

def ada_norm(stream, gain, shift):
    centred = stream - lax.optimization_barrier(jnp.mean(stream, axis=-1, keepdims=True))
    scale = lax.rsqrt(lax.optimization_barrier(jnp.mean(centred * centred, axis=-1, keepdims=True)) + norm_eps)
    return centred * scale * (1.0 + gain) + shift

def unpack(blocks):
    half = blocks.shape[1]
    width = blocks.shape[2]
    code_w = blocks[0:2].reshape(2 * half, width)
    phone_w = blocks[2]
    head_w = blocks[3:5].reshape(width, 2 * half)
    qkv_w = blocks[5:11].reshape(3, width, width)
    out_w = blocks[11:13].reshape(width, width)
    up_w = blocks[13:21].reshape(4, width, width)
    down_w = blocks[21:29].reshape(4 * width, width)
    return (code_w, phone_w, head_w, qkv_w, out_w, up_w, down_w)

def row_loss(blocks, table, phone_row, code_row, seg_row, section, target_row):
    code_w, phone_w, head_w, qkv_w, out_w, up_w, down_w = unpack(blocks)
    length = seg_row.shape[0]
    params = jnp.split(table[section], 6)
    levels = (jnp.arange(LEVELS) <= section).astype(jnp.float32)
    multi = lax.optimization_barrier(jnp.sum((code_row[:, :, None] == jnp.arange(CODES)[None, None, :]).astype(jnp.float32) * levels[None, :, None], axis=1))
    phone_hot = (phone_row[:, None] == jnp.arange(PHONES)[None, :]).astype(jnp.float32)
    embedded = low_back(jnp.dot(multi, code_w, precision=exact) + jnp.dot(phone_hot, phone_w, precision=exact))
    stream = embedded + sinusoid(positions(seg_row), D)
    normed = low(ada_norm(stream, params[0], params[1]))
    qkv = low_back(low(jnp.einsum('ld,kde->kle', normed, qkv_w, precision=exact)))
    heads = qkv.reshape(3, length, HEADS, HD)
    scores = low_back(jnp.einsum('lhe,mhe->hlm', heads[0], heads[1], precision=exact) * HD ** (-0.5))
    same = seg_row[:, None] == seg_row[None, :]
    scores = jnp.where(same[None], scores, -1000000000.0)
    probs = low(jax.nn.softmax(scores, axis=-1))
    mixed = low_back(low(jnp.einsum('hlm,mhe->lhe', probs, heads[2], precision=exact).reshape(length, D)))
    stream = stream + low_back(jnp.dot(mixed, out_w, precision=exact))
    normed = low(ada_norm(stream, params[2], params[3]))
    hidden = low_back(jnp.einsum('ld,gde->lge', normed, up_w, precision=exact))
    active = low(jax.nn.gelu(hidden, approximate=False)).reshape(length, FF)
    stream = stream + low_back(jnp.dot(active, down_w, precision=exact))
    normed = low(ada_norm(stream, params[4], params[5]))
    logits = low_back(jnp.dot(normed, head_w, precision=exact))
    log_norm = jax.nn.logsumexp(logits, axis=-1)
    picked = lax.optimization_barrier(jnp.sum(logits * (target_row[:, None] == jnp.arange(CODES)[None, :]).astype(jnp.float32), axis=-1))
    return jnp.sum(log_norm - picked)

def adam(weight, first, second, grad, rate, step):
    new_first = beta_one * first + (1.0 - beta_one) * grad
    new_second = beta_two * second + (1.0 - beta_two) * grad * grad
    fix_one = 1.0 - jnp.power(beta_one, step)
    fix_two = 1.0 - jnp.power(beta_two, step)
    update = new_first / fix_one / (jnp.sqrt(new_second / fix_two) + adam_eps)
    return (weight - rate * (update + decay_rate * weight), new_first, new_second)

def reference(masters, first_moment, second_moment, section_table, table_first, table_second, owners, step_count, phones, codes, segments, sections, targets):
    rounded = lax.optimization_barrier(masters.astype(jnp.bfloat16)).astype(jnp.float32)
    blocks = jnp.take(rounded, owners, axis=0)
    section_ids = sections[:, 0]
    section_hot = (section_ids[:, None] == jnp.arange(SECTIONS)[None, :]).astype(jnp.float32)
    counts = lax.optimization_barrier(jnp.sum(section_hot, axis=0)) * ROW_LEN
    row_weight = lax.optimization_barrier(jnp.sum(section_hot / (SECTIONS * counts)[None, :], axis=1))

    def loss_of(block_args, table_arg):

        def one(total, row):
            phone_row, code_row, seg_row, section, target_row, weight = row
            value = jax.checkpoint(row_loss)(block_args, table_arg, phone_row, code_row, seg_row, section, target_row)
            return (total + weight * value, None)
        total, _ = lax.scan(one, jnp.zeros((), jnp.float32), (phones, codes, segments, section_ids, targets, row_weight))
        return total
    loss, pull = jax.vjp(loss_of, blocks, section_table)
    block_grad, table_grad = pull(jnp.ones((), jnp.float32))
    grad_norm = jnp.sqrt(jnp.sum(block_grad * block_grad) + jnp.sum(table_grad * table_grad))
    clip_factor = jnp.minimum(1.0, clip_limit / grad_norm)
    slot_grad = jnp.zeros(masters.shape, jnp.float32).at[owners].set(block_grad)
    step = step_count[0].astype(jnp.float32)
    new_masters, new_first, new_second = adam(masters, first_moment, second_moment, slot_grad * clip_factor, learn_rate, step)
    new_table, new_table_first, new_table_second = adam(section_table, table_first, table_second, table_grad * clip_factor, table_rate, step)
    return (new_masters, new_first, new_second, new_table, new_table_first, new_table_second, grad_norm, loss)
```

```python
import functools
import math

import jax
import jax.numpy as jnp
from jax import lax
from jax.experimental import pallas as pl
from jax.experimental.pallas import tpu as pltpu
from jax.sharding import PartitionSpec as P

D = 1024
HEADS = 16
HD = 64
FF = 4096
CODES = 1024
LEVELS = 8
PHONES = 512
SECTIONS = 8
CORES = 2

clip_limit = 0.002
learn_rate = 0.02
table_rate = 0.1
beta_one = 0.9
beta_two = 0.95
adam_eps = 1e-08
decay_rate = 0.1
norm_eps = 1e-05
pos_scale = 0.1
exact = lax.Precision.HIGHEST
float_out = jnp.float32
low = jnp.bfloat16
MESH = pl.DeviceIdType.MESH
MIB = 1 << 20


class Place:
    def __init__(self, mesh):
        self.groups = mesh.shape["section"]
        self.batch = mesh.shape["batch"]
        self.ny = self.groups // CORES
        self.nx = 1 << (int(math.log2(self.batch)) // 2)
        self.nz = self.batch // self.nx
        self.panel = D // self.groups
        self.half = D // CORES

    def here(self):
        self.s = lax.axis_index("section")
        self.j = lax.axis_index("batch")
        self.y = self.s // CORES
        self.c = self.s % CORES
        self.z = self.j // self.nx
        self.x = self.j % self.nx

    def panel_of(self, s):
        return (s % CORES) * self.ny + s // CORES

    def section_peer(self, d):
        return (self.s + d) % self.groups

    def x_of(self, d):
        return (self.x + d) % self.nx

    def y_of(self, d):
        return (self.y + d) % self.ny

    def z_of(self, d):
        return (self.z + d) % self.nz

    def at_x(self, d):
        return (self.s, self.z * self.nx + self.x_of(d))

    def at_y(self, d):
        return (self.y_of(d) * CORES + self.c, self.j)

    def at_z(self, d):
        return (self.s, self.z_of(d) * self.nx + self.x)

    def at_core(self):
        return (self.y * CORES + (1 - self.c), self.j)

    def columns(self, index, width):
        return pl.ds(pl.multiple_of(index * width, width), width)

    def barrier(self):
        sem = pltpu.get_barrier_semaphore()
        peers = [(self.section_peer(d), self.j) for d in range(1, self.groups)]
        peers += [self.at_x(d) for d in range(1, self.nx)]
        peers += [self.at_z(d) for d in range(1, self.nz)]
        for peer in peers:
            pl.semaphore_signal(sem, inc=1, device_id=peer, device_id_type=MESH)
        pl.semaphore_wait(sem, len(peers))

    def small_slots(self):
        return (self.groups - 1) + (self.nx - 1) + (self.nz - 1)

    def small_sum(self, value, sent, landed, send_sem, recv_sem):
        slot = 0
        stages = (
            (self.groups, lambda d: (self.section_peer(d), self.j)),
            (self.nx, self.at_x),
            (self.nz, self.at_z),
        )
        for stage, (count, target) in enumerate(stages):
            sent[stage] = value
            copies = []
            for d in range(1, count):
                copy = remote(
                    sent.at[stage], landed.at[slot], send_sem.at[slot], recv_sem.at[slot], target(d)
                )
                copy.start()
                copies.append((copy, slot))
                slot += 1
            for copy, _ in copies:
                copy.wait()
            for _, where in copies:
                value = value + landed[where]
        return value


def remote(src, dst, send_sem, recv_sem, device):
    return pltpu.make_async_remote_copy(
        src_ref=src,
        dst_ref=dst,
        send_sem=send_sem,
        recv_sem=recv_sem,
        device_id=device,
        device_id_type=MESH,
    )


def gather_kernel(
    pc,
    owners_ref,
    masters_ref,
    table_ref,
    counts_ref,
    w_ref,
    table_out,
    counts_out,
    rounded,
    slots,
    pieces,
    sent,
    landed,
    a_send,
    a_recv,
    t_send,
    t_recv,
    own_sem,
    z_send,
    z_recv,
    e_send,
    e_recv,
    f_send,
    f_recv,
    c_send,
    c_recv,
    m_send,
    m_recv,
):
    pc.here()
    blocks = w_ref.shape[0]
    per_group = masters_ref.shape[0]
    own_sections = table_ref.shape[0]
    mine = pc.columns(pc.panel_of(pc.s), pc.panel)
    core_half = pc.columns(pc.c, pc.half)
    pc.barrier()
    rounded[...] = masters_ref[...].astype(low)
    starts = []
    for d in range(1, pc.groups):
        peer = pc.section_peer(d)
        columns = pc.columns(pc.panel_of(peer), pc.panel)
        copy = remote(
            rounded.at[:, :, columns],
            slots.at[pl.ds(pc.s * per_group, per_group)],
            a_send.at[d - 1],
            a_recv.at[d - 1],
            (peer, pc.j),
        )
        copy.start()
        starts.append(copy)
        copy = remote(
            table_ref,
            table_out.at[pl.ds(pc.s * own_sections, own_sections)],
            t_send.at[d - 1],
            t_recv.at[d - 1],
            (peer, pc.j),
        )
        copy.start()
        starts.append(copy)
    table_out[pl.ds(pc.s * own_sections, own_sections)] = table_ref[...]
    slots[pl.ds(pc.s * per_group, per_group)] = rounded[:, :, mine]
    counts_out[...] = pc.small_sum(counts_ref[...], sent, landed, m_send, m_recv)
    for copy in starts:
        copy.wait()
    for b in range(blocks):
        pieces[b] = slots[owners_ref[b]]

    def own(b):
        return pltpu.make_async_copy(
            pieces.at[b], w_ref.at[b, pc.z, pc.x, :, mine], own_sem.at[b]
        )

    def along_z(b):
        return [
            remote(
                pieces.at[b],
                w_ref.at[b, pc.z, pc.x, :, mine],
                z_send.at[b, d - 1],
                z_recv.at[b, d - 1],
                pc.at_z(d),
            )
            for d in range(1, pc.nz)
        ]

    def first_x(b):
        part = w_ref.at[b, :, pc.x, :, mine]
        return [
            remote(part, part, e_send.at[b, d - 1], e_recv.at[b, d - 1], pc.at_x(d))
            for d in range(1, pc.nx)
        ]

    def first_y(b):
        part = w_ref.at[b, :, pc.x, :, mine]
        return [
            remote(part, part, e_send.at[b, d - 1], e_recv.at[b, d - 1], pc.at_y(d))
            for d in range(1, pc.ny)
        ]

    def then_y(b):
        part = w_ref.at[b, :, :, :, mine]
        return [
            remote(part, part, f_send.at[b, d - 1], f_recv.at[b, d - 1], pc.at_y(d))
            for d in range(1, pc.ny)
        ]

    def then_x(b):
        part = w_ref.at[b, :, pc.x, :, core_half]
        return [
            remote(part, part, f_send.at[b, d - 1], f_recv.at[b, d - 1], pc.at_x(d))
            for d in range(1, pc.nx)
        ]

    def to_core(b):
        part = w_ref.at[b, :, :, :, core_half]
        return [remote(part, part, c_send.at[b], c_recv.at[b], pc.at_core())]

    def begin(copies):
        for copy in copies:
            copy.start()

    def landed_all(copies):
        for copy in copies:
            copy.wait_recv()

    def gone(copies):
        for copy in copies:
            copy.wait_send()

    def by_parity(b, even, odd, act):
        @pl.when(b % 2 == 0)
        def _():
            act(even(b))

        @pl.when(b % 2 == 1)
        def _():
            act(odd(b))

    ahead = 4

    def launch(b, carry):
        own(b).start()
        begin(along_z(b))
        return carry

    lax.fori_loop(0, min(ahead, blocks), launch, 0)

    def tick(t, carry):
        @pl.when(t + ahead < blocks)
        def _():
            launch(t + ahead, 0)

        @pl.when(t < blocks)
        def _():
            own(t).wait()
            landed_all(along_z(t))
            by_parity(t, first_x, first_y, begin)

        b = t - 2

        @pl.when((b >= 0) & (b < blocks))
        def _():
            by_parity(b, first_x, first_y, landed_all)
            by_parity(b, then_y, then_x, begin)

        e = t - 4

        @pl.when((e >= 0) & (e < blocks))
        def _():
            by_parity(e, then_y, then_x, landed_all)
            begin(to_core(e))

        return carry

    lax.fori_loop(0, blocks + 4, tick, 0)

    def finish(b, carry):
        landed_all(to_core(b))
        gone(to_core(b))
        gone(along_z(b))
        by_parity(b, first_x, first_y, gone)
        by_parity(b, then_y, then_x, gone)
        return carry

    lax.fori_loop(0, blocks, finish, 0)


def gather_weights(pc, masters, table, counts, owners):
    per_group, rows, _ = masters.shape
    blocks = owners.shape[0]
    own_sections = table.shape[0]
    hops = max(pc.nx, pc.ny) - 1
    dma = pltpu.SemaphoreType.DMA
    vmem = pl.BlockSpec(memory_space=pltpu.VMEM)
    w, table_all, counts_all = pl.pallas_call(
        functools.partial(gather_kernel, pc),
        out_shape=(
            jax.ShapeDtypeStruct((blocks, pc.nz, pc.nx, rows, D), low),
            jax.ShapeDtypeStruct((own_sections * pc.groups, 8, D), float_out),
            jax.ShapeDtypeStruct((8, 128), float_out),
        ),
        in_specs=[pl.BlockSpec(memory_space=pltpu.SMEM), vmem, vmem, vmem],
        out_specs=(pl.BlockSpec(memory_space=pl.ANY), vmem, vmem),
        scratch_shapes=[
            pltpu.VMEM((per_group, rows, D), low),
            pltpu.VMEM((per_group * pc.groups, rows, pc.panel), low),
            pltpu.VMEM((blocks, rows, pc.panel), low),
            pltpu.VMEM((3, 8, 128), float_out),
            pltpu.VMEM((pc.small_slots(), 8, 128), float_out),
            dma((pc.groups - 1,)),
            dma((pc.groups - 1,)),
            dma((pc.groups - 1,)),
            dma((pc.groups - 1,)),
            dma((blocks,)),
            dma((blocks, pc.nz - 1)),
            dma((blocks, pc.nz - 1)),
            dma((blocks, hops)),
            dma((blocks, hops)),
            dma((blocks, hops)),
            dma((blocks, hops)),
            dma((blocks,)),
            dma((blocks,)),
            dma((pc.small_slots(),)),
            dma((pc.small_slots(),)),
        ],
        name="gather_weights",
        compiler_params=pltpu.CompilerParams(
            collective_id=0, has_side_effects=True, vmem_limit_bytes=24 * MIB
        ),
    )(owners, masters, table, counts)
    return w.reshape(blocks, pc.nz * pc.nx * rows, D), table_all, counts_all


def reduce_kernel(pc, sources, *refs):
    count_in = len({s for s in sources for s in (s[0], s[2])})
    block_of_ref = refs[0]
    arrays = refs[1 : 1 + count_in]
    table_ref, loss_ref = refs[1 + count_in : 3 + count_in]
    out_ref, table_out, sums_out = refs[3 + count_in : 6 + count_in]
    (
        x_buf,
        y_buf,
        own_half,
        send_half,
        core_in,
        first_a,
        first_b,
        then_a,
        then_b,
        z_in,
        final,
        by_slot,
        square,
        table_in,
        table_mid,
        sent,
        landed,
        in_sem,
        c_send,
        c_recv,
        e_send,
        e_recv,
        f_send,
        f_recv,
        z_send,
        z_recv,
        a_send,
        a_recv,
        o_sem,
        t_send,
        t_recv,
        m_send,
        m_recv,
    ) = refs[6 + count_in :]
    pc.here()
    blocks = len(sources)
    per_group = out_ref.shape[0]
    own_sections = table_out.shape[0]
    rows = out_ref.shape[1]
    width = x_buf.shape[2]
    keep = pc.columns(pc.c, pc.half)
    away = pc.columns(1 - pc.c, pc.half)
    pc.barrier()

    def fetch(t, act):
        for b, (xs, xc, ys, yc) in enumerate(sources):

            @pl.when(t == b)
            def _(xs=xs, xc=xc, ys=ys, yc=yc, b=b):
                slot = b % 2
                x_src = arrays[xs].at[xc[0], :, pl.ds(xc[1], width)]
                y_src = arrays[ys].at[yc]
                act(pltpu.make_async_copy(x_src, x_buf.at[slot], in_sem.at[slot, 0]))
                act(pltpu.make_async_copy(y_src, y_buf.at[slot], in_sem.at[slot, 1]))

    def to_core(b):
        return [
            remote(
                send_half.at[b % 4], core_in.at[b], c_send.at[b], c_recv.at[b], pc.at_core()
            )
        ]

    def first_x(b):
        return [
            remote(
                core_in.at[b, :, pc.x_of(d)],
                first_a.at[b // 2, d - 1],
                e_send.at[b, d - 1],
                e_recv.at[b, d - 1],
                pc.at_x(d),
            )
            for d in range(1, pc.nx)
        ]

    def first_y(b):
        return [
            remote(
                core_in.at[b, :, :, :, pc.columns(pc.y_of(d), pc.panel)],
                first_b.at[b // 2, d - 1],
                e_send.at[b, d - 1],
                e_recv.at[b, d - 1],
                pc.at_y(d),
            )
            for d in range(1, pc.ny)
        ]

    def then_y(b):
        return [
            remote(
                first_a.at[b // 2, 0, :, :, pc.columns(pc.y_of(d), pc.panel)],
                then_a.at[b // 2, d - 1],
                f_send.at[b, d - 1],
                f_recv.at[b, d - 1],
                pc.at_y(d),
            )
            for d in range(1, pc.ny)
        ]

    def then_x(b):
        return [
            remote(
                first_b.at[b // 2, 0, :, pc.x_of(d)],
                then_b.at[b // 2, d - 1],
                f_send.at[b, d - 1],
                f_recv.at[b, d - 1],
                pc.at_x(d),
            )
            for d in range(1, pc.nx)
        ]

    def along_z(b, source):
        return [
            remote(
                source.at[b // 2, 0, pc.z_of(d)],
                z_in.at[b, d - 1],
                z_send.at[b, d - 1],
                z_recv.at[b, d - 1],
                pc.at_z(d),
            )
            for d in range(1, pc.nz)
        ]

    def begin(copies):
        for copy in copies:
            copy.start()

    def landed_all(copies):
        for copy in copies:
            copy.wait_recv()

    def gone(copies):
        for copy in copies:
            copy.wait_send()

    table_stage = []
    for d in range(1, pc.groups):
        peer = pc.section_peer(d)
        table_stage.append(
            remote(
                table_ref.at[pl.ds(peer * own_sections, own_sections)],
                table_in.at[d - 1],
                t_send.at[d - 1],
                t_recv.at[d - 1],
                (peer, pc.j),
            )
        )
    begin(table_stage)
    square[...] = jnp.zeros_like(square)
    final[blocks] = jnp.zeros(final.shape[1:], low)
    fetch(0, lambda copy: copy.start())

    def tick(t, carry):
        @pl.when(t + 1 < blocks)
        def _():
            fetch(t + 1, lambda copy: copy.start())

        @pl.when(t < blocks)
        def _():
            fetch(t, lambda copy: copy.wait())
            slot = t % 2
            own_half[slot] = lax.dot_general(
                x_buf[slot],
                y_buf[slot, :, keep],
                (((0,), (0,)), ((), ())),
                preferred_element_type=float_out,
            )

            @pl.when(t >= 4)
            def _():
                gone(to_core(t - 4))

            send_half[t % 4] = (
                lax.dot_general(
                    x_buf[slot],
                    y_buf[slot, :, away],
                    (((0,), (0,)), ((), ())),
                    preferred_element_type=float_out,
                )
                .astype(low)
                .reshape(send_half.shape[1:])
            )
            begin(to_core(t))

        b = t - 1

        @pl.when((b >= 0) & (b < blocks))
        def _():
            landed_all(to_core(b))
            core_in[b] = (
                core_in[b].astype(float_out) + own_half[b % 2].reshape(core_in.shape[1:])
            ).astype(low)

            @pl.when(b % 2 == 0)
            def _():
                begin(first_x(b))

            @pl.when(b % 2 == 1)
            def _():
                begin(first_y(b))

        e = t - 3

        @pl.when((e >= 0) & (e < blocks))
        def _():
            @pl.when(e % 2 == 0)
            def _():
                landed_all(first_x(e))
                total = core_in[e, :, pc.x].astype(float_out)
                for d in range(pc.nx - 1):
                    total = total + first_a[e // 2, d].astype(float_out)
                first_a[e // 2, 0] = total.astype(low)
                begin(then_y(e))

            @pl.when(e % 2 == 1)
            def _():
                landed_all(first_y(e))
                total = core_in[e, :, :, :, pc.columns(pc.y, pc.panel)].astype(float_out)
                for d in range(pc.ny - 1):
                    total = total + first_b[e // 2, d].astype(float_out)
                first_b[e // 2, 0] = total.astype(low)
                begin(then_x(e))

        f = t - 5

        @pl.when((f >= 0) & (f < blocks))
        def _():
            @pl.when(f % 2 == 0)
            def _():
                landed_all(then_y(f))
                total = first_a[f // 2, 0, :, :, pc.columns(pc.y, pc.panel)].astype(float_out)
                for d in range(pc.ny - 1):
                    total = total + then_a[f // 2, d].astype(float_out)
                then_a[f // 2, 0] = total.astype(low)
                begin(along_z(f, then_a))

            @pl.when(f % 2 == 1)
            def _():
                landed_all(then_x(f))
                total = first_b[f // 2, 0, :, pc.x].astype(float_out)
                for d in range(pc.nx - 1):
                    total = total + then_b[f // 2, d].astype(float_out)
                then_b[f // 2, 0] = total.astype(low)
                begin(along_z(f, then_b))

        g = t - 7

        @pl.when((g >= 0) & (g < blocks))
        def _():
            def close(source):
                landed_all(along_z(g, source))
                total = source[g // 2, 0, pc.z].astype(float_out)
                for d in range(pc.nz - 1):
                    total = total + z_in[g, d].astype(float_out)
                rounded = total.astype(low)
                final[g] = rounded
                wide = rounded.astype(float_out)
                square[...] += jnp.sum(wide * wide, axis=0, keepdims=True)

            @pl.when(g % 2 == 0)
            def _():
                close(then_a)

            @pl.when(g % 2 == 1)
            def _():
                close(then_b)

        return carry

    lax.fori_loop(0, blocks + 7, tick, 0)

    for i in range(per_group * pc.groups):
        by_slot[i] = final[block_of_ref[i]]
    mine = pc.columns(pc.panel_of(pc.s), pc.panel)
    ends = []
    for d in range(1, pc.groups):
        peer = pc.section_peer(d)
        ends.append(
            remote(
                by_slot.at[pl.ds(peer * per_group, per_group)],
                out_ref.at[:, :, mine],
                a_send.at[d - 1],
                a_recv.at[d - 1],
                (peer, pc.j),
            )
        )
    begin(ends)
    own = pltpu.make_async_copy(
        by_slot.at[pl.ds(pc.s * per_group, per_group)], out_ref.at[:, :, mine], o_sem
    )
    own.start()

    for copy in table_stage:
        copy.wait()
    total = table_ref[pl.ds(pc.s * own_sections, own_sections)]
    for d in range(pc.groups - 1):
        total = total + table_in[d]
    slot = pc.groups - 1
    for stage, (count, target) in enumerate(((pc.nx, pc.at_x), (pc.nz, pc.at_z))):
        table_mid[stage] = total
        copies = []
        for d in range(1, count):
            copies.append(
                (
                    remote(
                        table_mid.at[stage],
                        table_in.at[slot],
                        t_send.at[slot],
                        t_recv.at[slot],
                        target(d),
                    ),
                    slot,
                )
            )
            slot += 1
        begin([copy for copy, _ in copies])
        for copy, _ in copies:
            copy.wait()
        for _, where in copies:
            total = total + table_in[where]
    table_out[...] = total

    table_square = jnp.sum(total * total) / pc.batch
    lane = lax.broadcasted_iota(jnp.int32, (8, 128), 1)
    part = jnp.where(lane == 0, jnp.sum(square[...]) + table_square, loss_ref[...])
    sums_out[...] = pc.small_sum(part, sent, landed, m_send, m_recv)
    for copy in ends:
        copy.wait()
    own.wait()

    def finish(b, carry):
        gone(to_core(b))
        return carry

    lax.fori_loop(max(blocks - 4, 0), blocks, finish, 0)

    def finish_rest(b, carry):
        @pl.when(b % 2 == 0)
        def _():
            gone(first_x(b))
            gone(then_y(b))
            gone(along_z(b, then_a))

        @pl.when(b % 2 == 1)
        def _():
            gone(first_y(b))
            gone(then_x(b))
            gone(along_z(b, then_b))

        return carry

    lax.fori_loop(0, blocks, finish_rest, 0)


def reduce_grads(pc, arrays, sources, table, loss, block_of, per_group):
    blocks = len(sources)
    positions = arrays[0].shape[1]
    width = D // 2
    rows = width // pc.batch
    own_sections = SECTIONS // pc.groups
    hops = max(pc.nx, pc.ny) - 1
    evens, odds = (blocks + 1) // 2, blocks // 2
    steps = pc.small_slots()
    dma = pltpu.SemaphoreType.DMA
    vmem = pl.BlockSpec(memory_space=pltpu.VMEM)
    anyspace = pl.BlockSpec(memory_space=pl.ANY)
    nz, nx, ny, half, panel = pc.nz, pc.nx, pc.ny, pc.half, pc.panel
    return pl.pallas_call(
        functools.partial(reduce_kernel, pc, sources),
        out_shape=(
            jax.ShapeDtypeStruct((per_group, rows, D), low),
            jax.ShapeDtypeStruct((own_sections, 8, D), float_out),
            jax.ShapeDtypeStruct((8, 128), float_out),
        ),
        in_specs=[pl.BlockSpec(memory_space=pltpu.SMEM)] + [anyspace] * len(arrays) + [vmem, vmem],
        out_specs=(vmem, vmem, vmem),
        scratch_shapes=[
            pltpu.VMEM((2, positions, width), low),
            pltpu.VMEM((2, positions, D), low),
            pltpu.VMEM((2, width, half), float_out),
            pltpu.VMEM((4, nz, nx, rows, half), low),
            pltpu.VMEM((blocks, nz, nx, rows, half), low),
            pltpu.VMEM((evens, nx - 1, nz, rows, half), low),
            pltpu.VMEM((odds, ny - 1, nz, nx, rows, panel), low),
            pltpu.VMEM((evens, ny - 1, nz, rows, panel), low),
            pltpu.VMEM((odds, nx - 1, nz, rows, panel), low),
            pltpu.VMEM((blocks, nz - 1, rows, panel), low),
            pltpu.VMEM((blocks + 1, rows, panel), low),
            pltpu.VMEM((per_group * pc.groups, rows, panel), low),
            pltpu.VMEM((1, panel), float_out),
            pltpu.VMEM((steps, own_sections, 8, D), float_out),
            pltpu.VMEM((2, own_sections, 8, D), float_out),
            pltpu.VMEM((3, 8, 128), float_out),
            pltpu.VMEM((steps, 8, 128), float_out),
            dma((2, 2)),
            dma((blocks,)),
            dma((blocks,)),
            dma((blocks, hops)),
            dma((blocks, hops)),
            dma((blocks, hops)),
            dma((blocks, hops)),
            dma((blocks, nz - 1)),
            dma((blocks, nz - 1)),
            dma((pc.groups - 1,)),
            dma((pc.groups - 1,)),
            dma,
            dma((steps,)),
            dma((steps,)),
            dma((steps,)),
            dma((steps,)),
        ],
        name="reduce_grads",
        compiler_params=pltpu.CompilerParams(
            collective_id=1, has_side_effects=True, vmem_limit_bytes=56 * MIB
        ),
    )(block_of, *arrays, table, loss)


def positions(segs):
    index = jnp.arange(segs.shape[-1], dtype=jnp.int32)
    same = segs[..., :, None] == segs[..., None, :]
    starts = jnp.min(jnp.where(same, index, segs.shape[-1]), axis=-1)
    return (index - starts).astype(jnp.float32)


def sinusoid(place, width):
    column = jnp.arange(width)
    rate = jnp.exp(-(2 * (column // 2)).astype(jnp.float32) * (math.log(10000.0) / width))
    angle = place[..., None] * rate
    return pos_scale * jnp.where(column % 2 == 0, jnp.sin(angle), jnp.cos(angle))


def normalize(stream):
    centred = stream - jnp.mean(stream, axis=-1, keepdims=True)
    scale = lax.rsqrt(jnp.mean(centred * centred, axis=-1, keepdims=True) + norm_eps)
    return (centred * scale, scale)


def norm_back(grad, normed, scale, gain):
    inner = grad * (1.0 + gain)
    result = scale * (
        inner
        - jnp.mean(inner, axis=-1, keepdims=True)
        - normed * jnp.mean(inner * normed, axis=-1, keepdims=True)
    )
    return (result, jnp.sum(grad * normed, axis=1), jnp.sum(grad, axis=1))


def unpack(blocks):
    half = blocks.shape[1]
    width = blocks.shape[2]
    code_w = blocks[0:2].reshape(2 * half, width)
    phone_w = blocks[2]
    head_w = blocks[3:5].reshape(width, 2 * half)
    qkv_w = blocks[5:11].reshape(3, width, width)
    out_w = blocks[11:13].reshape(width, width)
    up_w = blocks[13:21].reshape(4, width, width)
    down_w = blocks[21:29].reshape(4, width, width)
    return (code_w, phone_w, head_w, qkv_w, out_w, up_w, down_w)


def attend_scores(queries, key_vecs, same):
    scores = jnp.einsum(
        "rlhe,rmhe->rhlm", queries, key_vecs, preferred_element_type=float_out
    ) * HD ** (-0.5)
    return jnp.where(same[:, None], scores, -1000000000.0)


def forward(matrices, params, phones, codes, segments, section_ids, targets):
    code_w, phone_w, head_w, qkv_w, out_w, up_w, down_w = matrices
    rows, length = segments.shape
    levels = (jnp.arange(LEVELS)[None, :] <= section_ids[:, None]).astype(jnp.bfloat16)
    vocab = jnp.arange(CODES)
    multi = jnp.zeros((rows, length, CODES), jnp.bfloat16)
    for level in range(LEVELS):
        multi = (
            multi
            + (codes[:, :, level, None] == vocab).astype(jnp.bfloat16)
            * levels[:, level, None, None]
        )
    phone_hot = (phones[:, :, None] == jnp.arange(PHONES)).astype(jnp.bfloat16)
    stream = jnp.einsum("rlc,cd->rld", multi, code_w, preferred_element_type=float_out)
    stream = stream + jnp.einsum(
        "rlp,pd->rld", phone_hot, phone_w, preferred_element_type=float_out
    )
    stream = stream + sinusoid(positions(segments), D)
    normed_one, scale_one = normalize(stream)
    input_one = (normed_one * (1.0 + params[:, 0]) + params[:, 1]).astype(jnp.bfloat16)
    qkv = jnp.einsum("rld,kde->krle", input_one, qkv_w, preferred_element_type=float_out).astype(
        jnp.bfloat16
    )
    heads = qkv.reshape(3, rows, length, HEADS, HD)
    same = segments[:, :, None] == segments[:, None, :]
    scores = attend_scores(heads[0], heads[1], same)
    log_total = jax.nn.logsumexp(scores, axis=-1)
    probs = jnp.exp(scores - log_total[..., None]).astype(jnp.bfloat16)
    mixed = jnp.einsum("rhlm,rmhe->rlhe", probs, heads[2], preferred_element_type=float_out)
    mixed = mixed.astype(jnp.bfloat16).reshape(rows, length, D)
    stream = stream + jnp.einsum("rld,de->rle", mixed, out_w, preferred_element_type=float_out)
    normed_two, scale_two = normalize(stream)
    input_two = (normed_two * (1.0 + params[:, 2]) + params[:, 3]).astype(jnp.bfloat16)
    hidden = jnp.einsum("rld,gde->grle", input_two, up_w, preferred_element_type=float_out)
    active = jax.nn.gelu(hidden, approximate=False).astype(jnp.bfloat16)
    stream = stream + jnp.einsum("grle,ged->rld", active, down_w, preferred_element_type=float_out)
    normed_three, scale_three = normalize(stream)
    input_three = (normed_three * (1.0 + params[:, 4]) + params[:, 5]).astype(jnp.bfloat16)
    logits = jnp.einsum("rld,dc->rlc", input_three, head_w, preferred_element_type=float_out)
    log_norm = jax.nn.logsumexp(logits, axis=-1)
    target_hot = (targets[:, :, None] == vocab).astype(jnp.float32)
    losses = log_norm - jnp.sum(logits * target_hot, axis=-1)
    kept = (
        multi,
        phone_hot,
        normed_one,
        scale_one,
        input_one,
        heads,
        same,
        log_total,
        mixed,
        normed_two,
        scale_two,
        input_two,
        hidden,
        active,
        normed_three,
        scale_three,
        input_three,
        logits,
        log_norm,
        target_hot,
    )
    return (kept, jnp.sum(losses, axis=1))


def backward(matrices, params, kept, row_weight):
    code_w, phone_w, head_w, qkv_w, out_w, up_w, down_w = matrices
    (
        multi,
        phone_hot,
        normed_one,
        scale_one,
        input_one,
        heads,
        same,
        log_total,
        mixed,
        normed_two,
        scale_two,
        input_two,
        hidden,
        active,
        normed_three,
        scale_three,
        input_three,
        logits,
        log_norm,
        target_hot,
    ) = kept
    rows, length = (same.shape[0], same.shape[1])
    predicted = jnp.exp(logits - log_norm[..., None])
    grad_logits = ((predicted - target_hot) * row_weight[:, None, None]).astype(jnp.bfloat16)
    grad_three = jnp.einsum("rlc,dc->rld", grad_logits, head_w, preferred_element_type=float_out)
    grad_stream, gain_three, shift_three = norm_back(
        grad_three, normed_three, scale_three, params[:, 4]
    )
    grad_ffn = grad_stream.astype(jnp.bfloat16)
    grad_active = jnp.einsum("rld,ged->grle", grad_ffn, down_w, preferred_element_type=float_out)
    _, gelu_pull = jax.vjp(lambda value: jax.nn.gelu(value, approximate=False), hidden)
    grad_hidden = gelu_pull(grad_active)[0].astype(jnp.bfloat16)
    grad_two = jnp.einsum("grle,gde->rld", grad_hidden, up_w, preferred_element_type=float_out)
    grad_norm_two, gain_two, shift_two = norm_back(grad_two, normed_two, scale_two, params[:, 2])
    grad_stream = grad_stream + grad_norm_two
    grad_attn = grad_stream.astype(jnp.bfloat16)
    grad_mixed = jnp.einsum("rle,de->rld", grad_attn, out_w, preferred_element_type=float_out)
    grad_mixed = grad_mixed.astype(jnp.bfloat16).reshape(rows, length, HEADS, HD)
    scores = attend_scores(heads[0], heads[1], same)
    probs = jnp.exp(scores - log_total[..., None])
    probs_low = probs.astype(jnp.bfloat16)
    grad_values = jnp.einsum(
        "rhlm,rlhe->rmhe", probs_low, grad_mixed, preferred_element_type=float_out
    )
    grad_probs = jnp.einsum(
        "rlhe,rmhe->rhlm", grad_mixed, heads[2], preferred_element_type=float_out
    )
    grad_scores = (
        probs * (grad_probs - jnp.sum(probs * grad_probs, axis=-1, keepdims=True))
    ).astype(jnp.bfloat16)
    grad_queries = jnp.einsum(
        "rhlm,rmhe->rlhe", grad_scores, heads[1], preferred_element_type=float_out
    ) * HD ** (-0.5)
    grad_key_vecs = jnp.einsum(
        "rhlm,rlhe->rmhe", grad_scores, heads[0], preferred_element_type=float_out
    ) * HD ** (-0.5)
    grad_qkv = (
        jnp.stack([grad_queries, grad_key_vecs, grad_values])
        .reshape(3, rows, length, D)
        .astype(jnp.bfloat16)
    )
    grad_one = jnp.einsum("krle,kde->rld", grad_qkv, qkv_w, preferred_element_type=float_out)
    grad_norm_one, gain_one, shift_one = norm_back(grad_one, normed_one, scale_one, params[:, 0])
    grad_embed = (grad_stream + grad_norm_one).astype(jnp.bfloat16)
    row_grads = jnp.stack(
        [gain_one, shift_one, gain_two, shift_two, gain_three, shift_three], axis=1
    )
    flat = (-1, rows * length)
    arrays = [
        multi.reshape(*flat, CODES),
        phone_hot.reshape(*flat, PHONES),
        input_three.reshape(*flat, D),
        input_one.reshape(*flat, D),
        mixed.reshape(*flat, D),
        input_two.reshape(*flat, D),
        active.reshape(*flat, D),
        grad_embed.reshape(*flat, D),
        grad_logits.reshape(*flat, CODES),
        grad_qkv.reshape(*flat, D),
        grad_attn.reshape(*flat, D),
        grad_hidden.reshape(*flat, D),
        grad_ffn.reshape(*flat, D),
    ]
    return arrays, row_grads


def block_sources():
    half = D // 2
    made = [(0, (0, 0), 7, 0), (0, (0, half), 7, 0), (1, (0, 0), 7, 0)]
    made += [(2, (0, i * half), 8, 0) for i in range(2)]
    made += [(3, (0, i * half), 9, k) for k in range(3) for i in range(2)]
    made += [(4, (0, i * half), 10, 0) for i in range(2)]
    made += [(5, (0, i * half), 11, g) for g in range(4) for i in range(2)]
    made += [(6, (g, i * half), 12, 0) for g in range(4) for i in range(2)]
    return tuple(made)


def adam(weight, first, second, grad, rate, step):
    new_first = beta_one * first + (1.0 - beta_one) * grad
    new_second = beta_two * second + (1.0 - beta_two) * grad * grad
    fix_one = 1.0 - jnp.power(beta_one, step)
    fix_two = 1.0 - jnp.power(beta_two, step)
    update = new_first / fix_one / (jnp.sqrt(new_second / fix_two) + adam_eps)
    return (weight - rate * (update + decay_rate * weight), new_first, new_second)


def per_device(
    pc,
    masters,
    first_moment,
    second_moment,
    section_table,
    table_first,
    table_second,
    owners,
    step_count,
    phones,
    codes,
    segments,
    sections,
    targets,
):
    section_ids = sections[:, 0]
    row_count = section_ids.shape[0]
    own_sections = section_table.shape[0]
    section_hot = (section_ids[:, None] == jnp.arange(SECTIONS)[None, :]).astype(jnp.float32)
    local_counts = jnp.sum(section_hot, axis=0) * segments.shape[1]
    padded = jnp.pad(section_table.reshape(own_sections, 6, D), ((0, 0), (0, 2), (0, 0)))
    blocks, table, counts = gather_weights(
        pc, masters, padded, jnp.broadcast_to(local_counts[:, None], (SECTIONS, 128)), owners
    )
    counts = counts[:, 0]
    matrices = unpack(blocks)
    params = jnp.einsum(
        "rs,sk->rk", section_hot, table[:, :6].reshape(SECTIONS, 6 * D), precision=exact
    ).reshape(row_count, 6, 1, D)
    kept, row_losses = forward(
        matrices, params, phones, codes, segments, section_ids, targets
    )
    row_weight = jnp.sum(section_hot / (SECTIONS * counts)[None, :], axis=1)
    arrays, row_grads = backward(matrices, params, kept, row_weight)
    table_local = jnp.einsum(
        "rs,rk->sk", section_hot, row_grads.reshape(row_count, 6 * D), precision=exact
    )
    table_local = jnp.pad(table_local.reshape(SECTIONS, 6, D), ((0, 0), (0, 2), (0, 0)))
    loss_part = jnp.broadcast_to(jnp.sum(row_weight * row_losses), (8, 128))
    slot_ids = jnp.arange(masters.shape[0] * pc.groups)
    held = owners[None, :] == slot_ids[:, None]
    block_of = jnp.min(jnp.where(held, jnp.arange(owners.shape[0]), owners.shape[0]), axis=1)
    own_grad, table_grad, sums = reduce_grads(
        pc, arrays, block_sources(), table_local, loss_part, block_of, masters.shape[0]
    )
    own_grad = own_grad.astype(jnp.float32)
    table_grad = table_grad[:, :6].reshape(own_sections, 6 * D)
    grad_norm = jnp.sqrt(sums[0, 0])
    loss = sums[0, 1]
    clip_factor = jnp.minimum(1.0, clip_limit / grad_norm)
    step = step_count[0].astype(jnp.float32)
    new_masters, new_first, new_second = adam(
        masters, first_moment, second_moment, own_grad * clip_factor, learn_rate, step
    )
    new_table, new_table_first, new_table_second = adam(
        section_table, table_first, table_second, table_grad * clip_factor, table_rate, step
    )
    return (
        new_masters,
        new_first,
        new_second,
        new_table,
        new_table_first,
        new_table_second,
        grad_norm,
        loss,
    )


def solution(mesh):
    return jax.shard_map(
        functools.partial(per_device, Place(mesh)),
        mesh=mesh,
        in_specs=(
            P("section", "batch", None),
            P("section", "batch", None),
            P("section", "batch", None),
            P("section", None),
            P("section", None),
            P("section", None),
            P(),
            P(),
            P(("section", "batch"), None),
            P(("section", "batch"), None, None),
            P(("section", "batch"), None),
            P(("section", "batch"), None),
            P(("section", "batch"), None),
        ),
        out_specs=(
            P("section", "batch", None),
            P("section", "batch", None),
            P("section", "batch", None),
            P("section", None),
            P("section", None),
            P("section", None),
            P(),
            P(),
        ),
        check_vma=False,
    )
```

```python
import functools
import math

import jax
import jax.numpy as jnp
import numpy as np
from jax import lax
from jax.experimental import pallas as pl
from jax.experimental.pallas import tpu as pltpu
from jax.sharding import PartitionSpec as P

D = 1024
HEADS = 16
HD = 64
CODES = 1024
LEVELS = 8
PHONES = 512
SECTIONS = 8
CORES = 2

clip_limit = 0.002
learn_rate = 0.02
table_rate = 0.1
beta_one = 0.9
beta_two = 0.95
adam_eps = 1e-08
decay_rate = 0.1
norm_eps = 1e-05
pos_scale = 0.1
float_out = jnp.float32
low = jnp.bfloat16
MESH = pl.DeviceIdType.MESH
MIB = 1 << 20


class Place:
    def __init__(self, mesh):
        self.groups = mesh.shape["section"]
        self.batch = mesh.shape["batch"]
        self.ny = self.groups // CORES
        self.nx = 1 << (int(math.log2(self.batch)) // 2)
        self.nz = self.batch // self.nx
        self.panel = D // self.groups
        self.half = D // CORES

    def here(self):
        self.s = lax.axis_index("section")
        self.j = lax.axis_index("batch")
        self.y = lax.div(self.s, CORES)
        self.c = lax.rem(self.s, CORES)
        self.z = lax.div(self.j, self.nx)
        self.x = lax.rem(self.j, self.nx)
        self.sections = [lax.rem(self.s + d, self.groups) for d in range(self.groups)]
        self.xs = [lax.rem(self.x + d, self.nx) for d in range(self.nx)]
        self.ys = [lax.rem(self.y + d, self.ny) for d in range(self.ny)]
        self.zs = [lax.rem(self.z + d, self.nz) for d in range(self.nz)]
        self.x_peers = [(self.s, self.z * self.nx + x) for x in self.xs]
        self.y_peers = [(y * CORES + self.c, self.j) for y in self.ys]
        self.z_peers = [(self.s, z * self.nx + self.x) for z in self.zs]
        self.core_peer = (self.y * CORES + (1 - self.c), self.j)

    def panel_of(self, s):
        return lax.rem(s, CORES) * self.ny + lax.div(s, CORES)

    def section_peer(self, d):
        return self.sections[d]

    def x_of(self, d):
        return self.xs[d]

    def y_of(self, d):
        return self.ys[d]

    def z_of(self, d):
        return self.zs[d]

    def at_x(self, d):
        return self.x_peers[d]

    def at_y(self, d):
        return self.y_peers[d]

    def at_z(self, d):
        return self.z_peers[d]

    def at_core(self):
        return self.core_peer

    def columns(self, index, width):
        return pl.ds(pl.multiple_of(index * width, width), width)

    def near_peers(self):
        return [
            (self.sections[d], self.z * self.nx + self.xs[e])
            for d in range(self.groups)
            for e in range(self.nx)
            if d or e
        ]

    def barrier(self):
        sem = pltpu.get_barrier_semaphore()
        peers = self.near_peers() + [self.at_z(d) for d in range(1, self.nz)]
        for peer in peers:
            pl.semaphore_signal(sem, inc=1, device_id=peer, device_id_type=MESH)
        pl.semaphore_wait(sem, len(peers))

    def small_slots(self):
        return (self.groups * self.nx - 1) + (self.nz - 1)

    def table_slots(self):
        return (self.groups - 1) + (self.nx - 1) + (self.nz - 1)

    def small_stages(self, held, sent, landed, send_sem, recv_sem):
        near = self.near_peers()
        far = [self.at_z(d) for d in range(1, self.nz)]

        def stage(number, peers, first):
            copies = [
                remote(
                    sent.at[number],
                    landed.at[first + n],
                    send_sem.at[first + n],
                    recv_sem.at[first + n],
                    peer,
                )
                for n, peer in enumerate(peers)
            ]

            def start():
                sent[number] = held[...]
                for copy in copies:
                    copy.start()

            def end():
                for copy in copies:
                    copy.wait()
                total = held[...]
                for n in range(len(peers)):
                    total = total + landed[first + n]
                held[...] = total

            return start, end

        return [stage(0, near, 0), stage(1, far, len(near))]


def remote(src, dst, send_sem, recv_sem, device):
    return pltpu.make_async_remote_copy(
        src_ref=src,
        dst_ref=dst,
        send_sem=send_sem,
        recv_sem=recv_sem,
        device_id=device,
        device_id_type=MESH,
    )


ROWS_AT_ONCE = 256
BLOCKS = 29
CODE, PHONE, QKV, OUT, UP, DOWN, HEAD = 0, 2, 3, 9, 11, 19, 27
FRONT = 9
OUTWARD = (0, 1, 2, 5, 6, 7, 8, 9, 10, 11, 12, *range(13, 29), 3, 4)
HOMEWARD = (3, 4, *range(21, 29), *range(13, 21), 11, 12, 5, 6, 7, 8, 9, 10, 0, 1, 2)


def begin(copies):
    for copy in copies:
        copy.start()


def landed_all(copies):
    for copy in copies:
        copy.wait_recv()


def gone(copies):
    for copy in copies:
        copy.wait_send()


LONG_EVERY = 7
LONG_OUT, LONG_HOME = 3, 1
LONGS = len(range(LONG_HOME, BLOCKS, LONG_EVERY))
NEARS = BLOCKS - LONGS


def place_among(b):
    return b - lax.div(b + (LONG_EVERY - 1 - LONG_HOME), LONG_EVERY)


def by_kind(b, at, near=None, far=None):
    long = lax.rem(b, LONG_EVERY) == at
    if near is not None:
        pl.when(jnp.logical_not(long))(near)
    if far is not None:
        pl.when(long)(far)


def rank_cuts(per_group):
    return sorted({0, min(2, per_group), min(4, per_group), per_group})


def rank_keys(owners_ref, order, per_group, groups):
    seen = [jnp.int32(0)] * groups
    keys = []
    for b in order:
        section = jnp.clip(lax.div(owners_ref[b], per_group), 0, groups - 1)
        rank = jnp.int32(0)
        for g in range(groups):
            rank = jnp.where(section == g, seen[g], rank)
            seen[g] = seen[g] + jnp.where(section == g, 1, 0)
        keys.append(section * per_group + jnp.minimum(rank, per_group - 1))
    return keys


def within(value, count):
    return (value >= 0) & (value < count)


def times(a, b):
    return lax.dot_general(a, b, (((1,), (0,)), ((), ())), preferred_element_type=float_out)


def times_t(a, b):
    return lax.dot_general(a, b, (((1,), (1,)), ((), ())), preferred_element_type=float_out)


def turned_times(a, b):
    return lax.dot_general(a, b, (((0,), (0,)), ((), ())), preferred_element_type=float_out)


def normalize(stream):
    centred = stream - jnp.mean(stream, axis=-1, keepdims=True)
    scale = lax.rsqrt(jnp.mean(centred * centred, axis=-1, keepdims=True) + norm_eps)
    return (centred * scale, scale)


def norm_back(grad, normed, scale, gain):
    inner = grad * (1.0 + gain)
    result = scale * (
        inner
        - jnp.mean(inner, axis=-1, keepdims=True)
        - normed * jnp.mean(inner * normed, axis=-1, keepdims=True)
    )
    return (
        result,
        jnp.sum(grad * normed, axis=0, keepdims=True),
        jnp.sum(grad, axis=0, keepdims=True),
    )


def rates():
    column = np.arange(D)
    return column, np.exp(-(2 * (column // 2)) * (math.log(10000.0) / D))


def index_waves(length):
    column, rate = rates()
    angle = np.arange(length)[:, None] * rate
    sine, cosine = np.sin(angle), np.cos(angle)
    even = column % 2 == 0
    same = pos_scale * np.where(even, sine, cosine)
    other = pos_scale * np.where(even, cosine, sine)
    return jnp.asarray(same, jnp.float32), jnp.asarray(other, jnp.float32)


def column_of(row):
    wide = jnp.broadcast_to(row.astype(float_out), (128, row.shape[1]))
    return wide.T[:, :1].astype(jnp.int32)


def masks():
    lane = lax.broadcasted_iota(jnp.int32, (1, 2 * HD), 1)
    return [(lane // HD == h).astype(low) for h in range(2)]


def in_turn(items, first, middle, last):
    ahead, behind = first(*items[0]), None
    for n, item in enumerate(items):
        now = ahead
        if n + 1 < len(items):
            ahead = first(*items[n + 1])
        made = middle(*item, *now)
        if behind is not None:
            last(*behind)
        behind = (*item, *made)
    last(*behind)


def attend_pairs(same, heads):
    turned = [v.astype(float_out).T.astype(low) for _, _, v in heads]
    outs = [[] for _ in heads]
    stats = [[] for _ in heads]
    scaled = [mask * HD ** (-0.5) for mask in masks()]

    def first(n, h):
        q, k, _ = heads[n]
        return (times_t(k, q * scaled[h]),)

    def middle(n, h, scores):
        scores = jnp.where(same, scores, -1000000000.0)
        top = jnp.max(scores, axis=0, keepdims=True)
        powers = jnp.exp(scores - top)
        total = jnp.sum(powers, axis=0, keepdims=True)
        stats[n].append(top + jnp.log(total))
        return ((powers * (1.0 / total)).astype(low),)

    def last(n, h, probs):
        outs[n].append(times(turned[n][h * HD : (h + 1) * HD], probs))

    in_turn([(n, h) for n in range(len(heads)) for h in range(2)], first, middle, last)
    return [jnp.concatenate(out, axis=0).T.astype(low) for out in outs], stats


def attend_pair_back(same, q, k, v, do, stats):
    k_turned = (k.astype(float_out) * HD ** (-0.5)).T.astype(low)
    width = q.shape[0] // 2
    q_of = [q * (mask * HD ** (-0.5)) for mask in masks()]
    do_of = [do * mask for mask in masks()]
    dq = [[], []]
    sums = [0.0, 0.0]

    def part(c):
        return slice(c * width, (c + 1) * width)

    def first(c, h):
        return times_t(k, q_of[h][part(c)]), times_t(v, do_of[h][part(c)])

    def middle(c, h, scores, grad):
        scores = jnp.where(same[:, part(c)], scores, -1000000000.0)
        probs = jnp.exp(scores - stats[h][:, part(c)])
        level = jnp.sum(probs * grad, axis=0, keepdims=True)
        return probs.astype(low), (probs * (grad - level)).astype(low)

    def last(c, h, probs, back):
        sums[0] = sums[0] + times(back, q_of[h][part(c)])
        sums[1] = sums[1] + times(probs, do_of[h][part(c)])
        dq[h].append(times(k_turned[h * HD : (h + 1) * HD], back))

    in_turn([(c, h) for c in range(2) for h in range(2)], first, middle, last)
    turned = jnp.concatenate([jnp.concatenate(parts, axis=1) for parts in dq], axis=0)
    return turned.T.astype(low), sums[0].astype(low), sums[1].astype(low)


def front_kernel(
    pc,
    owners_ref,
    ids_ref,
    masters_ref,
    raw_table,
    codes_ref,
    phones_ref,
    segs_ref,
    rate_ref,
    same_ref,
    other_ref,
    w_ref,
    params_ref,
    multi_out,
    hot_out,
    x_out,
    h_out,
    qkv_out,
    mixed_out,
    lse_ref,
    x1_out,
    h2_out,
    act_out,
    slope_out,
    x2_out,
    table_ref,
    seg_col,
    phone_col,
    code_cols,
    starts_ref,
    waves,
    rounded,
    ordered,
    counts_ref,
    *rest,
):
    parts = len(rank_cuts(ordered.shape[0])) - 1
    slots = rest[:parts]
    (
        pieces,
        table_all,
        wf,
        multi,
        hot,
        x0,
        h1,
        pool,
        wo,
        h2,
        act,
        slope,
        sent,
        landed,
        key_ref,
        in_sem,
        a_send,
        a_recv,
        t_send,
        t_recv,
        own_sem,
        z_send,
        z_recv,
        e_send,
        e_recv,
        f_send,
        f_recv,
        c_send,
        c_recv,
        m_send,
        m_recv,
        w_sem,
        out_sem,
        qkv_sem,
        mix_sem,
        o_sem,
        u_sem,
        d_sem,
        x1_sem,
        act_sem,
        x2_sem,
    ) = rest[parts:]
    pc.here()
    blocks = BLOCKS
    per_group, piece = rounded.shape[:2]
    own_sections = table_ref.shape[0]
    rows, length = segs_ref.shape
    steps = length // ROWS_AT_ONCE
    pairs = HEADS // 2
    mine = pc.columns(pc.panel_of(pc.s), pc.panel)
    core_half = pc.columns(pc.c, pc.half)
    loads = [
        pltpu.make_async_copy(
            masters_ref, x0.at[pl.ds(0, per_group * piece)], in_sem.at[0]
        ),
        pltpu.make_async_copy(same_ref, waves.at[0], in_sem.at[1]),
        pltpu.make_async_copy(other_ref, waves.at[1], in_sem.at[2]),
    ]
    begin(loads)
    keys = rank_keys(owners_ref, OUTWARD, per_group, pc.groups)
    for p in range(blocks):
        key_ref[p] = keys[p]
    base = pc.s * per_group
    slot_of = []
    for k in range(per_group):
        slot = jnp.int32(0)
        for p in range(blocks):
            slot = jnp.where(keys[p] == base + k, owners_ref[OUTWARD[p]] - base, slot)
        slot_of.append(slot)
    table_ref[...] = jnp.zeros_like(table_ref)
    for k in range(6):
        for n in range(own_sections):
            table_ref[n, k : k + 1] = raw_table[n : n + 1, k * D : (k + 1) * D]
    pc.barrier()
    loads[0].wait()
    rounded[...] = x0[: per_group * piece].astype(low).reshape(rounded.shape)
    for k in range(per_group):
        ordered[k] = rounded[jnp.clip(slot_of[k], 0, per_group - 1)]
    cuts = rank_cuts(per_group)
    for m, place in enumerate(slots):
        for k in range(cuts[m], cuts[m + 1]):
            place[pc.s, k - cuts[m]] = ordered[k, :, mine]

    def exchange(m):
        first, count = cuts[m], cuts[m + 1] - cuts[m]
        return [
            remote(
                ordered.at[
                    pl.ds(first, count),
                    :,
                    pc.columns(pc.panel_of(pc.section_peer(d)), pc.panel),
                ],
                slots[m].at[pc.s],
                a_send.at[m, d - 1],
                a_recv.at[m, d - 1],
                (pc.section_peer(d), pc.j),
            )
            for d in range(1, pc.groups)
        ]

    def table_exchange():
        return [
            remote(
                table_ref,
                table_all.at[pl.ds(pc.s * own_sections, own_sections)],
                t_send.at[d - 1],
                t_recv.at[d - 1],
                (pc.section_peer(d), pc.j),
            )
            for d in range(1, pc.groups)
        ]

    for m in range(len(cuts) - 1):
        begin(exchange(m))
    begin(table_exchange())
    table_all[pl.ds(pc.s * own_sections, own_sections)] = table_ref[...]
    section = lax.broadcasted_iota(jnp.int32, (SECTIONS, 128), 0)
    counts = jnp.zeros((SECTIONS, 128), jnp.float32)
    for r in range(rows):
        counts = counts + jnp.where(section == ids_ref[0, r], float(length), 0.0)
    counts_ref[...] = counts
    small = pc.small_stages(counts_ref, sent, landed, m_send, m_recv)

    def take_pieces(m):
        for copy in exchange(m):
            copy.wait()
        until = cuts[m + 1] if m + 2 < len(cuts) else blocks
        for p in range(cuts[m], until):
            key = jnp.clip(key_ref[p], 0, per_group * pc.groups - 1)
            section, rank = lax.div(key, per_group), lax.rem(key, per_group)
            found = slots[0][section, jnp.minimum(rank, cuts[1] - 1)]
            for n in range(1, m + 1):
                last = cuts[n + 1] - cuts[n] - 1
                here = slots[n][section, jnp.clip(rank - cuts[n], 0, last)]
                found = jnp.where(rank >= cuts[n], here, found)
            pieces[p] = found

    def set_params():
        for copy in table_exchange():
            copy.wait()
        line = lax.broadcasted_iota(jnp.int32, (8, D), 0)
        for r in range(rows):
            held = jnp.sum(
                jnp.where(section == ids_ref[0, r], counts_ref[...], 0.0), axis=0, keepdims=True
            )
            weight = 1.0 / (SECTIONS * jnp.concatenate([held] * (D // 128), axis=1))
            params_ref[r] = jnp.where(line == 6, weight, table_all[ids_ref[0, r]])

    def own(p):
        return pltpu.make_async_copy(
            pieces.at[p], w_ref.at[p, pc.z, pc.x, :, mine], own_sem.at[p]
        )

    def along_z(p):
        return [
            remote(
                pieces.at[p],
                w_ref.at[p, pc.z, pc.x, :, mine],
                z_send.at[p, d - 1],
                z_recv.at[p, d - 1],
                pc.at_z(d),
            )
            for d in range(1, pc.nz)
        ]

    def spread(p, part, send_sem, recv_sem, count, target, source=None, first=0):
        source = part if source is None else source
        return [
            remote(
                source,
                part,
                send_sem.at[p, first + d - 1],
                recv_sem.at[p, first + d - 1],
                target(d),
            )
            for d in range(1, count)
        ]

    middle_z = pc.nz // 2
    lower, upper = pl.ds(0, middle_z), pl.ds(middle_z, pc.nz - middle_z)

    def first_x(p):
        part = w_ref.at[p, lower, pc.x, :, mine]
        return spread(p, part, e_send, e_recv, pc.nx, pc.at_x)

    def first_y(p):
        part = w_ref.at[p, upper, pc.x, :, mine]
        return spread(p, part, e_send, e_recv, pc.ny, pc.at_y, first=pc.nx - 1)

    def then_y(p):
        part = w_ref.at[p, lower, :, :, mine]
        return spread(p, part, f_send, f_recv, pc.ny, pc.at_y)

    def then_x(p):
        part = w_ref.at[p, upper, pc.x, :, core_half]
        return spread(p, part, f_send, f_recv, pc.nx, pc.at_x, first=pc.ny - 1)

    def far_x(p):
        part = w_ref.at[p, pc.z, pc.x, :, mine]
        return spread(p, part, e_send, e_recv, pc.nx, pc.at_x, pieces.at[p])

    def far_y(p):
        part = w_ref.at[p, pc.z, :, :, mine]
        return spread(p, part, f_send, f_recv, pc.ny, pc.at_y)

    def ring(p, k):
        part = w_ref.at[p, pc.z_of((pc.nz - k + 1) % pc.nz), :, :, core_half]
        return [remote(part, part, z_send.at[p, k - 1], z_recv.at[p, k - 1], pc.at_z(1))]

    def to_core(p):
        part = w_ref.at[p, :, :, :, core_half]
        return [remote(part, part, c_send.at[p], c_recv.at[p], pc.at_core())]

    def into_vmem(p):
        return pltpu.make_async_copy(w_ref.at[p], wf.at[p], w_sem.at[p])

    for r in range(rows):
        at = pl.ds(r * length, length)
        tall = jnp.concatenate(
            [codes_ref[r].astype(float_out), jnp.zeros((128 - LEVELS, length), float_out)], axis=0
        )
        code_cols[at] = tall.T.astype(jnp.int32)
        seg_col[pl.ds(r * length, length)] = column_of(segs_ref[r : r + 1])
        phone_col[pl.ds(r * length, length)] = column_of(phones_ref[r : r + 1])
        starts = [
            jnp.sum(jnp.where(segs_ref[r : r + 1] < k, 1.0, 0.0), axis=1, keepdims=True)
            for k in (0, 1, 2)
        ]
        angle = jnp.concatenate(starts, axis=0) * rate_ref[...]
        odd = lax.broadcasted_iota(jnp.int32, angle.shape, 1) % 2
        starts_ref[r, 0:3] = jnp.cos(angle)
        starts_ref[r, 3:6] = jnp.where(odd == 1, 1.0, -1.0) * jnp.sin(angle)

    def chunk(i):
        return pl.ds(i * ROWS_AT_ONCE, ROWS_AT_ONCE)

    def embed_out(i):
        made = ((multi, multi_out), (hot, hot_out), (x0, x_out), (h1, h_out))
        return [
            pltpu.make_async_copy(a.at[chunk(i)], b.at[chunk(i)], out_sem.at[i, n])
            for n, (a, b) in enumerate(made)
        ]

    def qkv_copy(n):
        return pltpu.make_async_copy(pool.at[n], qkv_out.at[n], qkv_sem.at[n])

    def weight(first, count=2):
        return wf[first : first + count].reshape(count * D // 2, D)

    def prepare_step(i):
        at = chunk(i)
        r, local = i // steps, pl.ds((i % steps) * ROWS_AT_ONCE, ROWS_AT_ONCE)
        vocab = lax.broadcasted_iota(jnp.int32, (ROWS_AT_ONCE, CODES), 1)
        count = jnp.zeros((ROWS_AT_ONCE, CODES), jnp.float32)
        for level in range(LEVELS):
            code = code_cols[at, level : level + 1]
            code = jnp.where(ids_ref[0, r] >= level, code, -1)
            count = count + jnp.where(code == vocab, 1.0, 0.0)
        multi[at] = count.astype(low)
        names = lax.broadcasted_iota(jnp.int32, (ROWS_AT_ONCE, PHONES), 1)
        hot[at] = jnp.where(phone_col[at] == names, 1.0, 0.0).astype(low)
        segs = seg_col[at]
        cosine, sine = (
            jnp.where(
                segs == 0,
                starts_ref[r, k : k + 1],
                jnp.where(segs == 1, starts_ref[r, k + 1 : k + 2], starts_ref[r, k + 2 : k + 3]),
            )
            for k in (0, 3)
        )
        x0[at] = waves[0, local] * cosine + waves[1, local] * sine

    def embed_step(i):
        at, r = chunk(i), i // steps
        stream = times(multi[at], weight(CODE)) + times(hot[at], weight(PHONE, 1)) + x0[at]
        x0[at] = stream
        normed, _ = normalize(stream)
        h1[at] = (normed * (1.0 + params_ref[r, 0:1]) + params_ref[r, 1:2]).astype(low)
        begin(embed_out(i))

    def project_step(k):
        for r in range(rows):
            made = times(h1[r * length : (r + 1) * length], wf[pl.ds(QKV + 2 * k, 2)].reshape(D, D))
            pool[rows * k + r] = made.astype(low).reshape(pool.shape[1:])
            qkv_copy(rows * k + r).start()

    def row(r):
        return pl.ds(r * length, length)

    def mixed_copy(r):
        return pltpu.make_async_copy(pool.at[3 * rows + r], mixed_out.at[r], mix_sem.at[r])

    def attend_step(n):
        r, h = lax.div(2 * n, pairs), lax.rem(2 * n, pairs)
        same = seg_col[row(r)] == segs_ref[pl.ds(r, 1)]
        at = [pc.columns(h + e, 2 * HD) for e in range(2)]
        outs, stats = attend_pairs(
            same,
            [
                [
                    pool[rows * k + r, :, :, :, columns].reshape(length, 2 * HD)
                    for k in range(3)
                ]
                for columns in at
            ],
        )
        for e in range(2):
            pool[3 * rows + r, :, :, :, at[e]] = outs[e].reshape(*pool.shape[1:4], 2 * HD)
            for k, lse in enumerate(stats[e]):
                lse_ref[r, h + e, k : k + 1] = lse

        @pl.when(h + 2 == pairs)
        def _():
            mixed_copy(r).start()

    def out_weight():
        return pltpu.make_async_copy(w_ref.at[pl.ds(OUT, 2)], wo, o_sem)

    def up_weight():
        return pltpu.make_async_copy(w_ref.at[pl.ds(UP, 8)], wf.at[pl.ds(0, 8)], u_sem)

    def down_weight(p):
        return pltpu.make_async_copy(w_ref.at[p], pool.at[p - DOWN], d_sem.at[p - DOWN])

    def stream_copies(i):
        return [
            pltpu.make_async_copy(x0.at[chunk(i)], x1_out.at[chunk(i)], x1_sem.at[i, 0]),
            pltpu.make_async_copy(h2.at[chunk(i)], h2_out.at[chunk(i)], x1_sem.at[i, 1]),
        ]

    def act_copy(i):
        return pltpu.make_async_copy(
            act.at[:, chunk(i)], act_out.at[:, chunk(i)], act_sem.at[i, 0]
        )

    def slope_copy(i):
        return pltpu.make_async_copy(
            slope.at[i % 2], slope_out.at[:, chunk(i)], act_sem.at[i, 1]
        )

    def out_step(i):
        at, r = chunk(i), i // steps
        for copy in embed_out(i):
            copy.wait()
        depth = pc.nz // steps
        mixed = pool[3 * rows + r, pl.ds(i % steps * depth, depth)].reshape(ROWS_AT_ONCE, D)
        stream = x0[at] + times(mixed, wo[...].reshape(D, D))
        x0[at] = stream
        normed, _ = normalize(stream)
        h2[at] = (normed * (1.0 + params_ref[r, 2:3]) + params_ref[r, 3:4]).astype(low)
        begin(stream_copies(i))

    def up_step(i):
        at = chunk(i)

        @pl.when(i >= 2)
        def _():
            slope_copy(i - 2).wait()

        for g in range(4):
            u = times(h2[at], weight(2 * g))
            cdf = 0.5 + 0.5 * lax.erf(u * math.sqrt(0.5))
            density = jnp.exp(-0.5 * (u * u)) * (1.0 / math.sqrt(2.0 * math.pi))
            act[g, at] = (u * cdf).astype(low)
            slope[i % 2, g] = (cdf + u * density).astype(low)
        begin([act_copy(i), slope_copy(i)])

    def x2_copy(r):
        return pltpu.make_async_copy(x0.at[row(r)], x2_out.at[row(r)], x2_sem.at[r])

    def down_step(g):
        down_weight(DOWN + 2 * g).wait()
        down_weight(DOWN + 2 * g + 1).wait()
        for r in range(rows):
            at = row(r)
            x0[at] = x0[at] + times(act[g, at], pool[2 * g : 2 * g + 2].reshape(D, D))
            if g == 3:
                x2_copy(r).start()

    ahead = 4
    hops = pc.nz - 1
    embed_steps = rows * steps
    lands = [
        p + (2 * hops + 1 if p % LONG_EVERY == LONG_OUT else 6) for p in range(blocks)
    ]
    embed_from = max(lands[:QKV]) + 1
    project_from = max(
        embed_from + embed_steps,
        *(max(lands[QKV + 2 * k : QKV + 2 * k + 2]) + 1 - k for k in range(3)),
    )
    attend_from = project_from + 3
    out_from = max(attend_from + rows * pairs // 2, max(lands[OUT:UP]) + 2)
    out_ticks = embed_steps // 2
    up_fetch = max(max(lands[UP:DOWN]) + 1, attend_from)
    up_from = max(out_from + out_ticks, up_fetch + 1)
    late = max(1, out_from + out_ticks - min(lands[DOWN:HEAD]))
    down_at = []
    for g in range(4):
        landed_by = max(lands[DOWN + 2 * g : DOWN + 2 * g + 2]) + late + 1
        after = down_at[-1] + 1 if down_at else up_from + embed_steps
        down_at.append(max(landed_by, after))

    def step(p, body):
        pl.when(within(p, blocks))(lambda: body(p))

    def launch(p):
        own(p).start()
        by_kind(p, LONG_OUT, lambda: begin(along_z(p)), lambda: begin(far_x(p)))

    def far_second(p):
        def far():
            own(p).wait()
            landed_all(far_x(p))
            begin(far_y(p))

        by_kind(p, LONG_OUT, far=far)

    def first(p):
        def near():
            own(p).wait()
            landed_all(along_z(p))
            begin(first_x(p) + first_y(p))

        def far():
            landed_all(far_y(p))
            begin(ring(p, 1))

        by_kind(p, LONG_OUT, near, far)

    def ring_on(k):
        def body(p):
            def far():
                landed_all(ring(p, k - 1))
                begin(ring(p, k))

            by_kind(p, LONG_OUT, far=far)

        return body

    def then(p):
        def near():
            landed_all(first_x(p))
            begin(then_y(p))
            landed_all(first_y(p))
            begin(then_x(p))

        by_kind(p, LONG_OUT, near)

    def core_near(p):
        def near():
            landed_all(then_y(p) + then_x(p))
            begin(to_core(p))

        by_kind(p, LONG_OUT, near)

    def core_far(p):
        def far():
            landed_all(ring(p, hops))
            begin(to_core(p))

        by_kind(p, LONG_OUT, far=far)

    def held(p):
        @pl.when((p >= DOWN) & (p < HEAD))
        def _():
            down_weight(p).start()

    def arrived(p):
        landed_all(to_core(p))

        @pl.when(p < FRONT)
        def _():
            into_vmem(p).start()

    sent_after = 2 * hops + 4

    def sent_off(p):
        gone(to_core(p))

        def near():
            gone(along_z(p) + first_x(p) + first_y(p) + then_y(p) + then_x(p))

        def far():
            gone(far_x(p) + far_y(p))
            for k in range(1, pc.nz):
                gone(ring(p, k))

        by_kind(p, LONG_OUT, near, far)

    def tick(turn, carry):
        t = turn - ahead
        for m in range(len(cuts) - 1):
            pl.when(turn == cuts[m])(functools.partial(take_pieces, m))
        step(turn, launch)
        step(t + 2, far_second)
        step(t, first)
        step(t - 2, then)
        for k in range(2, pc.nz):
            step(t - 2 * (k - 1), ring_on(k))
        step(t - 5, core_near)
        step(t - 2 * hops, core_far)
        step(t - 6, lambda p: by_kind(p, LONG_OUT, lambda: arrived(p)))
        step(t - 2 * hops - 1, lambda p: by_kind(p, LONG_OUT, far=lambda: arrived(p)))
        step(t - 6 - late, lambda p: by_kind(p, LONG_OUT, lambda: held(p)))
        step(t - 2 * hops - 1 - late, lambda p: by_kind(p, LONG_OUT, far=lambda: held(p)))

        for stage, (start, end) in enumerate(small):
            pl.when(turn == ahead + 1 + 2 * stage)(start)
            pl.when(turn == ahead + 2 + 2 * stage)(end)
        pl.when(turn == ahead + 7)(set_params)

        @pl.when(t == 0)
        def _():
            loads[1].wait()
            loads[2].wait()

        @pl.when(within(t, embed_steps))
        def _():
            prepare_step(t)

        @pl.when(t == embed_from)
        def _():
            for p in range(QKV):
                into_vmem(p).wait()

        @pl.when(within(t - embed_from, embed_steps))
        def _():
            embed_step(t - embed_from)

        @pl.when(within(t - project_from, 3))
        def _():
            k = t - project_from
            into_vmem(QKV + 2 * k).wait()
            into_vmem(QKV + 2 * k + 1).wait()
            project_step(k)

        @pl.when(within(t - attend_from, rows * pairs // 2))
        def _():
            attend_step(t - attend_from)

        @pl.when(t == out_from - 1)
        def _():
            out_weight().start()

        @pl.when(t == up_fetch)
        def _():
            up_weight().start()

        @pl.when(t == out_from)
        def _():
            out_weight().wait()
            for n in range(3 * rows):
                qkv_copy(n).wait()

        @pl.when(within(t - out_from, out_ticks))
        def _():
            out_step(2 * (t - out_from))
            out_step(2 * (t - out_from) + 1)

        @pl.when(t == out_from + out_ticks - 1)
        def _():
            for r in range(rows):
                mixed_copy(r).wait()

        @pl.when(t == up_from)
        def _():
            up_weight().wait()

        @pl.when(within(t - up_from, embed_steps))
        def _():
            up_step(t - up_from)

        for g in range(4):

            @pl.when(t == down_at[g])
            def _(g=g):
                if g == 0:
                    for i in range(embed_steps):
                        for copy in stream_copies(i):
                            copy.wait()
                down_step(g)

        step(t - sent_after, sent_off)
        return carry

    last = max(blocks + 6, blocks + 2 * hops, down_at[-1] + 1)
    lax.fori_loop(0, last + ahead, tick, 0)

    def finish(p, carry):
        sent_off(p)
        return carry

    lax.fori_loop(last - sent_after, blocks, finish, 0)
    for i in range(embed_steps):
        act_copy(i).wait()
    for i in range(embed_steps - 2, embed_steps):
        slope_copy(i).wait()
    for r in range(rows):
        x2_copy(r).wait()


def like(shape, dtype=low):
    return jax.ShapeDtypeStruct(shape, dtype)


def front(pc, owners, ids, masters, table, codes, phones, segments):
    per_group, piece, _ = masters.shape
    rows, length = segments.shape
    total = rows * length
    rate = jnp.asarray(rates()[1][None], jnp.float32)
    own_sections = table.shape[0]
    hops = pc.nx - 1 + pc.ny - 1
    same, other = index_waves(length)
    small = pc.small_slots()
    embed_steps = total // ROWS_AT_ONCE
    cuts = rank_cuts(per_group)
    dma = pltpu.SemaphoreType.DMA
    vmem = pl.BlockSpec(memory_space=pltpu.VMEM)
    smem = pl.BlockSpec(memory_space=pltpu.SMEM)
    far = pl.BlockSpec(memory_space=pl.ANY)
    return pl.pallas_call(
        functools.partial(front_kernel, pc),
        out_shape=(
            like((BLOCKS, pc.nz, pc.nx, piece, D)),
            like((rows, 8, D), float_out),
            like((total, CODES)),
            like((total, PHONES)),
            like((total, D), float_out),
            like((total, D)),
            like((3 * rows, pc.nz, pc.nx, piece, D)),
            like((rows, pc.nz, pc.nx, piece, D)),
            like((rows, HEADS // 2, 2, length), float_out),
            like((total, D), float_out),
            like((total, D)),
            like((4, total, D)),
            like((4, total, D)),
            like((total, D), float_out),
        ),
        in_specs=[smem, smem, far] + [vmem] * 5 + [far, far],
        out_specs=(far, vmem, far, far, far, far, far, far, vmem, far, far, far, far, far),
        scratch_shapes=[
            pltpu.VMEM((own_sections, 8, D), float_out),
            pltpu.VMEM((total, 1), jnp.int32),
            pltpu.VMEM((total, 1), jnp.int32),
            pltpu.VMEM((total, 128), jnp.int32),
            pltpu.VMEM((rows, 8, D), float_out),
            pltpu.VMEM((2, length, D), float_out),
            pltpu.VMEM((per_group, piece, D), low),
            pltpu.VMEM((per_group, piece, D), low),
            pltpu.VMEM((SECTIONS, 128), float_out),
            *(
                pltpu.VMEM((pc.groups, b - a, piece, pc.panel), low)
                for a, b in zip(cuts[:-1], cuts[1:], strict=True)
            ),
            pltpu.VMEM((BLOCKS, piece, pc.panel), low),
            pltpu.VMEM((own_sections * pc.groups, 8, D), float_out),
            pltpu.VMEM((FRONT, pc.nz, pc.nx, piece, D), low),
            pltpu.VMEM((total, CODES), low),
            pltpu.VMEM((total, PHONES), low),
            pltpu.VMEM((total, D), float_out),
            pltpu.VMEM((total, D), low),
            pltpu.VMEM((max(4 * rows, 8), pc.nz, pc.nx, piece, D), low),
            pltpu.VMEM((2, pc.nz, pc.nx, piece, D), low),
            pltpu.VMEM((total, D), low),
            pltpu.VMEM((4, total, D), low),
            pltpu.VMEM((2, 4, ROWS_AT_ONCE, D), low),
            pltpu.VMEM((2, 8, 128), float_out),
            pltpu.VMEM((small, 8, 128), float_out),
            pltpu.SMEM((BLOCKS,), jnp.int32),
            dma((3,)),
            dma((3, pc.groups - 1)),
            dma((3, pc.groups - 1)),
            dma((pc.groups - 1,)),
            dma((pc.groups - 1,)),
            dma((BLOCKS,)),
            dma((BLOCKS, pc.nz - 1)),
            dma((BLOCKS, pc.nz - 1)),
            dma((BLOCKS, hops)),
            dma((BLOCKS, hops)),
            dma((BLOCKS, hops)),
            dma((BLOCKS, hops)),
            dma((BLOCKS,)),
            dma((BLOCKS,)),
            dma((small,)),
            dma((small,)),
            dma((FRONT,)),
            dma((embed_steps, 4)),
            dma((3 * rows,)),
            dma((rows,)),
            dma,
            dma,
            dma((8,)),
            dma((embed_steps, 2)),
            dma((embed_steps, 2)),
            dma((rows,)),
        ],
        name="front",
        compiler_params=pltpu.CompilerParams(
            collective_id=0, has_side_effects=True, vmem_limit_bytes=62 * MIB
        ),
    )(owners, ids, masters.reshape(-1, D), table, codes, phones, segments, rate, same, other)


FAR = ("h3", "act", "h2", "mixed", "h1", "multi", "hot", "dlogits", "dffn", "du", "dattn")


HOME = (
    (0, 2, "h3", "dlogits"),
    (2, 8, "act", "dffn"),
    (10, 8, "h2", "du"),
    (18, 2, "mixed", "dattn"),
    (20, 6, "h1", "dqkv"),
    (26, 2, "multi", "demb"),
    (28, 1, "hot", "demb"),
)


def back_kernel(pc, *refs):
    held = dict(zip(FAR, refs[2 : 2 + len(FAR)], strict=True))
    owners_ref, ids_ref = refs[:2]
    (
        qkv_ref,
        do_ref,
        x0_ref,
        dx_ref,
        w_ref,
        lse_ref,
        segs_ref,
        params_ref,
        rows_ref,
        loss_ref,
        out_ref,
        table_out,
        sums_out,
        seg_col,
        block_of_ref,
        key_ref,
        rank_ref,
        arrived,
        sums_ref,
        x_buf,
        y_buf,
        own_half,
        send_half,
        core_in,
        first_a,
        first_b,
        then_in,
        z_in,
        far_z,
        far_yx,
        far_in,
        final,
        by_slot,
        square,
        heads,
        dqkv,
        demb,
        qkv_w,
        chunks,
        row_sums,
        table_mine,
        table_in,
        table_mid,
        sent,
        landed,
        in_sem,
        head_sem,
        chunk_sem,
        w_sem,
        free_sem,
        c_send,
        c_recv,
        e_send,
        e_recv,
        f_send,
        f_recv,
        z_send,
        z_recv,
        a_send,
        a_recv,
        t_send,
        t_recv,
        m_send,
        m_recv,
    ) = refs[2 + len(FAR) :]
    held["dqkv"], held["demb"] = dqkv, demb
    pc.here()
    blocks = BLOCKS
    per_group = out_ref.shape[0]
    own_sections = table_out.shape[0]
    rows, length = segs_ref.shape
    pairs = HEADS // 2
    steps = length // ROWS_AT_ONCE
    attend_steps, embed_steps = rows * pairs, rows * steps
    width = x_buf.shape[2]
    keep = pc.columns(pc.c, pc.half)
    away = pc.columns(1 - pc.c, pc.half)
    core_slots = core_in.shape[0]
    hops = pc.nz - 1
    release = 2 * pc.nz - 1

    def fetch(t):
        for from_, count, xs, ys in HOME:
            u = t - from_

            @pl.when(within(u, count))
            def _(xs=xs, ys=ys, u=u):
                slot = lax.rem(t, 2)
                x_ref, y_ref = held[xs], held[ys]
                columns = pc.columns(lax.rem(u, 2), width)
                x_src = x_ref.at[lax.div(u, 2), :, columns] if len(x_ref.shape) == 3 else x_ref.at[:, columns]
                y_src = y_ref.at[lax.div(u, 2)] if len(y_ref.shape) == 3 else y_ref
                pltpu.make_async_copy(x_src, x_buf.at[slot], in_sem.at[slot, 0]).start()
                pltpu.make_async_copy(y_src, y_buf.at[slot], in_sem.at[slot, 1]).start()

    def fetched(slot):
        for n, buf in enumerate((x_buf, y_buf)):
            pltpu.make_async_copy(buf.at[slot], buf.at[slot], in_sem.at[slot, n]).wait()

    def head_copies(n):
        r, h, slot = n // pairs, n % pairs, n % 2
        at, columns = pl.ds(r * length, length), pc.columns(h, 2 * HD)
        copies = [
            pltpu.make_async_copy(
                qkv_ref.at[k, at, columns], heads.at[slot, k], head_sem.at[slot, k]
            )
            for k in range(3)
        ]
        copies.append(
            pltpu.make_async_copy(do_ref.at[at, columns], heads.at[slot, 3], head_sem.at[slot, 3])
        )
        return copies

    def chunk(i):
        return pl.ds(i * ROWS_AT_ONCE, ROWS_AT_ONCE)

    def chunk_copies(i):
        slot = i % 2
        return [
            pltpu.make_async_copy(x0_ref.at[chunk(i)], chunks.at[slot, 0], chunk_sem.at[slot, 0]),
            pltpu.make_async_copy(dx_ref.at[chunk(i)], chunks.at[slot, 1], chunk_sem.at[slot, 1]),
        ]

    weight_copy = pltpu.make_async_copy(w_ref.at[pl.ds(QKV, 6)], qkv_w, w_sem)

    def attend_back_step(n):
        r, h, slot = n // pairs, n % pairs, n % 2
        at, columns = pl.ds(r * length, length), pc.columns(h, 2 * HD)
        same = seg_col[at] == segs_ref[pl.ds(r, 1)]
        stats = [lse_ref[r, h, k : k + 1] for k in range(2)]
        made = attend_pair_back(same, *(heads[slot, k] for k in range(4)), stats)
        for k in range(3):
            dqkv[k, at, columns] = made[k]

    def embed_back_step(i):
        for copy in chunk_copies(i):
            copy.wait()
        r, slot = i // steps, i % 2
        dh = 0.0
        for k in range(3):
            dh = dh + times_t(
                dqkv[k, chunk(i)], qkv_w[2 * k : 2 * k + 2].reshape(D, D)
            )
        normed, scale = normalize(chunks[slot, 0])
        dx, gain, shift = norm_back(dh, normed, scale, params_ref[r, 0:1])
        demb[chunk(i)] = (chunks[slot, 1] + dx).astype(low)
        row_sums[r, 0:2] += jnp.concatenate([gain, shift], axis=0)

    def to_core(b):
        return [
            remote(
                send_half.at[lax.rem(b, 4)],
                core_in.at[lax.rem(b, core_slots)],
                c_send.at[b],
                c_recv.at[b],
                pc.at_core(),
            )
        ]

    middle_z = pc.nz // 2
    lower, upper = slice(0, middle_z), slice(middle_z, pc.nz)
    lower_at, upper_at = pl.ds(0, middle_z), pl.ds(middle_z, pc.nz - middle_z)

    def first_x(b):
        return [
            remote(
                core_in.at[lax.rem(b, core_slots), lower_at, pc.x_of(d)],
                first_a.at[place_among(b), d - 1],
                e_send.at[b, d - 1],
                e_recv.at[b, d - 1],
                pc.at_x(d),
            )
            for d in range(1, pc.nx)
        ]

    def first_y(b):
        return [
            remote(
                core_in.at[
                    lax.rem(b, core_slots), upper_at, :, :, pc.columns(pc.y_of(d), pc.panel)
                ],
                first_b.at[place_among(b), d - 1],
                e_send.at[b, pc.nx - 1 + d - 1],
                e_recv.at[b, pc.nx - 1 + d - 1],
                pc.at_y(d),
            )
            for d in range(1, pc.ny)
        ]

    def then_y(b):
        return [
            remote(
                first_a.at[place_among(b), 0, :, :, pc.columns(pc.y_of(d), pc.panel)],
                then_in.at[place_among(b), d - 1, lower_at],
                f_send.at[b, d - 1],
                f_recv.at[b, d - 1],
                pc.at_y(d),
            )
            for d in range(1, pc.ny)
        ]

    def then_x(b):
        return [
            remote(
                first_b.at[place_among(b), 0, :, pc.x_of(d)],
                then_in.at[place_among(b), d - 1, upper_at],
                f_send.at[b, pc.ny - 1 + d - 1],
                f_recv.at[b, pc.ny - 1 + d - 1],
                pc.at_x(d),
            )
            for d in range(1, pc.nx)
        ]

    def along_z(b):
        return [
            remote(
                then_in.at[place_among(b), 0, pc.z_of(d)],
                z_in.at[place_among(b), d - 1],
                z_send.at[b, d - 1],
                z_recv.at[b, d - 1],
                pc.at_z(d),
            )
            for d in range(1, pc.nz)
        ]

    def ring(b, k):
        n = lax.div(b, LONG_EVERY)
        source = (
            core_in.at[lax.rem(b, core_slots), pc.z_of(hops)] if k == 1 else far_z.at[n, k - 2]
        )
        return [
            remote(source, far_z.at[n, k - 1], z_send.at[b, k - 1], z_recv.at[b, k - 1], pc.at_z(1))
        ]

    def far_y(b):
        n = lax.div(b, LONG_EVERY)
        return [
            remote(
                far_z.at[n, hops - 1, :, :, pc.columns(pc.y_of(d), pc.panel)],
                far_yx.at[n, d - 1],
                f_send.at[b, d - 1],
                f_recv.at[b, d - 1],
                pc.at_y(d),
            )
            for d in range(1, pc.ny)
        ]

    def far_x(b):
        n = lax.div(b, LONG_EVERY)
        return [
            remote(
                far_yx.at[n, 0, pc.x_of(d)],
                far_in.at[n, d - 1],
                e_send.at[b, d - 1],
                e_recv.at[b, d - 1],
                pc.at_x(d),
            )
            for d in range(1, pc.nx)
        ]

    def summed(own, landed_ref, index, count):
        total = own.astype(float_out)
        for d in range(count - 1):
            total = total + landed_ref[index, d].astype(float_out)
        return total

    def table_stage():
        return [
            remote(
                table_mine.at[pl.ds(pc.section_peer(d) * own_sections, own_sections)],
                table_in.at[d - 1],
                t_send.at[d - 1],
                t_recv.at[d - 1],
                (pc.section_peer(d), pc.j),
            )
            for d in range(1, pc.groups)
        ]

    def table_hop(stage):
        count, target = ((pc.nx, pc.at_x), (pc.nz, pc.at_z))[stage]
        first = pc.groups - 1 + stage * (pc.nx - 1)
        return [
            remote(
                table_mid.at[stage],
                table_in.at[first + d - 1],
                t_send.at[first + d - 1],
                t_recv.at[first + d - 1],
                target(d),
            )
            for d in range(1, count)
        ]

    def table_landed(copies, own, first):
        for copy in copies:
            copy.wait()
        total = own
        for n in range(len(copies)):
            total = total + table_in[first + n]
        return total

    def table_after_section():
        own = table_mine[pl.ds(pc.s * own_sections, own_sections)]
        table_mid[0] = table_landed(table_stage(), own, 0)
        begin(table_hop(0))

    def table_after_x():
        table_mid[1] = table_landed(table_hop(0), table_mid[0], pc.groups - 1)
        begin(table_hop(1))

    def table_after_z():
        first = pc.groups - 1 + pc.nx - 1
        table_out[...] = table_landed(table_hop(1), table_mid[1], first)

    fetch(0)
    begin(head_copies(0))
    weight_copy.start()
    pc.barrier()
    square[...] = jnp.zeros_like(square)
    final[blocks] = jnp.zeros(final.shape[1:], low)
    row_sums[...] = rows_ref[...]
    for r in range(rows):
        seg_col[pl.ds(r * length, length)] = column_of(segs_ref[r : r + 1])

    base = pc.s * per_group

    def rank_blocks():
        keys = rank_keys(owners_ref, HOMEWARD[::-1], per_group, pc.groups)[::-1]
        for b in range(blocks):
            key_ref[b] = keys[b]
        for i in range(per_group):
            rank = jnp.int32(per_group)
            for b in range(blocks):
                rank = jnp.where(owners_ref[HOMEWARD[b]] == base + i, keys[b] - base, rank)
            rank_ref[i] = rank

        def find(i, carry):
            where = jnp.int32(blocks)
            for b in range(blocks):
                where = jnp.where(key_ref[b] == i, b, where)
            block_of_ref[i] = where
            return carry

        lax.fori_loop(0, per_group * pc.groups, find, 0)

    arrived[:, per_group] = jnp.zeros((pc.groups, *arrived.shape[2:]), low)
    early = per_group // 2
    panel = pc.panel_of(pc.s)

    def exchange(m):
        ranks = pl.ds(early, per_group - early) if m == 0 else pl.ds(0, early)
        return [
            remote(
                by_slot.at[pc.section_peer(d), ranks],
                arrived.at[panel, ranks],
                a_send.at[m, d - 1],
                a_recv.at[m, d - 1],
                (pc.section_peer(d), pc.j),
            )
            for d in range(1, pc.groups)
        ]

    def send_ranks(m):
        for k in range(early, per_group) if m == 0 else range(early):
            for g in range(pc.groups):
                where = jnp.clip(block_of_ref[g * per_group + k], 0, blocks)
                by_slot[g, k] = final[where]
            arrived[panel, k] = by_slot[pc.s, k]
        begin(exchange(m))

    def step(b, body):
        pl.when(within(b, blocks))(lambda: body(b))

    def first(b):
        landed_all(to_core(b))
        at = lax.rem(b, core_slots)
        core_in[at] = (
            core_in[at].astype(float_out) + own_half[lax.rem(b, 2)].reshape(core_in.shape[1:])
        ).astype(low)
        by_kind(
            b,
            LONG_HOME,
            lambda: begin(first_x(b) + first_y(b)),
            lambda: begin(ring(b, 1)),
        )

    def then(b):
        at, n = lax.rem(b, core_slots), place_among(b)

        def near():
            landed_all(first_x(b))
            first_a[n, 0] = summed(core_in[at, lower, pc.x], first_a, n, pc.nx).astype(low)
            begin(then_y(b))
            landed_all(first_y(b))
            mine = pc.columns(pc.y, pc.panel)
            first_b[n, 0] = summed(
                core_in[at, upper, :, :, mine], first_b, n, pc.ny
            ).astype(low)
            begin(then_x(b))

        by_kind(b, LONG_HOME, near)

    def ring_on(k):
        def body(b):
            def far():
                landed_all(ring(b, k))
                n, held_for = lax.div(b, LONG_EVERY), pc.z_of((2 * pc.nz - 1 - k) % pc.nz)
                far_z[n, k - 1] = (
                    far_z[n, k - 1].astype(float_out)
                    + core_in[lax.rem(b, core_slots), held_for].astype(float_out)
                ).astype(low)
                begin(ring(b, k + 1) if k < hops else far_y(b))

            by_kind(b, LONG_HOME, far=far)

        return body

    def third(b):
        n = place_among(b)

        def near():
            landed_all(then_y(b))
            total = first_a[n, 0, :, :, pc.columns(pc.y, pc.panel)].astype(float_out)
            for d in range(pc.ny - 1):
                total = total + then_in[n, d, lower].astype(float_out)
            then_in[n, 0, lower] = total.astype(low)
            landed_all(then_x(b))
            total = first_b[n, 0, :, pc.x].astype(float_out)
            for d in range(pc.nx - 1):
                total = total + then_in[n, d, upper].astype(float_out)
            then_in[n, 0, upper] = total.astype(low)
            begin(along_z(b))

        by_kind(b, LONG_HOME, near)

    def far_third(b):
        def far():
            landed_all(far_y(b))
            n, mine = lax.div(b, LONG_EVERY), pc.columns(pc.y, pc.panel)
            far_yx[n, 0] = summed(far_z[n, hops - 1, :, :, mine], far_yx, n, pc.ny).astype(low)
            begin(far_x(b))

        by_kind(b, LONG_HOME, far=far)

    def let_go(b):
        by_kind(
            b,
            LONG_HOME,
            lambda: gone(first_x(b) + first_y(b)),
            lambda: gone(ring(b, 1)),
        )

        @pl.when(b < blocks - core_slots)
        def _():
            pl.semaphore_signal(free_sem, inc=1, device_id=pc.at_core(), device_id_type=MESH)

    def settle(b, total):
        rounded = total.astype(low)
        final[b] = rounded
        wide = rounded.astype(float_out)
        square[...] += jnp.sum(wide * wide, axis=0, keepdims=True)

    def close(b):
        n = place_among(b)

        def near():
            landed_all(along_z(b))
            settle(b, summed(then_in[n, 0, pc.z], z_in, n, pc.nz))

        by_kind(b, LONG_HOME, near)

    def far_close(b):
        def far():
            landed_all(far_x(b))
            n = lax.div(b, LONG_EVERY)
            settle(b, summed(far_yx[n, 0, pc.x], far_in, n, pc.nx))

        by_kind(b, LONG_HOME, far=far)

    def sent_off(b):
        def far():
            for k in range(2, pc.nz):
                gone(ring(b, k))
            gone(far_y(b) + far_x(b))

        by_kind(
            b,
            LONG_HOME,
            lambda: gone(then_y(b) + then_x(b) + along_z(b)),
            far,
        )

    early_at = 1 + max(
        b + (release + 4 if b % LONG_EVERY == LONG_HOME else 7) for b in range(blocks - early)
    )

    def weigh(t):
        slot = lax.rem(t, 2)
        send_half[lax.rem(t, 4)] = (
            turned_times(x_buf[slot], y_buf[slot, :, away])
            .astype(low)
            .reshape(send_half.shape[1:])
        )
        own_half[slot] = turned_times(x_buf[slot], y_buf[slot, :, keep])

    def make_ready(t):
        fetched(lax.rem(t, 2))

        @pl.when(t >= 4)
        def _():
            gone(to_core(t - 4))

    def leave(t):
        @pl.when(t >= core_slots)
        def _():
            pl.semaphore_wait(free_sem, 1)

        begin(to_core(t))

    def serve(t):
        step(t - 1, first)
        step(t - 3, then)
        for k in range(1, pc.nz):
            step(t - 2 * k - 1, ring_on(k))
        step(t - 5, third)
        step(t - release, let_go)
        step(t - release - 2, far_third)
        step(t - 7, close)
        step(t - release - 4, far_close)

    def attending(t, carry):
        fetch(t + 1)

        @pl.when(t + 1 < attend_steps)
        def _():
            begin(head_copies(t + 1))

        for copy in head_copies(t):
            copy.wait()
        make_ready(t)
        weigh(t)
        attend_back_step(t)
        leave(t)
        serve(t)
        return carry

    def later(t, carry):
        pl.when(t + 1 < blocks)(lambda: fetch(t + 1))
        i = lax.div(t - attend_steps, 2)
        odd = lax.rem(t - attend_steps, 2)

        @pl.when((t < attend_steps + 2 * embed_steps) & (odd == 0))
        def _():
            begin(chunk_copies(i))

        @pl.when(t < blocks)
        def _():
            make_ready(t)
            weigh(t)
            leave(t)

        serve(t)
        pl.when(t == blocks - 2)(rank_blocks)
        pl.when(t == early_at)(lambda: send_ranks(0))

        @pl.when((t < attend_steps + 2 * embed_steps) & (odd == 1))
        def _():
            @pl.when(t == attend_steps + 1)
            def _():
                weight_copy.wait()

            embed_back_step(i)

        table_at = attend_steps + 2 * embed_steps

        @pl.when(t == table_at)
        def _():
            for section in range(own_sections * pc.groups):
                total = jnp.zeros(row_sums.shape[1:], float_out)
                for r in range(rows):
                    total = total + jnp.where(ids_ref[0, r] == section, row_sums[r], 0.0)
                table_mine[section] = total
            begin(table_stage())

        pl.when(t == table_at + 4)(table_after_section)
        pl.when(t == table_at + 8)(table_after_x)
        for k in range(2):
            b = 2 * (t - table_at) + k
            pl.when((t >= table_at) & (b < sent_in_loop))(functools.partial(sent_off, b))

        return carry

    last_long = LONG_HOME + (LONGS - 1) * LONG_EVERY
    last_tick = attend_steps + 2 * embed_steps + 8
    ticks = max(
        last_tick + 1, blocks + 7, blocks + release, last_long + release + 5, early_at + 1
    )
    sent_in_loop = min(blocks - 7, 2 * (ticks - attend_steps - 2 * embed_steps))
    lax.fori_loop(0, attend_steps, attending, 0)
    lax.fori_loop(attend_steps, ticks, later, 0)

    send_ranks(1)

    table_after_z()
    total = table_out[...]
    table_square = jnp.sum(total * total) / pc.batch
    lane = lax.broadcasted_iota(jnp.int32, (8, 128), 1)
    part = jnp.where(lane == 0, jnp.sum(square[...]) + table_square, loss_ref[...])
    sums_ref[...] = part
    for start, end in pc.small_stages(sums_ref, sent, landed, m_send, m_recv):
        start()
        end()
    sums_out[...] = sums_ref[...]
    for copy in exchange(0) + exchange(1):
        copy.wait()
    for i in range(per_group):
        for q in range(pc.groups):
            rank = jnp.clip(rank_ref[i], 0, per_group)
            out_ref[i, :, q * pc.panel : (q + 1) * pc.panel] = arrived[q, rank]

    for b in range(blocks - 4, blocks):
        gone(to_core(b))

    def finish(b, carry):
        sent_off(b)
        return carry

    lax.fori_loop(sent_in_loop, blocks, finish, 0)


def back(pc, owners, ids, arrays, near, per_group):
    total = arrays[0].shape[0]
    rows, length = near[6].shape
    width = D // 2
    piece = width // pc.batch
    own_sections = SECTIONS // pc.groups
    hops = pc.nx - 1 + pc.ny - 1
    blocks = BLOCKS
    steps, small = pc.table_slots(), pc.small_slots()
    dma = pltpu.SemaphoreType.DMA
    vmem = pl.BlockSpec(memory_space=pltpu.VMEM)
    smem = pl.BlockSpec(memory_space=pltpu.SMEM)
    far = pl.BlockSpec(memory_space=pl.ANY)
    nz, nx, ny, half, panel = pc.nz, pc.nx, pc.ny, pc.half, pc.panel
    return pl.pallas_call(
        functools.partial(back_kernel, pc),
        out_shape=(
            like((per_group, piece, D)),
            like((own_sections, 8, D), float_out),
            like((8, 128), float_out),
        ),
        in_specs=[smem, smem] + [far] * len(arrays) + [far] * 5 + [vmem] * 5,
        out_specs=(vmem, vmem, vmem),
        scratch_shapes=[
            pltpu.VMEM((total, 1), jnp.int32),
            pltpu.SMEM((per_group * pc.groups,), jnp.int32),
            pltpu.SMEM((BLOCKS,), jnp.int32),
            pltpu.SMEM((per_group,), jnp.int32),
            pltpu.VMEM((pc.groups, per_group + 1, piece, panel), low),
            pltpu.VMEM((8, 128), float_out),
            pltpu.VMEM((2, total, width), low),
            pltpu.VMEM((2, total, D), low),
            pltpu.VMEM((2, width, half), float_out),
            pltpu.VMEM((4, nz, nx, piece, half), low),
            pltpu.VMEM((2 * nz + 4, nz, nx, piece, half), low),
            pltpu.VMEM((NEARS, nx - 1, nz // 2, piece, half), low),
            pltpu.VMEM((NEARS, ny - 1, nz - nz // 2, nx, piece, panel), low),
            pltpu.VMEM((NEARS, max(nx, ny) - 1, nz, piece, panel), low),
            pltpu.VMEM((NEARS, nz - 1, piece, panel), low),
            pltpu.VMEM((LONGS, nz - 1, nx, piece, half), low),
            pltpu.VMEM((LONGS, ny - 1, nx, piece, panel), low),
            pltpu.VMEM((LONGS, nx - 1, piece, panel), low),
            pltpu.VMEM((blocks + 1, piece, panel), low),
            pltpu.VMEM((pc.groups, per_group, piece, panel), low),
            pltpu.VMEM((1, panel), float_out),
            pltpu.VMEM((2, 4, length, 2 * HD), low),
            pltpu.VMEM((3, total, D), low),
            pltpu.VMEM((total, D), low),
            pltpu.VMEM((6, nz, nx, piece, D), low),
            pltpu.VMEM((2, 2, ROWS_AT_ONCE, D), float_out),
            pltpu.VMEM((rows, 8, D), float_out),
            pltpu.VMEM((own_sections * pc.groups, 8, D), float_out),
            pltpu.VMEM((steps, own_sections, 8, D), float_out),
            pltpu.VMEM((2, own_sections, 8, D), float_out),
            pltpu.VMEM((2, 8, 128), float_out),
            pltpu.VMEM((small, 8, 128), float_out),
            dma((2, 2)),
            dma((2, 4)),
            dma((2, 2)),
            dma,
            pltpu.SemaphoreType.REGULAR,
            dma((blocks,)),
            dma((blocks,)),
            dma((blocks, hops)),
            dma((blocks, hops)),
            dma((blocks, hops)),
            dma((blocks, hops)),
            dma((blocks, nz - 1)),
            dma((blocks, nz - 1)),
            dma((2, pc.groups - 1)),
            dma((2, pc.groups - 1)),
            dma((steps,)),
            dma((steps,)),
            dma((small,)),
            dma((small,)),
        ],
        name="back",
        compiler_params=pltpu.CompilerParams(
            collective_id=1, has_side_effects=True, vmem_limit_bytes=62 * MIB
        ),
    )(owners, ids, *arrays, *near)


def matrix(ref, first, count=2):
    return ref[first : first + count].reshape(count * ref.shape[1], ref.shape[2])


def row_block(width, count=ROWS_AT_ONCE):
    return pl.BlockSpec((count, width), lambda i: (i, 0))


def plane_block(planes, width=D, count=ROWS_AT_ONCE):
    return pl.BlockSpec((planes, count, width), lambda i: (0, i, 0))


def per_row(steps, height=8):
    return pl.BlockSpec((1, height, D), lambda i: (i // steps, 0, 0))


def compiler(mib):
    return pltpu.CompilerParams(vmem_limit_bytes=mib * MIB)


def cost(flops, reach, deep=0):
    return pl.CostEstimate(flops=flops, bytes_accessed=reach, transcendentals=deep)


def middle_kernel(
    steps,
    slope_ref,
    x1_ref,
    x2_ref,
    params_ref,
    targets_ref,
    w_ref,
    h3_ref,
    dlogits_ref,
    dffn_ref,
    du_ref,
    dattn_ref,
    do_ref,
    dx_ref,
    rows_ref,
    loss_ref,
    out_w,
    up_w,
    down_w,
    head_w,
    sems,
):
    step = pl.program_id(0)
    loads = [
        pltpu.make_async_copy(w_ref.at[pl.ds(first, dst.shape[0])], dst, sems.at[n])
        for n, (first, dst) in enumerate(
            ((HEAD, head_w), (DOWN, down_w), (UP, up_w), (OUT, out_w))
        )
    ]

    def ready(n):
        pl.when(step == 0)(loads[n].wait)

    pl.when(step == 0)(lambda: begin(loads))
    par = [params_ref[0, k : k + 1] for k in range(7)]
    n3, scale3 = normalize(x2_ref[...])
    h3 = (n3 * (1.0 + par[4]) + par[5]).astype(low)
    h3_ref[...] = h3
    ready(0)
    logits = times(h3, matrix(head_w, 0))
    top = jnp.max(logits, axis=-1, keepdims=True)
    lse = top + jnp.log(jnp.sum(jnp.exp(logits - top), axis=-1, keepdims=True))
    vocab = lax.broadcasted_iota(jnp.int32, logits.shape, 1)
    wanted = targets_ref[
        pl.ds(step // steps, 1),
        pl.ds(pl.multiple_of(step % steps * ROWS_AT_ONCE, ROWS_AT_ONCE), ROWS_AT_ONCE),
    ]
    picked = column_of(wanted) == vocab
    losses = lse - jnp.sum(jnp.where(picked, logits, 0.0), axis=-1, keepdims=True)
    weight = par[6]
    dlogits = ((jnp.exp(logits - lse) - jnp.where(picked, 1.0, 0.0)) * weight).astype(low)
    dlogits_ref[...] = dlogits
    dh3 = times_t(dlogits, matrix(head_w, 0))
    dx2, gain3, shift3 = norm_back(dh3, n3, scale3, par[4])
    dffn = dx2.astype(low)
    dffn_ref[...] = dffn
    dh2 = 0.0
    ready(1)
    ready(2)
    for g in range(4):
        du = (times_t(dffn, matrix(down_w, 2 * g)) * slope_ref[g].astype(float_out)).astype(low)
        du_ref[g] = du
        dh2 = dh2 + times_t(du, matrix(up_w, 2 * g))
    n2, scale2 = normalize(x1_ref[...])
    dx1, gain2, shift2 = norm_back(dh2, n2, scale2, par[2])
    dx1 = dx1 + dx2
    dx_ref[...] = dx1
    dattn = dx1.astype(low)
    dattn_ref[...] = dattn
    ready(3)
    do_ref[...] = times_t(dattn, matrix(out_w, 0)).astype(low)
    grads = jnp.concatenate([gain2, shift2, gain3, shift3], axis=0)

    @pl.when(step == 0)
    def _():
        loss_ref[...] = jnp.zeros_like(loss_ref)

    @pl.when(step % steps == 0)
    def _():
        rows_ref[...] = jnp.zeros_like(rows_ref)

    rows_ref[0, 2:6] += grads
    loss_ref[...] += jnp.sum(losses) * weight[:, :128]


def middle(w, slope, x1, x2, params, targets, length):
    total = x1.shape[0]
    steps = length // ROWS_AT_ONCE
    rows = total // length
    return pl.pallas_call(
        functools.partial(middle_kernel, steps),
        grid=(total // ROWS_AT_ONCE,),
        out_shape=(
            like((total, D)),
            like((total, CODES)),
            like((total, D)),
            like((4, total, D)),
            like((total, D)),
            like((total, D)),
            like((total, D), float_out),
            like((rows, 8, D), float_out),
            like((8, 128), float_out),
        ),
        in_specs=[
            plane_block(4),
            row_block(D),
            row_block(D),
            per_row(steps),
            pl.BlockSpec(targets.shape, lambda i: (0, 0)),
            pl.BlockSpec(memory_space=pl.ANY),
        ],
        out_specs=(
            row_block(D),
            row_block(CODES),
            row_block(D),
            plane_block(4),
            row_block(D),
            row_block(D),
            row_block(D),
            per_row(steps),
            pl.BlockSpec((8, 128), lambda i: (0, 0)),
        ),
        scratch_shapes=[
            *(pltpu.VMEM((count, D // 2, D), low) for count in (2, 8, 8, 2)),
            pltpu.SemaphoreType.DMA((4,)),
        ],
        name="middle",
        compiler_params=compiler(62),
        cost_estimate=cost(22 * total * D * D, 60 * MIB, 2 * total * D),
    )(slope, x1, x2, params, targets, w)


def adam(weight, first, second, grad, rate, fixes):
    new_first = beta_one * first + (1.0 - beta_one) * grad
    new_second = beta_two * second + (1.0 - beta_two) * grad * grad
    update = new_first * fixes[0] / (jnp.sqrt(new_second * fixes[1]) + adam_eps)
    return (weight - rate * (update + decay_rate * weight), new_first, new_second)


def update_kernel(
    step_ref,
    sums_ref,
    table_grad_ref,
    table_ref,
    table_first_ref,
    table_second_ref,
    grad_ref,
    masters_ref,
    first_ref,
    second_ref,
    new_masters,
    new_first,
    new_second,
    new_table,
    new_table_first,
    new_table_second,
    norm_ref,
    loss_ref,
    grad,
    state,
    made,
    in_sem,
    out_sem,
):
    slots = masters_ref.shape[0]

    def loads(i):
        copies = [pltpu.make_async_copy(grad_ref.at[i], grad.at[i], in_sem.at[i, 3])]
        for n, ref in enumerate((masters_ref, first_ref, second_ref)):
            copies.append(pltpu.make_async_copy(ref.at[i], state.at[n, i], in_sem.at[i, n]))
        return copies

    def stores(i):
        return [
            pltpu.make_async_copy(made.at[n, i], ref.at[i], out_sem.at[i, n])
            for n, ref in enumerate((new_masters, new_first, new_second))
        ]

    for i in range(slots):
        begin(loads(i))
    step = jnp.full((1, 128), step_ref[0]).astype(float_out)
    fixes = [
        1.0 / (1.0 - jnp.exp(step * math.log(beta)))[:, :1] for beta in (beta_one, beta_two)
    ]
    norm = jnp.sqrt(sums_ref[0:1, 0:1])
    clip = jnp.minimum(1.0, clip_limit / norm)
    norm_ref[...] = norm
    loss_ref[...] = sums_ref[0:1, 1:2]
    for n in range(table_ref.shape[0]):
        for k in range(6):
            at = (slice(n, n + 1), slice(k * D, (k + 1) * D))
            new_table[at], new_table_first[at], new_table_second[at] = adam(
                table_ref[at],
                table_first_ref[at],
                table_second_ref[at],
                table_grad_ref[n, k : k + 1] * clip,
                table_rate,
                fixes,
            )

    def one(i, carry):
        for copy in loads(i):
            copy.wait()
        results = adam(
            state[0, i],
            state[1, i],
            state[2, i],
            grad[i].astype(float_out) * clip,
            learn_rate,
            fixes,
        )
        for n, value in enumerate(results):
            made[n, i] = value
        begin(stores(i))
        return carry

    lax.fori_loop(0, slots, one, 0)
    for i in range(slots):
        for copy in stores(i):
            copy.wait()


def update(step, sums, grad, masters, first, second, table_grad, table, table_first, table_second):
    slots = masters.shape[0]
    vmem = pl.BlockSpec(memory_space=pltpu.VMEM)
    far = pl.BlockSpec(memory_space=pl.ANY)
    dma = pltpu.SemaphoreType.DMA
    return pl.pallas_call(
        update_kernel,
        out_shape=(
            *(like(masters.shape, float_out) for _ in range(3)),
            *(like(table.shape, float_out) for _ in range(3)),
            like((1, 1), float_out),
            like((1, 1), float_out),
        ),
        in_specs=[pl.BlockSpec(memory_space=pltpu.SMEM)] + [vmem] * 5 + [far] * 4,
        out_specs=(far, far, far, vmem, vmem, vmem, vmem, vmem),
        scratch_shapes=[
            pltpu.VMEM(grad.shape, low),
            pltpu.VMEM((3, *masters.shape), float_out),
            pltpu.VMEM((3, *masters.shape), float_out),
            dma((slots, 4)),
            dma((slots, 3)),
        ],
        name="update",
        compiler_params=compiler(62),
        cost_estimate=cost(20 * masters.size, 28 * masters.size),
    )(step, sums, table_grad, table, table_first, table_second, grad, masters, first, second)


def per_device(
    pc,
    masters,
    first_moment,
    second_moment,
    section_table,
    table_first,
    table_second,
    owners,
    step_count,
    phones,
    codes,
    segments,
    sections,
    targets,
):
    row_count, length = segments.shape
    ids = sections.reshape(1, row_count)
    blocks, params, multi, phone_hot, x0, h1, qkv, mixed, lse, x1, h2, act, slope, x2 = front(
        pc, owners, ids, masters, section_table, codes.swapaxes(1, 2), phones, segments
    )
    w = blocks.reshape(BLOCKS, D // 2, D)
    qkv = qkv.reshape(3, row_count * length, D)
    mixed = mixed.reshape(row_count * length, D)
    h3, dlogits, dffn, du, dattn, do, dx1, row_sums, loss_part = middle(
        w, slope, x1, x2, params, targets, length
    )
    own_grad, table_grad, sums = back(
        pc,
        owners,
        ids,
        (h3, act, h2, mixed, h1, multi, phone_hot, dlogits, dffn, du, dattn),
        (qkv, do, x0, dx1, blocks, lse, segments, params, row_sums, loss_part),
        masters.shape[0],
    )
    *state, grad_norm, loss = update(
        step_count,
        sums,
        own_grad,
        masters,
        first_moment,
        second_moment,
        table_grad,
        section_table,
        table_first,
        table_second,
    )
    return (*state, grad_norm.reshape(()), loss.reshape(()))


def solution(mesh):
    return jax.shard_map(
        functools.partial(per_device, Place(mesh)),
        mesh=mesh,
        in_specs=(
            P("section", "batch", None),
            P("section", "batch", None),
            P("section", "batch", None),
            P("section", None),
            P("section", None),
            P("section", None),
            P(),
            P(),
            P(("section", "batch"), None),
            P(("section", "batch"), None, None),
            P(("section", "batch"), None),
            P(("section", "batch"), None),
            P(("section", "batch"), None),
        ),
        out_specs=(
            P("section", "batch", None),
            P("section", "batch", None),
            P("section", "batch", None),
            P("section", None),
            P("section", None),
            P("section", None),
            P(),
            P(),
        ),
        check_vma=False,
    )
```

```python
import functools
import math

import jax
import jax.numpy as jnp
import numpy as np
from jax import lax
from jax.experimental import pallas as pl
from jax.experimental.pallas import tpu as pltpu
from jax.sharding import PartitionSpec as P

D = 1024
HEADS = 16
HD = 64
CODES = 1024
LEVELS = 8
PHONES = 512
SECTIONS = 8
CORES = 2

clip_limit = 0.002
learn_rate = 0.02
table_rate = 0.1
beta_one = 0.9
beta_two = 0.95
adam_eps = 1e-08
decay_rate = 0.1
norm_eps = 1e-05
pos_scale = 0.1
float_out = jnp.float32
low = jnp.bfloat16
MESH = pl.DeviceIdType.MESH
MIB = 1 << 20


class Place:
    def __init__(self, mesh):
        self.groups = mesh.shape["section"]
        self.batch = mesh.shape["batch"]
        self.ny = self.groups // CORES
        self.nx = 1 << (int(math.log2(self.batch)) // 2)
        self.nz = self.batch // self.nx
        self.panel = D // self.groups
        self.half = D // CORES

    def here(self):
        self.s = lax.axis_index("section")
        self.j = lax.axis_index("batch")
        self.y = lax.div(self.s, CORES)
        self.c = lax.rem(self.s, CORES)
        self.z = lax.div(self.j, self.nx)
        self.x = lax.rem(self.j, self.nx)
        self.sections = [lax.rem(self.s + d, self.groups) for d in range(self.groups)]
        self.xs = [lax.rem(self.x + d, self.nx) for d in range(self.nx)]
        self.ys = [lax.rem(self.y + d, self.ny) for d in range(self.ny)]
        self.zs = [lax.rem(self.z + d, self.nz) for d in range(self.nz)]
        self.x_peers = [(self.s, self.z * self.nx + x) for x in self.xs]
        self.y_peers = [(y * CORES + self.c, self.j) for y in self.ys]
        self.z_peers = [(self.s, z * self.nx + self.x) for z in self.zs]
        self.core_peer = (self.y * CORES + (1 - self.c), self.j)

    def panel_of(self, s):
        return lax.rem(s, CORES) * self.ny + lax.div(s, CORES)

    def section_peer(self, d):
        return self.sections[d]

    def x_of(self, d):
        return self.xs[d]

    def y_of(self, d):
        return self.ys[d]

    def z_of(self, d):
        return self.zs[d]

    def at_x(self, d):
        return self.x_peers[d]

    def at_y(self, d):
        return self.y_peers[d]

    def at_z(self, d):
        return self.z_peers[d]

    def at_core(self):
        return self.core_peer

    def columns(self, index, width):
        return pl.ds(pl.multiple_of(index * width, width), width)

    def near_peers(self):
        return [
            (self.sections[d], self.z * self.nx + self.xs[e])
            for d in range(self.groups)
            for e in range(self.nx)
            if d or e
        ]

    def barrier(self):
        sem = pltpu.get_barrier_semaphore()
        peers = self.near_peers() + [self.at_z(d) for d in range(1, self.nz)]
        for peer in peers:
            pl.semaphore_signal(sem, inc=1, device_id=peer, device_id_type=MESH)
        pl.semaphore_wait(sem, len(peers))

    def small_slots(self):
        return (self.groups * self.nx - 1) + (self.nz - 1)

    def table_slots(self):
        return (self.groups - 1) + (self.nx - 1) + (self.nz - 1)

    def small_stages(self, held, sent, landed, send_sem, recv_sem):
        near = self.near_peers()
        far = [self.at_z(d) for d in range(1, self.nz)]

        def stage(number, peers, first):
            copies = [
                remote(
                    sent.at[number],
                    landed.at[first + n],
                    send_sem.at[first + n],
                    recv_sem.at[first + n],
                    peer,
                )
                for n, peer in enumerate(peers)
            ]

            def start():
                sent[number] = held[...]
                for copy in copies:
                    copy.start()

            def end():
                for copy in copies:
                    copy.wait()
                total = held[...]
                for n in range(len(peers)):
                    total = total + landed[first + n]
                held[...] = total

            return start, end

        return [stage(0, near, 0), stage(1, far, len(near))]


def remote(src, dst, send_sem, recv_sem, device):
    return pltpu.make_async_remote_copy(
        src_ref=src,
        dst_ref=dst,
        send_sem=send_sem,
        recv_sem=recv_sem,
        device_id=device,
        device_id_type=MESH,
    )


ROWS_AT_ONCE = 256
BLOCKS = 29
CODE, PHONE, QKV, OUT, UP, DOWN, HEAD = 0, 2, 3, 9, 11, 19, 27
FRONT = 9
OUTWARD = (0, 1, 2, 5, 6, 7, 8, 9, 10, 11, 12, *range(13, 29), 3, 4)
HOMEWARD = (3, 4, *range(21, 29), *range(13, 21), 11, 12, 5, 6, 7, 8, 9, 10, 0, 1, 2)


def begin(copies):
    for copy in copies:
        copy.start()


def landed_all(copies):
    for copy in copies:
        copy.wait_recv()


def gone(copies):
    for copy in copies:
        copy.wait_send()


LONG_EVERY = 7
LONG_OUT, LONG_HOME = 3, 1
LONGS = len(range(LONG_HOME, BLOCKS, LONG_EVERY))
NEARS = BLOCKS - LONGS


def place_among(b):
    return b - lax.div(b + (LONG_EVERY - 1 - LONG_HOME), LONG_EVERY)


def by_kind(b, at, near=None, far=None):
    long = lax.rem(b, LONG_EVERY) == at
    if near is not None:
        pl.when(jnp.logical_not(long))(near)
    if far is not None:
        pl.when(long)(far)


def rank_cuts(per_group):
    return sorted({0, min(2, per_group), min(4, per_group), per_group})


def rank_keys(owners_ref, order, per_group, groups):
    seen = [jnp.int32(0)] * groups
    keys = []
    for b in order:
        section = jnp.clip(lax.div(owners_ref[b], per_group), 0, groups - 1)
        rank = jnp.int32(0)
        for g in range(groups):
            rank = jnp.where(section == g, seen[g], rank)
            seen[g] = seen[g] + jnp.where(section == g, 1, 0)
        keys.append(section * per_group + jnp.minimum(rank, per_group - 1))
    return keys


def within(value, count):
    return (value >= 0) & (value < count)


def times(a, b):
    return lax.dot_general(a, b, (((1,), (0,)), ((), ())), preferred_element_type=float_out)


def times_t(a, b):
    return lax.dot_general(a, b, (((1,), (1,)), ((), ())), preferred_element_type=float_out)


def turned_times(a, b):
    return lax.dot_general(a, b, (((0,), (0,)), ((), ())), preferred_element_type=float_out)


def normalize(stream):
    centred = stream - jnp.mean(stream, axis=-1, keepdims=True)
    scale = lax.rsqrt(jnp.mean(centred * centred, axis=-1, keepdims=True) + norm_eps)
    return (centred * scale, scale)


def norm_back(grad, normed, scale, gain):
    inner = grad * (1.0 + gain)
    result = scale * (
        inner
        - jnp.mean(inner, axis=-1, keepdims=True)
        - normed * jnp.mean(inner * normed, axis=-1, keepdims=True)
    )
    return (
        result,
        jnp.sum(grad * normed, axis=0, keepdims=True),
        jnp.sum(grad, axis=0, keepdims=True),
    )


def rates():
    column = np.arange(D)
    return column, np.exp(-(2 * (column // 2)) * (math.log(10000.0) / D))


def index_waves(length):
    column, rate = rates()
    angle = np.arange(length)[:, None] * rate
    sine, cosine = np.sin(angle), np.cos(angle)
    even = column % 2 == 0
    same = pos_scale * np.where(even, sine, cosine)
    other = pos_scale * np.where(even, cosine, sine)
    return jnp.asarray(same, jnp.float32), jnp.asarray(other, jnp.float32)


def column_of(row):
    wide = jnp.broadcast_to(row.astype(float_out), (128, row.shape[1]))
    return wide.T[:, :1].astype(jnp.int32)


def masks():
    lane = lax.broadcasted_iota(jnp.int32, (1, 2 * HD), 1)
    return [(lane // HD == h).astype(low) for h in range(2)]


def in_turn(items, first, middle, last):
    ahead, behind = first(*items[0]), None
    for n, item in enumerate(items):
        now = ahead
        if n + 1 < len(items):
            ahead = first(*items[n + 1])
        made = middle(*item, *now)
        if behind is not None:
            last(*behind)
        behind = (*item, *made)
    last(*behind)


def attend_pairs(same, heads):
    turned = [v.astype(float_out).T.astype(low) for _, _, v in heads]
    outs = [[] for _ in heads]
    stats = [[] for _ in heads]
    scaled = [mask * HD ** (-0.5) for mask in masks()]

    def first(n, h):
        q, k, _ = heads[n]
        return (times_t(k, q * scaled[h]),)

    def middle(n, h, scores):
        scores = jnp.where(same, scores, -1000000000.0)
        top = jnp.max(scores, axis=0, keepdims=True)
        powers = jnp.exp(scores - top)
        total = jnp.sum(powers, axis=0, keepdims=True)
        stats[n].append(top + jnp.log(total))
        return ((powers * (1.0 / total)).astype(low),)

    def last(n, h, probs):
        outs[n].append(times(turned[n][h * HD : (h + 1) * HD], probs))

    in_turn([(n, h) for n in range(len(heads)) for h in range(2)], first, middle, last)
    return [jnp.concatenate(out, axis=0).T.astype(low) for out in outs], stats


def attend_pair_back(same, q, k, v, do, stats):
    k_turned = (k.astype(float_out) * HD ** (-0.5)).T.astype(low)
    width = q.shape[0] // 2
    q_of = [q * (mask * HD ** (-0.5)) for mask in masks()]
    do_of = [do * mask for mask in masks()]
    dq = [[], []]
    sums = [0.0, 0.0]

    def part(c):
        return slice(c * width, (c + 1) * width)

    def first(c, h):
        return times_t(k, q_of[h][part(c)]), times_t(v, do_of[h][part(c)])

    def middle(c, h, scores, grad):
        scores = jnp.where(same[:, part(c)], scores, -1000000000.0)
        probs = jnp.exp(scores - stats[h][:, part(c)])
        level = jnp.sum(probs * grad, axis=0, keepdims=True)
        return probs.astype(low), (probs * (grad - level)).astype(low)

    def last(c, h, probs, back):
        sums[0] = sums[0] + times(back, q_of[h][part(c)])
        sums[1] = sums[1] + times(probs, do_of[h][part(c)])
        dq[h].append(times(k_turned[h * HD : (h + 1) * HD], back))

    in_turn([(c, h) for c in range(2) for h in range(2)], first, middle, last)
    turned = jnp.concatenate([jnp.concatenate(parts, axis=1) for parts in dq], axis=0)
    return turned.T.astype(low), sums[0].astype(low), sums[1].astype(low)


def front_kernel(
    pc,
    owners_ref,
    ids_ref,
    masters_ref,
    raw_table,
    codes_ref,
    phones_ref,
    segs_ref,
    rate_ref,
    same_ref,
    other_ref,
    w_ref,
    params_ref,
    multi_out,
    hot_out,
    x_out,
    h_out,
    qkv_out,
    mixed_out,
    lse_ref,
    x1_out,
    h2_out,
    act_out,
    slope_out,
    x2_out,
    table_ref,
    seg_col,
    phone_col,
    code_cols,
    starts_ref,
    waves,
    rounded,
    ordered,
    counts_ref,
    *rest,
):
    parts = len(rank_cuts(ordered.shape[0])) - 1
    slots = rest[:parts]
    (
        pieces,
        table_all,
        wf,
        multi,
        hot,
        x0,
        h1,
        pool,
        wo,
        h2,
        act,
        slope,
        sent,
        landed,
        key_ref,
        in_sem,
        a_send,
        a_recv,
        t_send,
        t_recv,
        own_sem,
        z_send,
        z_recv,
        e_send,
        e_recv,
        f_send,
        f_recv,
        c_send,
        c_recv,
        m_send,
        m_recv,
        w_sem,
        out_sem,
        qkv_sem,
        mix_sem,
        o_sem,
        u_sem,
        d_sem,
        x1_sem,
        act_sem,
        x2_sem,
    ) = rest[parts:]
    pc.here()
    blocks = BLOCKS
    per_group, piece = rounded.shape[:2]
    own_sections = table_ref.shape[0]
    rows, length = segs_ref.shape
    steps = length // ROWS_AT_ONCE
    pairs = HEADS // 2
    mine = pc.columns(pc.panel_of(pc.s), pc.panel)
    core_half = pc.columns(pc.c, pc.half)
    loads = [
        pltpu.make_async_copy(
            masters_ref, x0.at[pl.ds(0, per_group * piece)], in_sem.at[0]
        ),
        pltpu.make_async_copy(same_ref, waves.at[0], in_sem.at[1]),
        pltpu.make_async_copy(other_ref, waves.at[1], in_sem.at[2]),
    ]
    begin(loads)
    keys = rank_keys(owners_ref, OUTWARD, per_group, pc.groups)
    for p in range(blocks):
        key_ref[p] = keys[p]
    base = pc.s * per_group
    slot_of = []
    for k in range(per_group):
        slot = jnp.int32(0)
        for p in range(blocks):
            slot = jnp.where(keys[p] == base + k, owners_ref[OUTWARD[p]] - base, slot)
        slot_of.append(slot)
    table_ref[...] = jnp.zeros_like(table_ref)
    for k in range(6):
        for n in range(own_sections):
            table_ref[n, k : k + 1] = raw_table[n : n + 1, k * D : (k + 1) * D]
    pc.barrier()
    loads[0].wait()
    rounded[...] = x0[: per_group * piece].astype(low).reshape(rounded.shape)
    for k in range(per_group):
        ordered[k] = rounded[jnp.clip(slot_of[k], 0, per_group - 1)]
    cuts = rank_cuts(per_group)
    for m, place in enumerate(slots):
        for k in range(cuts[m], cuts[m + 1]):
            place[pc.s, k - cuts[m]] = ordered[k, :, mine]

    def exchange(m):
        first, count = cuts[m], cuts[m + 1] - cuts[m]
        return [
            remote(
                ordered.at[
                    pl.ds(first, count),
                    :,
                    pc.columns(pc.panel_of(pc.section_peer(d)), pc.panel),
                ],
                slots[m].at[pc.s],
                a_send.at[m, d - 1],
                a_recv.at[m, d - 1],
                (pc.section_peer(d), pc.j),
            )
            for d in range(1, pc.groups)
        ]

    def table_exchange():
        return [
            remote(
                table_ref,
                table_all.at[pl.ds(pc.s * own_sections, own_sections)],
                t_send.at[d - 1],
                t_recv.at[d - 1],
                (pc.section_peer(d), pc.j),
            )
            for d in range(1, pc.groups)
        ]

    for m in range(len(cuts) - 1):
        begin(exchange(m))
    begin(table_exchange())
    table_all[pl.ds(pc.s * own_sections, own_sections)] = table_ref[...]
    section = lax.broadcasted_iota(jnp.int32, (SECTIONS, 128), 0)
    counts = jnp.zeros((SECTIONS, 128), jnp.float32)
    for r in range(rows):
        counts = counts + jnp.where(section == ids_ref[0, r], float(length), 0.0)
    counts_ref[...] = counts
    small = pc.small_stages(counts_ref, sent, landed, m_send, m_recv)

    def take_pieces(m):
        for copy in exchange(m):
            copy.wait()
        until = cuts[m + 1] if m + 2 < len(cuts) else blocks
        for p in range(cuts[m], until):
            key = jnp.clip(key_ref[p], 0, per_group * pc.groups - 1)
            section, rank = lax.div(key, per_group), lax.rem(key, per_group)
            found = slots[0][section, jnp.minimum(rank, cuts[1] - 1)]
            for n in range(1, m + 1):
                last = cuts[n + 1] - cuts[n] - 1
                here = slots[n][section, jnp.clip(rank - cuts[n], 0, last)]
                found = jnp.where(rank >= cuts[n], here, found)
            pieces[p] = found

    def set_params():
        for copy in table_exchange():
            copy.wait()
        line = lax.broadcasted_iota(jnp.int32, (8, D), 0)
        for r in range(rows):
            held = jnp.sum(
                jnp.where(section == ids_ref[0, r], counts_ref[...], 0.0), axis=0, keepdims=True
            )
            weight = 1.0 / (SECTIONS * jnp.concatenate([held] * (D // 128), axis=1))
            params_ref[r] = jnp.where(line == 6, weight, table_all[ids_ref[0, r]])

    def own(p):
        return pltpu.make_async_copy(
            pieces.at[p], w_ref.at[p, pc.z, pc.x, :, mine], own_sem.at[p]
        )

    def along_z(p):
        return [
            remote(
                pieces.at[p],
                w_ref.at[p, pc.z, pc.x, :, mine],
                z_send.at[p, d - 1],
                z_recv.at[p, d - 1],
                pc.at_z(d),
            )
            for d in range(1, pc.nz)
        ]

    def spread(p, part, send_sem, recv_sem, count, target, source=None, first=0):
        source = part if source is None else source
        return [
            remote(
                source,
                part,
                send_sem.at[p, first + d - 1],
                recv_sem.at[p, first + d - 1],
                target(d),
            )
            for d in range(1, count)
        ]

    middle_z = pc.nz // 2
    lower, upper = pl.ds(0, middle_z), pl.ds(middle_z, pc.nz - middle_z)

    def first_x(p):
        part = w_ref.at[p, lower, pc.x, :, mine]
        return spread(p, part, e_send, e_recv, pc.nx, pc.at_x)

    def first_y(p):
        part = w_ref.at[p, upper, pc.x, :, mine]
        return spread(p, part, e_send, e_recv, pc.ny, pc.at_y, first=pc.nx - 1)

    def then_y(p):
        part = w_ref.at[p, lower, :, :, mine]
        return spread(p, part, f_send, f_recv, pc.ny, pc.at_y)

    def then_x(p):
        part = w_ref.at[p, upper, pc.x, :, core_half]
        return spread(p, part, f_send, f_recv, pc.nx, pc.at_x, first=pc.ny - 1)

    def far_x(p):
        part = w_ref.at[p, pc.z, pc.x, :, mine]
        return spread(p, part, e_send, e_recv, pc.nx, pc.at_x, pieces.at[p])

    def far_y(p):
        part = w_ref.at[p, pc.z, :, :, mine]
        return spread(p, part, f_send, f_recv, pc.ny, pc.at_y)

    def ring(p, k):
        part = w_ref.at[p, pc.z_of((pc.nz - k + 1) % pc.nz), :, :, core_half]
        return [remote(part, part, z_send.at[p, k - 1], z_recv.at[p, k - 1], pc.at_z(1))]

    def to_core(p):
        part = w_ref.at[p, :, :, :, core_half]
        return [remote(part, part, c_send.at[p], c_recv.at[p], pc.at_core())]

    def into_vmem(p):
        return pltpu.make_async_copy(w_ref.at[p], wf.at[p], w_sem.at[p])

    for r in range(rows):
        at = pl.ds(r * length, length)
        tall = jnp.concatenate(
            [codes_ref[r].astype(float_out), jnp.zeros((128 - LEVELS, length), float_out)], axis=0
        )
        code_cols[at] = tall.T.astype(jnp.int32)
        seg_col[pl.ds(r * length, length)] = column_of(segs_ref[r : r + 1])
        phone_col[pl.ds(r * length, length)] = column_of(phones_ref[r : r + 1])
        starts = [
            jnp.sum(jnp.where(segs_ref[r : r + 1] < k, 1.0, 0.0), axis=1, keepdims=True)
            for k in (0, 1, 2)
        ]
        angle = jnp.concatenate(starts, axis=0) * rate_ref[...]
        odd = lax.broadcasted_iota(jnp.int32, angle.shape, 1) % 2
        starts_ref[r, 0:3] = jnp.cos(angle)
        starts_ref[r, 3:6] = jnp.where(odd == 1, 1.0, -1.0) * jnp.sin(angle)

    def chunk(i):
        return pl.ds(i * ROWS_AT_ONCE, ROWS_AT_ONCE)

    def embed_out(i):
        made = ((multi, multi_out), (hot, hot_out), (x0, x_out), (h1, h_out))
        return [
            pltpu.make_async_copy(a.at[chunk(i)], b.at[chunk(i)], out_sem.at[i, n])
            for n, (a, b) in enumerate(made)
        ]

    def qkv_copy(n):
        return pltpu.make_async_copy(pool.at[n], qkv_out.at[n], qkv_sem.at[n])

    def weight(first, count=2):
        return wf[first : first + count].reshape(count * D // 2, D)

    def prepare_step(i):
        at = chunk(i)
        r, local = i // steps, pl.ds((i % steps) * ROWS_AT_ONCE, ROWS_AT_ONCE)
        vocab = lax.broadcasted_iota(jnp.int32, (ROWS_AT_ONCE, CODES), 1)
        count = jnp.zeros((ROWS_AT_ONCE, CODES), jnp.float32)
        for level in range(LEVELS):
            code = code_cols[at, level : level + 1]
            code = jnp.where(ids_ref[0, r] >= level, code, -1)
            count = count + jnp.where(code == vocab, 1.0, 0.0)
        multi[at] = count.astype(low)
        names = lax.broadcasted_iota(jnp.int32, (ROWS_AT_ONCE, PHONES), 1)
        hot[at] = jnp.where(phone_col[at] == names, 1.0, 0.0).astype(low)
        segs = seg_col[at]
        cosine, sine = (
            jnp.where(
                segs == 0,
                starts_ref[r, k : k + 1],
                jnp.where(segs == 1, starts_ref[r, k + 1 : k + 2], starts_ref[r, k + 2 : k + 3]),
            )
            for k in (0, 3)
        )
        x0[at] = waves[0, local] * cosine + waves[1, local] * sine

    def embed_step(i):
        at, r = chunk(i), i // steps
        stream = times(multi[at], weight(CODE)) + times(hot[at], weight(PHONE, 1)) + x0[at]
        x0[at] = stream
        normed, _ = normalize(stream)
        h1[at] = (normed * (1.0 + params_ref[r, 0:1]) + params_ref[r, 1:2]).astype(low)
        begin(embed_out(i))

    def project_step(k):
        for r in range(rows):
            made = times(h1[r * length : (r + 1) * length], wf[pl.ds(QKV + 2 * k, 2)].reshape(D, D))
            pool[rows * k + r] = made.astype(low).reshape(pool.shape[1:])
            qkv_copy(rows * k + r).start()

    def row(r):
        return pl.ds(r * length, length)

    def mixed_copy(r):
        return pltpu.make_async_copy(pool.at[3 * rows + r], mixed_out.at[r], mix_sem.at[r])

    def attend_step(n):
        r, h = lax.div(2 * n, pairs), lax.rem(2 * n, pairs)
        same = seg_col[row(r)] == segs_ref[pl.ds(r, 1)]
        at = [pc.columns(h + e, 2 * HD) for e in range(2)]
        outs, stats = attend_pairs(
            same,
            [
                [
                    pool[rows * k + r, :, :, :, columns].reshape(length, 2 * HD)
                    for k in range(3)
                ]
                for columns in at
            ],
        )
        for e in range(2):
            pool[3 * rows + r, :, :, :, at[e]] = outs[e].reshape(*pool.shape[1:4], 2 * HD)
            for k, lse in enumerate(stats[e]):
                lse_ref[r, h + e, k : k + 1] = lse

        @pl.when(h + 2 == pairs)
        def _():
            mixed_copy(r).start()

    def out_weight():
        return pltpu.make_async_copy(w_ref.at[pl.ds(OUT, 2)], wo, o_sem)

    def up_weight():
        return pltpu.make_async_copy(w_ref.at[pl.ds(UP, 8)], wf.at[pl.ds(0, 8)], u_sem)

    def down_weight(p):
        return pltpu.make_async_copy(w_ref.at[p], pool.at[p - DOWN], d_sem.at[p - DOWN])

    def stream_copies(i):
        return [
            pltpu.make_async_copy(x0.at[chunk(i)], x1_out.at[chunk(i)], x1_sem.at[i, 0]),
            pltpu.make_async_copy(h2.at[chunk(i)], h2_out.at[chunk(i)], x1_sem.at[i, 1]),
        ]

    def act_copy(i):
        return pltpu.make_async_copy(
            act.at[:, chunk(i)], act_out.at[:, chunk(i)], act_sem.at[i, 0]
        )

    def slope_copy(i):
        return pltpu.make_async_copy(
            slope.at[i % 2], slope_out.at[:, chunk(i)], act_sem.at[i, 1]
        )

    def out_step(i):
        at, r = chunk(i), i // steps
        for copy in embed_out(i):
            copy.wait()
        depth = pc.nz // steps
        mixed = pool[3 * rows + r, pl.ds(i % steps * depth, depth)].reshape(ROWS_AT_ONCE, D)
        stream = x0[at] + times(mixed, wo[...].reshape(D, D))
        x0[at] = stream
        normed, _ = normalize(stream)
        h2[at] = (normed * (1.0 + params_ref[r, 2:3]) + params_ref[r, 3:4]).astype(low)
        begin(stream_copies(i))

    def up_step(i):
        at = chunk(i)

        @pl.when(i >= 2)
        def _():
            slope_copy(i - 2).wait()

        for g in range(4):
            u = times(h2[at], weight(2 * g))
            cdf = 0.5 + 0.5 * lax.erf(u * math.sqrt(0.5))
            density = jnp.exp(-0.5 * (u * u)) * (1.0 / math.sqrt(2.0 * math.pi))
            act[g, at] = (u * cdf).astype(low)
            slope[i % 2, g] = (cdf + u * density).astype(low)
        begin([act_copy(i), slope_copy(i)])

    def x2_copy(r):
        return pltpu.make_async_copy(x0.at[row(r)], x2_out.at[row(r)], x2_sem.at[r])

    def down_step(g):
        down_weight(DOWN + 2 * g).wait()
        down_weight(DOWN + 2 * g + 1).wait()
        for r in range(rows):
            at = row(r)
            x0[at] = x0[at] + times(act[g, at], pool[2 * g : 2 * g + 2].reshape(D, D))
            if g == 3:
                x2_copy(r).start()

    ahead = 4
    hops = pc.nz - 1
    embed_steps = rows * steps
    lands = [
        p + (2 * hops + 1 if p % LONG_EVERY == LONG_OUT else 6) for p in range(blocks)
    ]
    embed_from = max(lands[:QKV]) + 1
    project_from = max(
        embed_from + embed_steps,
        *(max(lands[QKV + 2 * k : QKV + 2 * k + 2]) + 1 - k for k in range(3)),
    )
    attend_from = project_from + 3
    out_from = max(attend_from + rows * pairs // 2, max(lands[OUT:UP]) + 2)
    out_ticks = embed_steps // 2
    up_fetch = max(max(lands[UP:DOWN]) + 1, attend_from)
    up_from = max(out_from + out_ticks, up_fetch + 1)
    free_at = out_from + out_ticks
    direct = max([p + 1 for p in range(DOWN, HEAD) if lands[p] < free_at], default=DOWN)
    copied = {p: max(lands[p], free_at if p < direct else 0) for p in range(DOWN, HEAD)}
    down_at = []
    for g in range(4):
        landed_by = max(copied[DOWN + 2 * g], copied[DOWN + 2 * g + 1]) + 1
        after = down_at[-1] + 1 if down_at else up_from + embed_steps
        down_at.append(max(landed_by, after))

    def step(p, body):
        pl.when(within(p, blocks))(lambda: body(p))

    def launch(p):
        own(p).start()
        by_kind(p, LONG_OUT, lambda: begin(along_z(p)), lambda: begin(far_x(p)))

    def far_second(p):
        def far():
            own(p).wait()
            landed_all(far_x(p))
            begin(far_y(p))

        by_kind(p, LONG_OUT, far=far)

    def first(p):
        def near():
            own(p).wait()
            landed_all(along_z(p))
            begin(first_x(p) + first_y(p))

        def far():
            landed_all(far_y(p))
            begin(ring(p, 1))

        by_kind(p, LONG_OUT, near, far)

    def ring_on(k):
        def body(p):
            def far():
                landed_all(ring(p, k - 1))
                begin(ring(p, k))

            by_kind(p, LONG_OUT, far=far)

        return body

    def then(p):
        def near():
            landed_all(first_x(p))
            begin(then_y(p))
            landed_all(first_y(p))
            begin(then_x(p))

        by_kind(p, LONG_OUT, near)

    def core_near(p):
        def near():
            landed_all(then_y(p) + then_x(p))
            begin(to_core(p))

        by_kind(p, LONG_OUT, near)

    def core_far(p):
        def far():
            landed_all(ring(p, hops))
            begin(to_core(p))

        by_kind(p, LONG_OUT, far=far)

    def arrived(p):
        landed_all(to_core(p))

        @pl.when(p < FRONT)
        def _():
            into_vmem(p).start()

        @pl.when((p >= direct) & (p < HEAD))
        def _():
            down_weight(p).start()

    sent_after = 2 * hops + 4

    def sent_off(p):
        gone(to_core(p))

        def near():
            gone(along_z(p) + first_x(p) + first_y(p) + then_y(p) + then_x(p))

        def far():
            gone(far_x(p) + far_y(p))
            for k in range(1, pc.nz):
                gone(ring(p, k))

        by_kind(p, LONG_OUT, near, far)

    def tick(turn, carry):
        t = turn - ahead
        for m in range(len(cuts) - 1):
            pl.when(turn == cuts[m])(functools.partial(take_pieces, m))
        step(turn, launch)
        step(t + 2, far_second)
        step(t, first)
        step(t - 2, then)
        for k in range(2, pc.nz):
            step(t - 2 * (k - 1), ring_on(k))
        step(t - 5, core_near)
        step(t - 2 * hops, core_far)
        step(t - 6, lambda p: by_kind(p, LONG_OUT, lambda: arrived(p)))
        step(t - 2 * hops - 1, lambda p: by_kind(p, LONG_OUT, far=lambda: arrived(p)))
        for p in range(DOWN, direct):
            pl.when(t == copied[p])(down_weight(p).start)

        for stage, (start, end) in enumerate(small):
            pl.when(turn == ahead + 1 + 2 * stage)(start)
            pl.when(turn == ahead + 2 + 2 * stage)(end)
        pl.when(turn == ahead + 7)(set_params)

        @pl.when(t == 0)
        def _():
            loads[1].wait()
            loads[2].wait()

        @pl.when(within(t, embed_steps))
        def _():
            prepare_step(t)

        @pl.when(t == embed_from)
        def _():
            for p in range(QKV):
                into_vmem(p).wait()

        @pl.when(within(t - embed_from, embed_steps))
        def _():
            embed_step(t - embed_from)

        @pl.when(within(t - project_from, 3))
        def _():
            k = t - project_from
            into_vmem(QKV + 2 * k).wait()
            into_vmem(QKV + 2 * k + 1).wait()
            project_step(k)

        @pl.when(within(t - attend_from, rows * pairs // 2))
        def _():
            attend_step(t - attend_from)

        @pl.when(t == out_from - 1)
        def _():
            out_weight().start()

        @pl.when(t == up_fetch)
        def _():
            up_weight().start()

        @pl.when(t == out_from)
        def _():
            out_weight().wait()
            for n in range(3 * rows):
                qkv_copy(n).wait()

        @pl.when(within(t - out_from, out_ticks))
        def _():
            out_step(2 * (t - out_from))
            out_step(2 * (t - out_from) + 1)

        @pl.when(t == out_from + out_ticks - 1)
        def _():
            for r in range(rows):
                mixed_copy(r).wait()

        @pl.when(t == up_from)
        def _():
            up_weight().wait()

        @pl.when(within(t - up_from, embed_steps))
        def _():
            up_step(t - up_from)

        for g in range(4):

            @pl.when(t == down_at[g])
            def _(g=g):
                if g == 0:
                    for i in range(embed_steps):
                        for copy in stream_copies(i):
                            copy.wait()
                down_step(g)

        step(t - sent_after, sent_off)
        return carry

    last = max(blocks + 6, blocks + 2 * hops, down_at[-1] + 1)
    lax.fori_loop(0, last + ahead, tick, 0)

    def finish(p, carry):
        sent_off(p)
        return carry

    lax.fori_loop(last - sent_after, blocks, finish, 0)
    for i in range(embed_steps):
        act_copy(i).wait()
    for i in range(embed_steps - 2, embed_steps):
        slope_copy(i).wait()
    for r in range(rows):
        x2_copy(r).wait()


def like(shape, dtype=low):
    return jax.ShapeDtypeStruct(shape, dtype)


def front(pc, owners, ids, masters, table, codes, phones, segments):
    per_group, piece, _ = masters.shape
    rows, length = segments.shape
    total = rows * length
    rate = jnp.asarray(rates()[1][None], jnp.float32)
    own_sections = table.shape[0]
    hops = pc.nx - 1 + pc.ny - 1
    same, other = index_waves(length)
    small = pc.small_slots()
    embed_steps = total // ROWS_AT_ONCE
    cuts = rank_cuts(per_group)
    dma = pltpu.SemaphoreType.DMA
    vmem = pl.BlockSpec(memory_space=pltpu.VMEM)
    smem = pl.BlockSpec(memory_space=pltpu.SMEM)
    far = pl.BlockSpec(memory_space=pl.ANY)
    return pl.pallas_call(
        functools.partial(front_kernel, pc),
        out_shape=(
            like((BLOCKS, pc.nz, pc.nx, piece, D)),
            like((rows, 8, D), float_out),
            like((total, CODES)),
            like((total, PHONES)),
            like((total, D), float_out),
            like((total, D)),
            like((3 * rows, pc.nz, pc.nx, piece, D)),
            like((rows, pc.nz, pc.nx, piece, D)),
            like((rows, HEADS // 2, 2, length), float_out),
            like((total, D), float_out),
            like((total, D)),
            like((4, total, D)),
            like((4, total, D)),
            like((total, D), float_out),
        ),
        in_specs=[smem, smem, far] + [vmem] * 5 + [far, far],
        out_specs=(far, vmem, far, far, far, far, far, far, vmem, far, far, far, far, far),
        scratch_shapes=[
            pltpu.VMEM((own_sections, 8, D), float_out),
            pltpu.VMEM((total, 1), jnp.int32),
            pltpu.VMEM((total, 1), jnp.int32),
            pltpu.VMEM((total, 128), jnp.int32),
            pltpu.VMEM((rows, 8, D), float_out),
            pltpu.VMEM((2, length, D), float_out),
            pltpu.VMEM((per_group, piece, D), low),
            pltpu.VMEM((per_group, piece, D), low),
            pltpu.VMEM((SECTIONS, 128), float_out),
            *(
                pltpu.VMEM((pc.groups, b - a, piece, pc.panel), low)
                for a, b in zip(cuts[:-1], cuts[1:], strict=True)
            ),
            pltpu.VMEM((BLOCKS, piece, pc.panel), low),
            pltpu.VMEM((own_sections * pc.groups, 8, D), float_out),
            pltpu.VMEM((FRONT, pc.nz, pc.nx, piece, D), low),
            pltpu.VMEM((total, CODES), low),
            pltpu.VMEM((total, PHONES), low),
            pltpu.VMEM((total, D), float_out),
            pltpu.VMEM((total, D), low),
            pltpu.VMEM((max(4 * rows, 8), pc.nz, pc.nx, piece, D), low),
            pltpu.VMEM((2, pc.nz, pc.nx, piece, D), low),
            pltpu.VMEM((total, D), low),
            pltpu.VMEM((4, total, D), low),
            pltpu.VMEM((2, 4, ROWS_AT_ONCE, D), low),
            pltpu.VMEM((2, 8, 128), float_out),
            pltpu.VMEM((small, 8, 128), float_out),
            pltpu.SMEM((BLOCKS,), jnp.int32),
            dma((3,)),
            dma((3, pc.groups - 1)),
            dma((3, pc.groups - 1)),
            dma((pc.groups - 1,)),
            dma((pc.groups - 1,)),
            dma((BLOCKS,)),
            dma((BLOCKS, pc.nz - 1)),
            dma((BLOCKS, pc.nz - 1)),
            dma((BLOCKS, hops)),
            dma((BLOCKS, hops)),
            dma((BLOCKS, hops)),
            dma((BLOCKS, hops)),
            dma((BLOCKS,)),
            dma((BLOCKS,)),
            dma((small,)),
            dma((small,)),
            dma((FRONT,)),
            dma((embed_steps, 4)),
            dma((3 * rows,)),
            dma((rows,)),
            dma,
            dma,
            dma((8,)),
            dma((embed_steps, 2)),
            dma((embed_steps, 2)),
            dma((rows,)),
        ],
        name="front",
        compiler_params=pltpu.CompilerParams(
            collective_id=0, has_side_effects=True, vmem_limit_bytes=62 * MIB
        ),
    )(owners, ids, masters.reshape(-1, D), table, codes, phones, segments, rate, same, other)


FAR = ("h3", "act", "h2", "mixed", "h1", "multi", "hot", "dlogits", "dffn", "du", "dattn")


HOME = (
    (0, 2, "h3", "dlogits"),
    (2, 8, "act", "dffn"),
    (10, 8, "h2", "du"),
    (18, 2, "mixed", "dattn"),
    (20, 6, "h1", "dqkv"),
    (26, 2, "multi", "demb"),
    (28, 1, "hot", "demb"),
)


def back_kernel(pc, *refs):
    held = dict(zip(FAR, refs[2 : 2 + len(FAR)], strict=True))
    owners_ref, ids_ref = refs[:2]
    (
        qkv_ref,
        do_ref,
        x0_ref,
        dx_ref,
        w_ref,
        lse_ref,
        segs_ref,
        params_ref,
        rows_ref,
        loss_ref,
        out_ref,
        table_out,
        sums_out,
        seg_col,
        block_of_ref,
        key_ref,
        rank_ref,
        arrived,
        sums_ref,
        x_buf,
        y_buf,
        own_half,
        send_half,
        core_in,
        first_a,
        first_b,
        then_in,
        z_in,
        far_z,
        far_yx,
        far_in,
        final,
        by_slot,
        square,
        heads,
        dqkv,
        demb,
        qkv_w,
        chunks,
        row_sums,
        table_mine,
        table_in,
        table_mid,
        sent,
        landed,
        in_sem,
        head_sem,
        chunk_sem,
        w_sem,
        free_sem,
        c_send,
        c_recv,
        e_send,
        e_recv,
        f_send,
        f_recv,
        z_send,
        z_recv,
        a_send,
        a_recv,
        t_send,
        t_recv,
        m_send,
        m_recv,
    ) = refs[2 + len(FAR) :]
    held["dqkv"], held["demb"] = dqkv, demb
    pc.here()
    blocks = BLOCKS
    per_group = out_ref.shape[0]
    own_sections = table_out.shape[0]
    rows, length = segs_ref.shape
    pairs = HEADS // 2
    steps = length // ROWS_AT_ONCE
    attend_steps, embed_steps = rows * pairs, rows * steps
    width = x_buf.shape[2]
    keep = pc.columns(pc.c, pc.half)
    away = pc.columns(1 - pc.c, pc.half)
    core_slots = core_in.shape[0]
    hops = pc.nz - 1
    release = 2 * pc.nz - 1

    def fetch(t):
        for from_, count, xs, ys in HOME:
            u = t - from_

            @pl.when(within(u, count))
            def _(xs=xs, ys=ys, u=u):
                slot = lax.rem(t, 2)
                x_ref, y_ref = held[xs], held[ys]
                columns = pc.columns(lax.rem(u, 2), width)
                x_src = x_ref.at[lax.div(u, 2), :, columns] if len(x_ref.shape) == 3 else x_ref.at[:, columns]
                y_src = y_ref.at[lax.div(u, 2)] if len(y_ref.shape) == 3 else y_ref
                pltpu.make_async_copy(x_src, x_buf.at[slot], in_sem.at[slot, 0]).start()
                pltpu.make_async_copy(y_src, y_buf.at[slot], in_sem.at[slot, 1]).start()

    def fetched(slot):
        for n, buf in enumerate((x_buf, y_buf)):
            pltpu.make_async_copy(buf.at[slot], buf.at[slot], in_sem.at[slot, n]).wait()

    def head_copies(n):
        r, h, slot = n // pairs, n % pairs, n % 2
        at, columns = pl.ds(r * length, length), pc.columns(h, 2 * HD)
        copies = [
            pltpu.make_async_copy(
                qkv_ref.at[k, at, columns], heads.at[slot, k], head_sem.at[slot, k]
            )
            for k in range(3)
        ]
        copies.append(
            pltpu.make_async_copy(do_ref.at[at, columns], heads.at[slot, 3], head_sem.at[slot, 3])
        )
        return copies

    def chunk(i):
        return pl.ds(i * ROWS_AT_ONCE, ROWS_AT_ONCE)

    def chunk_copies(i):
        slot = i % 2
        return [
            pltpu.make_async_copy(x0_ref.at[chunk(i)], chunks.at[slot, 0], chunk_sem.at[slot, 0]),
            pltpu.make_async_copy(dx_ref.at[chunk(i)], chunks.at[slot, 1], chunk_sem.at[slot, 1]),
        ]

    weight_copy = pltpu.make_async_copy(w_ref.at[pl.ds(QKV, 6)], qkv_w, w_sem)

    def attend_back_step(n):
        r, h, slot = n // pairs, n % pairs, n % 2
        at, columns = pl.ds(r * length, length), pc.columns(h, 2 * HD)
        same = seg_col[at] == segs_ref[pl.ds(r, 1)]
        stats = [lse_ref[r, h, k : k + 1] for k in range(2)]
        made = attend_pair_back(same, *(heads[slot, k] for k in range(4)), stats)
        for k in range(3):
            dqkv[k, at, columns] = made[k]

    def embed_back_step(i):
        for copy in chunk_copies(i):
            copy.wait()
        r, slot = i // steps, i % 2
        dh = 0.0
        for k in range(3):
            dh = dh + times_t(
                dqkv[k, chunk(i)], qkv_w[2 * k : 2 * k + 2].reshape(D, D)
            )
        normed, scale = normalize(chunks[slot, 0])
        dx, gain, shift = norm_back(dh, normed, scale, params_ref[r, 0:1])
        demb[chunk(i)] = (chunks[slot, 1] + dx).astype(low)
        row_sums[r, 0:2] += jnp.concatenate([gain, shift], axis=0)

    def to_core(b):
        return [
            remote(
                send_half.at[lax.rem(b, 4)],
                core_in.at[lax.rem(b, core_slots)],
                c_send.at[b],
                c_recv.at[b],
                pc.at_core(),
            )
        ]

    middle_z = pc.nz // 2
    lower, upper = slice(0, middle_z), slice(middle_z, pc.nz)
    lower_at, upper_at = pl.ds(0, middle_z), pl.ds(middle_z, pc.nz - middle_z)

    def first_x(b):
        return [
            remote(
                core_in.at[lax.rem(b, core_slots), lower_at, pc.x_of(d)],
                first_a.at[place_among(b), d - 1],
                e_send.at[b, d - 1],
                e_recv.at[b, d - 1],
                pc.at_x(d),
            )
            for d in range(1, pc.nx)
        ]

    def first_y(b):
        return [
            remote(
                core_in.at[
                    lax.rem(b, core_slots), upper_at, :, :, pc.columns(pc.y_of(d), pc.panel)
                ],
                first_b.at[place_among(b), d - 1],
                e_send.at[b, pc.nx - 1 + d - 1],
                e_recv.at[b, pc.nx - 1 + d - 1],
                pc.at_y(d),
            )
            for d in range(1, pc.ny)
        ]

    def then_y(b):
        return [
            remote(
                first_a.at[place_among(b), 0, :, :, pc.columns(pc.y_of(d), pc.panel)],
                then_in.at[place_among(b), d - 1, lower_at],
                f_send.at[b, d - 1],
                f_recv.at[b, d - 1],
                pc.at_y(d),
            )
            for d in range(1, pc.ny)
        ]

    def then_x(b):
        return [
            remote(
                first_b.at[place_among(b), 0, :, pc.x_of(d)],
                then_in.at[place_among(b), d - 1, upper_at],
                f_send.at[b, pc.ny - 1 + d - 1],
                f_recv.at[b, pc.ny - 1 + d - 1],
                pc.at_x(d),
            )
            for d in range(1, pc.nx)
        ]

    def along_z(b):
        return [
            remote(
                then_in.at[place_among(b), 0, pc.z_of(d)],
                z_in.at[place_among(b), d - 1],
                z_send.at[b, d - 1],
                z_recv.at[b, d - 1],
                pc.at_z(d),
            )
            for d in range(1, pc.nz)
        ]

    def ring(b, k):
        n = lax.div(b, LONG_EVERY)
        source = (
            core_in.at[lax.rem(b, core_slots), pc.z_of(hops)] if k == 1 else far_z.at[n, k - 2]
        )
        return [
            remote(source, far_z.at[n, k - 1], z_send.at[b, k - 1], z_recv.at[b, k - 1], pc.at_z(1))
        ]

    def far_y(b):
        n = lax.div(b, LONG_EVERY)
        return [
            remote(
                far_z.at[n, hops - 1, :, :, pc.columns(pc.y_of(d), pc.panel)],
                far_yx.at[n, d - 1],
                f_send.at[b, d - 1],
                f_recv.at[b, d - 1],
                pc.at_y(d),
            )
            for d in range(1, pc.ny)
        ]

    def far_x(b):
        n = lax.div(b, LONG_EVERY)
        return [
            remote(
                far_yx.at[n, 0, pc.x_of(d)],
                far_in.at[n, d - 1],
                e_send.at[b, d - 1],
                e_recv.at[b, d - 1],
                pc.at_x(d),
            )
            for d in range(1, pc.nx)
        ]

    def summed(own, landed_ref, index, count):
        total = own.astype(float_out)
        for d in range(count - 1):
            total = total + landed_ref[index, d].astype(float_out)
        return total

    def table_stage():
        return [
            remote(
                table_mine.at[pl.ds(pc.section_peer(d) * own_sections, own_sections)],
                table_in.at[d - 1],
                t_send.at[d - 1],
                t_recv.at[d - 1],
                (pc.section_peer(d), pc.j),
            )
            for d in range(1, pc.groups)
        ]

    def table_hop(stage):
        count, target = ((pc.nx, pc.at_x), (pc.nz, pc.at_z))[stage]
        first = pc.groups - 1 + stage * (pc.nx - 1)
        return [
            remote(
                table_mid.at[stage],
                table_in.at[first + d - 1],
                t_send.at[first + d - 1],
                t_recv.at[first + d - 1],
                target(d),
            )
            for d in range(1, count)
        ]

    def table_landed(copies, own, first):
        for copy in copies:
            copy.wait()
        total = own
        for n in range(len(copies)):
            total = total + table_in[first + n]
        return total

    def table_after_section():
        own = table_mine[pl.ds(pc.s * own_sections, own_sections)]
        table_mid[0] = table_landed(table_stage(), own, 0)
        begin(table_hop(0))

    def table_after_x():
        table_mid[1] = table_landed(table_hop(0), table_mid[0], pc.groups - 1)
        begin(table_hop(1))

    def table_after_z():
        first = pc.groups - 1 + pc.nx - 1
        table_out[...] = table_landed(table_hop(1), table_mid[1], first)

    fetch(0)
    begin(head_copies(0))
    weight_copy.start()
    pc.barrier()
    square[...] = jnp.zeros_like(square)
    final[blocks] = jnp.zeros(final.shape[1:], low)
    row_sums[...] = rows_ref[...]
    for r in range(rows):
        seg_col[pl.ds(r * length, length)] = column_of(segs_ref[r : r + 1])

    base = pc.s * per_group

    def rank_blocks():
        keys = rank_keys(owners_ref, HOMEWARD[::-1], per_group, pc.groups)[::-1]
        for b in range(blocks):
            key_ref[b] = keys[b]
        for i in range(per_group):
            rank = jnp.int32(per_group)
            for b in range(blocks):
                rank = jnp.where(owners_ref[HOMEWARD[b]] == base + i, keys[b] - base, rank)
            rank_ref[i] = rank

        def find(i, carry):
            where = jnp.int32(blocks)
            for b in range(blocks):
                where = jnp.where(key_ref[b] == i, b, where)
            block_of_ref[i] = where
            return carry

        lax.fori_loop(0, per_group * pc.groups, find, 0)

    arrived[:, per_group] = jnp.zeros((pc.groups, *arrived.shape[2:]), low)
    early = per_group // 2
    panel = pc.panel_of(pc.s)

    def exchange(m):
        ranks = pl.ds(early, per_group - early) if m == 0 else pl.ds(0, early)
        return [
            remote(
                by_slot.at[pc.section_peer(d), ranks],
                arrived.at[panel, ranks],
                a_send.at[m, d - 1],
                a_recv.at[m, d - 1],
                (pc.section_peer(d), pc.j),
            )
            for d in range(1, pc.groups)
        ]

    def send_ranks(m):
        for k in range(early, per_group) if m == 0 else range(early):
            for g in range(pc.groups):
                where = jnp.clip(block_of_ref[g * per_group + k], 0, blocks)
                by_slot[g, k] = final[where]
            arrived[panel, k] = by_slot[pc.s, k]
        begin(exchange(m))

    def step(b, body):
        pl.when(within(b, blocks))(lambda: body(b))

    def first(b):
        landed_all(to_core(b))
        at = lax.rem(b, core_slots)
        core_in[at] = (
            core_in[at].astype(float_out) + own_half[lax.rem(b, 2)].reshape(core_in.shape[1:])
        ).astype(low)
        by_kind(
            b,
            LONG_HOME,
            lambda: begin(first_x(b) + first_y(b)),
            lambda: begin(ring(b, 1)),
        )

    def then(b):
        at, n = lax.rem(b, core_slots), place_among(b)

        def near():
            landed_all(first_x(b))
            first_a[n, 0] = summed(core_in[at, lower, pc.x], first_a, n, pc.nx).astype(low)
            begin(then_y(b))
            landed_all(first_y(b))
            mine = pc.columns(pc.y, pc.panel)
            first_b[n, 0] = summed(
                core_in[at, upper, :, :, mine], first_b, n, pc.ny
            ).astype(low)
            begin(then_x(b))

        by_kind(b, LONG_HOME, near)

    def ring_on(k):
        def body(b):
            def far():
                landed_all(ring(b, k))
                n, held_for = lax.div(b, LONG_EVERY), pc.z_of((2 * pc.nz - 1 - k) % pc.nz)
                far_z[n, k - 1] = (
                    far_z[n, k - 1].astype(float_out)
                    + core_in[lax.rem(b, core_slots), held_for].astype(float_out)
                ).astype(low)
                begin(ring(b, k + 1) if k < hops else far_y(b))

            by_kind(b, LONG_HOME, far=far)

        return body

    def third(b):
        n = place_among(b)

        def near():
            landed_all(then_y(b))
            total = first_a[n, 0, :, :, pc.columns(pc.y, pc.panel)].astype(float_out)
            for d in range(pc.ny - 1):
                total = total + then_in[n, d, lower].astype(float_out)
            then_in[n, 0, lower] = total.astype(low)
            landed_all(then_x(b))
            total = first_b[n, 0, :, pc.x].astype(float_out)
            for d in range(pc.nx - 1):
                total = total + then_in[n, d, upper].astype(float_out)
            then_in[n, 0, upper] = total.astype(low)
            begin(along_z(b))

        by_kind(b, LONG_HOME, near)

    def far_third(b):
        def far():
            landed_all(far_y(b))
            n, mine = lax.div(b, LONG_EVERY), pc.columns(pc.y, pc.panel)
            far_yx[n, 0] = summed(far_z[n, hops - 1, :, :, mine], far_yx, n, pc.ny).astype(low)
            begin(far_x(b))

        by_kind(b, LONG_HOME, far=far)

    def let_go(b):
        by_kind(
            b,
            LONG_HOME,
            lambda: gone(first_x(b) + first_y(b)),
            lambda: gone(ring(b, 1)),
        )

        @pl.when(b < blocks - core_slots)
        def _():
            pl.semaphore_signal(free_sem, inc=1, device_id=pc.at_core(), device_id_type=MESH)

    def settle(b, total):
        rounded = total.astype(low)
        final[b] = rounded
        wide = rounded.astype(float_out)
        square[...] += jnp.sum(wide * wide, axis=0, keepdims=True)

    def close(b):
        n = place_among(b)

        def near():
            landed_all(along_z(b))
            settle(b, summed(then_in[n, 0, pc.z], z_in, n, pc.nz))

        by_kind(b, LONG_HOME, near)

    def far_close(b):
        def far():
            landed_all(far_x(b))
            n = lax.div(b, LONG_EVERY)
            settle(b, summed(far_yx[n, 0, pc.x], far_in, n, pc.nx))

        by_kind(b, LONG_HOME, far=far)

    def sent_off(b):
        def far():
            for k in range(2, pc.nz):
                gone(ring(b, k))
            gone(far_y(b) + far_x(b))

        by_kind(
            b,
            LONG_HOME,
            lambda: gone(then_y(b) + then_x(b) + along_z(b)),
            far,
        )

    early_at = 1 + max(
        b + (release + 4 if b % LONG_EVERY == LONG_HOME else 7) for b in range(blocks - early)
    )

    def weigh(t):
        slot = lax.rem(t, 2)
        send_half[lax.rem(t, 4)] = (
            turned_times(x_buf[slot], y_buf[slot, :, away])
            .astype(low)
            .reshape(send_half.shape[1:])
        )
        own_half[slot] = turned_times(x_buf[slot], y_buf[slot, :, keep])

    def make_ready(t):
        fetched(lax.rem(t, 2))

        @pl.when(t >= 4)
        def _():
            gone(to_core(t - 4))

    def leave(t):
        @pl.when(t >= core_slots)
        def _():
            pl.semaphore_wait(free_sem, 1)

        begin(to_core(t))

    def serve(t):
        step(t - 1, first)
        step(t - 3, then)
        for k in range(1, pc.nz):
            step(t - 2 * k - 1, ring_on(k))
        step(t - 5, third)
        step(t - release, let_go)
        step(t - release - 2, far_third)
        step(t - 7, close)
        step(t - release - 4, far_close)

    def attending(t, carry):
        fetch(t + 1)

        @pl.when(t + 1 < attend_steps)
        def _():
            begin(head_copies(t + 1))

        for copy in head_copies(t):
            copy.wait()
        make_ready(t)
        weigh(t)
        attend_back_step(t)
        leave(t)
        serve(t)
        return carry

    def later(t, carry):
        pl.when(t + 1 < blocks)(lambda: fetch(t + 1))
        i = lax.div(t - attend_steps, 2)
        odd = lax.rem(t - attend_steps, 2)

        @pl.when((t < attend_steps + 2 * embed_steps) & (odd == 0))
        def _():
            begin(chunk_copies(i))

        @pl.when(t < blocks)
        def _():
            make_ready(t)
            weigh(t)
            leave(t)

        serve(t)
        pl.when(t == blocks - 2)(rank_blocks)
        pl.when(t == early_at)(lambda: send_ranks(0))

        @pl.when((t < attend_steps + 2 * embed_steps) & (odd == 1))
        def _():
            @pl.when(t == attend_steps + 1)
            def _():
                weight_copy.wait()

            embed_back_step(i)

        table_at = attend_steps + 2 * embed_steps

        @pl.when(t == table_at)
        def _():
            for section in range(own_sections * pc.groups):
                total = jnp.zeros(row_sums.shape[1:], float_out)
                for r in range(rows):
                    total = total + jnp.where(ids_ref[0, r] == section, row_sums[r], 0.0)
                table_mine[section] = total
            begin(table_stage())

        pl.when(t == table_at + 4)(table_after_section)
        pl.when(t == table_at + 8)(table_after_x)
        for k in range(2):
            b = 2 * (t - table_at) + k
            pl.when((t >= table_at) & (b < sent_in_loop))(functools.partial(sent_off, b))

        return carry

    last_long = LONG_HOME + (LONGS - 1) * LONG_EVERY
    last_tick = attend_steps + 2 * embed_steps + 8
    ticks = max(
        last_tick + 1, blocks + 7, blocks + release, last_long + release + 5, early_at + 1
    )
    sent_in_loop = min(blocks - 7, 2 * (ticks - attend_steps - 2 * embed_steps))
    lax.fori_loop(0, attend_steps, attending, 0)
    lax.fori_loop(attend_steps, ticks, later, 0)

    send_ranks(1)

    table_after_z()
    total = table_out[...]
    table_square = jnp.sum(total * total) / pc.batch
    lane = lax.broadcasted_iota(jnp.int32, (8, 128), 1)
    part = jnp.where(lane == 0, jnp.sum(square[...]) + table_square, loss_ref[...])
    sums_ref[...] = part
    for start, end in pc.small_stages(sums_ref, sent, landed, m_send, m_recv):
        start()
        end()
    sums_out[...] = sums_ref[...]
    for copy in exchange(0) + exchange(1):
        copy.wait()
    for i in range(per_group):
        for q in range(pc.groups):
            rank = jnp.clip(rank_ref[i], 0, per_group)
            out_ref[i, :, q * pc.panel : (q + 1) * pc.panel] = arrived[q, rank]

    for b in range(blocks - 4, blocks):
        gone(to_core(b))

    def finish(b, carry):
        sent_off(b)
        return carry

    lax.fori_loop(sent_in_loop, blocks, finish, 0)


def back(pc, owners, ids, arrays, near, per_group):
    total = arrays[0].shape[0]
    rows, length = near[6].shape
    width = D // 2
    piece = width // pc.batch
    own_sections = SECTIONS // pc.groups
    hops = pc.nx - 1 + pc.ny - 1
    blocks = BLOCKS
    steps, small = pc.table_slots(), pc.small_slots()
    dma = pltpu.SemaphoreType.DMA
    vmem = pl.BlockSpec(memory_space=pltpu.VMEM)
    smem = pl.BlockSpec(memory_space=pltpu.SMEM)
    far = pl.BlockSpec(memory_space=pl.ANY)
    nz, nx, ny, half, panel = pc.nz, pc.nx, pc.ny, pc.half, pc.panel
    return pl.pallas_call(
        functools.partial(back_kernel, pc),
        out_shape=(
            like((per_group, piece, D)),
            like((own_sections, 8, D), float_out),
            like((8, 128), float_out),
        ),
        in_specs=[smem, smem] + [far] * len(arrays) + [far] * 5 + [vmem] * 5,
        out_specs=(vmem, vmem, vmem),
        scratch_shapes=[
            pltpu.VMEM((total, 1), jnp.int32),
            pltpu.SMEM((per_group * pc.groups,), jnp.int32),
            pltpu.SMEM((BLOCKS,), jnp.int32),
            pltpu.SMEM((per_group,), jnp.int32),
            pltpu.VMEM((pc.groups, per_group + 1, piece, panel), low),
            pltpu.VMEM((8, 128), float_out),
            pltpu.VMEM((2, total, width), low),
            pltpu.VMEM((2, total, D), low),
            pltpu.VMEM((2, width, half), float_out),
            pltpu.VMEM((4, nz, nx, piece, half), low),
            pltpu.VMEM((2 * nz + 4, nz, nx, piece, half), low),
            pltpu.VMEM((NEARS, nx - 1, nz // 2, piece, half), low),
            pltpu.VMEM((NEARS, ny - 1, nz - nz // 2, nx, piece, panel), low),
            pltpu.VMEM((NEARS, max(nx, ny) - 1, nz, piece, panel), low),
            pltpu.VMEM((NEARS, nz - 1, piece, panel), low),
            pltpu.VMEM((LONGS, nz - 1, nx, piece, half), low),
            pltpu.VMEM((LONGS, ny - 1, nx, piece, panel), low),
            pltpu.VMEM((LONGS, nx - 1, piece, panel), low),
            pltpu.VMEM((blocks + 1, piece, panel), low),
            pltpu.VMEM((pc.groups, per_group, piece, panel), low),
            pltpu.VMEM((1, panel), float_out),
            pltpu.VMEM((2, 4, length, 2 * HD), low),
            pltpu.VMEM((3, total, D), low),
            pltpu.VMEM((total, D), low),
            pltpu.VMEM((6, nz, nx, piece, D), low),
            pltpu.VMEM((2, 2, ROWS_AT_ONCE, D), float_out),
            pltpu.VMEM((rows, 8, D), float_out),
            pltpu.VMEM((own_sections * pc.groups, 8, D), float_out),
            pltpu.VMEM((steps, own_sections, 8, D), float_out),
            pltpu.VMEM((2, own_sections, 8, D), float_out),
            pltpu.VMEM((2, 8, 128), float_out),
            pltpu.VMEM((small, 8, 128), float_out),
            dma((2, 2)),
            dma((2, 4)),
            dma((2, 2)),
            dma,
            pltpu.SemaphoreType.REGULAR,
            dma((blocks,)),
            dma((blocks,)),
            dma((blocks, hops)),
            dma((blocks, hops)),
            dma((blocks, hops)),
            dma((blocks, hops)),
            dma((blocks, nz - 1)),
            dma((blocks, nz - 1)),
            dma((2, pc.groups - 1)),
            dma((2, pc.groups - 1)),
            dma((steps,)),
            dma((steps,)),
            dma((small,)),
            dma((small,)),
        ],
        name="back",
        compiler_params=pltpu.CompilerParams(
            collective_id=1, has_side_effects=True, vmem_limit_bytes=62 * MIB
        ),
    )(owners, ids, *arrays, *near)


def matrix(ref, first, count=2):
    return ref[first : first + count].reshape(count * ref.shape[1], ref.shape[2])


def row_block(width, count=ROWS_AT_ONCE):
    return pl.BlockSpec((count, width), lambda i: (i, 0))


def plane_block(planes, width=D, count=ROWS_AT_ONCE):
    return pl.BlockSpec((planes, count, width), lambda i: (0, i, 0))


def per_row(steps, height=8):
    return pl.BlockSpec((1, height, D), lambda i: (i // steps, 0, 0))


def compiler(mib):
    return pltpu.CompilerParams(vmem_limit_bytes=mib * MIB)


def cost(flops, reach, deep=0):
    return pl.CostEstimate(flops=flops, bytes_accessed=reach, transcendentals=deep)


def middle_kernel(
    steps,
    slope_ref,
    x1_ref,
    x2_ref,
    params_ref,
    targets_ref,
    w_ref,
    h3_ref,
    dlogits_ref,
    dffn_ref,
    du_ref,
    dattn_ref,
    do_ref,
    dx_ref,
    rows_ref,
    loss_ref,
    out_w,
    up_w,
    down_w,
    head_w,
    sems,
):
    step = pl.program_id(0)
    parts = [(HEAD, head_w, 0)]
    for g in range(4):
        parts += [(DOWN + 2 * g, down_w, 2 * g), (UP + 2 * g, up_w, 2 * g)]
    parts.append((OUT, out_w, 0))
    loads = [
        pltpu.make_async_copy(w_ref.at[pl.ds(first, 2)], dst.at[pl.ds(at, 2)], sems.at[n])
        for n, (first, dst, at) in enumerate(parts)
    ]

    def ready(*numbers):
        @pl.when(step == 0)
        def _():
            for n in numbers:
                loads[n].wait()

    pl.when(step == 0)(lambda: begin(loads))
    par = [params_ref[0, k : k + 1] for k in range(7)]
    n3, scale3 = normalize(x2_ref[...])
    h3 = (n3 * (1.0 + par[4]) + par[5]).astype(low)
    h3_ref[...] = h3
    ready(0)
    logits = times(h3, matrix(head_w, 0))
    top = jnp.max(logits, axis=-1, keepdims=True)
    lse = top + jnp.log(jnp.sum(jnp.exp(logits - top), axis=-1, keepdims=True))
    vocab = lax.broadcasted_iota(jnp.int32, logits.shape, 1)
    wanted = targets_ref[
        pl.ds(step // steps, 1),
        pl.ds(pl.multiple_of(step % steps * ROWS_AT_ONCE, ROWS_AT_ONCE), ROWS_AT_ONCE),
    ]
    picked = column_of(wanted) == vocab
    losses = lse - jnp.sum(jnp.where(picked, logits, 0.0), axis=-1, keepdims=True)
    weight = par[6]
    dlogits = ((jnp.exp(logits - lse) - jnp.where(picked, 1.0, 0.0)) * weight).astype(low)
    dlogits_ref[...] = dlogits
    dh3 = times_t(dlogits, matrix(head_w, 0))
    dx2, gain3, shift3 = norm_back(dh3, n3, scale3, par[4])
    dffn = dx2.astype(low)
    dffn_ref[...] = dffn
    dh2 = 0.0
    for g in range(4):
        ready(1 + 2 * g, 2 + 2 * g)
        du = (times_t(dffn, matrix(down_w, 2 * g)) * slope_ref[g].astype(float_out)).astype(low)
        du_ref[g] = du
        dh2 = dh2 + times_t(du, matrix(up_w, 2 * g))
    n2, scale2 = normalize(x1_ref[...])
    dx1, gain2, shift2 = norm_back(dh2, n2, scale2, par[2])
    dx1 = dx1 + dx2
    dx_ref[...] = dx1
    dattn = dx1.astype(low)
    dattn_ref[...] = dattn
    ready(9)
    do_ref[...] = times_t(dattn, matrix(out_w, 0)).astype(low)
    grads = jnp.concatenate([gain2, shift2, gain3, shift3], axis=0)

    @pl.when(step == 0)
    def _():
        loss_ref[...] = jnp.zeros_like(loss_ref)

    @pl.when(step % steps == 0)
    def _():
        rows_ref[...] = jnp.zeros_like(rows_ref)

    rows_ref[0, 2:6] += grads
    loss_ref[...] += jnp.sum(losses) * weight[:, :128]


def middle(w, slope, x1, x2, params, targets, length):
    total = x1.shape[0]
    steps = length // ROWS_AT_ONCE
    rows = total // length
    return pl.pallas_call(
        functools.partial(middle_kernel, steps),
        grid=(total // ROWS_AT_ONCE,),
        out_shape=(
            like((total, D)),
            like((total, CODES)),
            like((total, D)),
            like((4, total, D)),
            like((total, D)),
            like((total, D)),
            like((total, D), float_out),
            like((rows, 8, D), float_out),
            like((8, 128), float_out),
        ),
        in_specs=[
            plane_block(4),
            row_block(D),
            row_block(D),
            per_row(steps),
            pl.BlockSpec(targets.shape, lambda i: (0, 0)),
            pl.BlockSpec(memory_space=pl.ANY),
        ],
        out_specs=(
            row_block(D),
            row_block(CODES),
            row_block(D),
            plane_block(4),
            row_block(D),
            row_block(D),
            row_block(D),
            per_row(steps),
            pl.BlockSpec((8, 128), lambda i: (0, 0)),
        ),
        scratch_shapes=[
            *(pltpu.VMEM((count, D // 2, D), low) for count in (2, 8, 8, 2)),
            pltpu.SemaphoreType.DMA((10,)),
        ],
        name="middle",
        compiler_params=compiler(62),
        cost_estimate=cost(22 * total * D * D, 60 * MIB, 2 * total * D),
    )(slope, x1, x2, params, targets, w)


def adam(weight, first, second, grad, rate, fixes):
    new_first = beta_one * first + (1.0 - beta_one) * grad
    new_second = beta_two * second + (1.0 - beta_two) * grad * grad
    update = new_first * fixes[0] / (jnp.sqrt(new_second * fixes[1]) + adam_eps)
    return (weight - rate * (update + decay_rate * weight), new_first, new_second)


SLOTS_AT_ONCE = 2


def update_kernel(
    step_ref,
    sums_ref,
    table_grad_ref,
    table_ref,
    table_first_ref,
    table_second_ref,
    grad_ref,
    masters_ref,
    first_ref,
    second_ref,
    new_masters,
    new_first,
    new_second,
    new_table,
    new_table_first,
    new_table_second,
    norm_ref,
    loss_ref,
    grad,
    state,
    made,
    in_sem,
    out_sem,
):
    turns = masters_ref.shape[0] // SLOTS_AT_ONCE

    def part(i):
        return pl.ds(i * SLOTS_AT_ONCE, SLOTS_AT_ONCE)

    def loads(i):
        copies = [pltpu.make_async_copy(grad_ref.at[part(i)], grad.at[part(i)], in_sem.at[i, 3])]
        for n, ref in enumerate((masters_ref, first_ref, second_ref)):
            copies.append(
                pltpu.make_async_copy(ref.at[part(i)], state.at[n, part(i)], in_sem.at[i, n])
            )
        return copies

    def stores(i):
        return [
            pltpu.make_async_copy(made.at[n, part(i)], ref.at[part(i)], out_sem.at[i, n])
            for n, ref in enumerate((new_masters, new_first, new_second))
        ]

    for i in range(turns):
        begin(loads(i))
    step = jnp.full((1, 128), step_ref[0]).astype(float_out)
    fixes = [
        1.0 / (1.0 - jnp.exp(step * math.log(beta)))[:, :1] for beta in (beta_one, beta_two)
    ]
    norm = jnp.sqrt(sums_ref[0:1, 0:1])
    clip = jnp.minimum(1.0, clip_limit / norm)
    norm_ref[...] = norm
    loss_ref[...] = sums_ref[0:1, 1:2]
    for n in range(table_ref.shape[0]):
        for k in range(6):
            at = (slice(n, n + 1), slice(k * D, (k + 1) * D))
            new_table[at], new_table_first[at], new_table_second[at] = adam(
                table_ref[at],
                table_first_ref[at],
                table_second_ref[at],
                table_grad_ref[n, k : k + 1] * clip,
                table_rate,
                fixes,
            )

    def one(i, carry):
        for copy in loads(i):
            copy.wait()
        results = adam(
            state[0, part(i)],
            state[1, part(i)],
            state[2, part(i)],
            grad[part(i)].astype(float_out) * clip,
            learn_rate,
            fixes,
        )
        for n, value in enumerate(results):
            made[n, part(i)] = value
        begin(stores(i))
        return carry

    lax.fori_loop(0, turns, one, 0)
    for i in range(turns):
        for copy in stores(i):
            copy.wait()


def update(step, sums, grad, masters, first, second, table_grad, table, table_first, table_second):
    turns = masters.shape[0] // SLOTS_AT_ONCE
    vmem = pl.BlockSpec(memory_space=pltpu.VMEM)
    far = pl.BlockSpec(memory_space=pl.ANY)
    dma = pltpu.SemaphoreType.DMA
    return pl.pallas_call(
        update_kernel,
        out_shape=(
            *(like(masters.shape, float_out) for _ in range(3)),
            *(like(table.shape, float_out) for _ in range(3)),
            like((1, 1), float_out),
            like((1, 1), float_out),
        ),
        in_specs=[pl.BlockSpec(memory_space=pltpu.SMEM)] + [vmem] * 5 + [far] * 4,
        out_specs=(far, far, far, vmem, vmem, vmem, vmem, vmem),
        scratch_shapes=[
            pltpu.VMEM(grad.shape, low),
            pltpu.VMEM((3, *masters.shape), float_out),
            pltpu.VMEM((3, *masters.shape), float_out),
            dma((turns, 4)),
            dma((turns, 3)),
        ],
        name="update",
        compiler_params=compiler(62),
        cost_estimate=cost(20 * masters.size, 28 * masters.size),
    )(step, sums, table_grad, table, table_first, table_second, grad, masters, first, second)


def per_device(
    pc,
    masters,
    first_moment,
    second_moment,
    section_table,
    table_first,
    table_second,
    owners,
    step_count,
    phones,
    codes,
    segments,
    sections,
    targets,
):
    row_count, length = segments.shape
    ids = sections.reshape(1, row_count)
    blocks, params, multi, phone_hot, x0, h1, qkv, mixed, lse, x1, h2, act, slope, x2 = front(
        pc, owners, ids, masters, section_table, codes.swapaxes(1, 2), phones, segments
    )
    w = blocks.reshape(BLOCKS, D // 2, D)
    qkv = qkv.reshape(3, row_count * length, D)
    mixed = mixed.reshape(row_count * length, D)
    h3, dlogits, dffn, du, dattn, do, dx1, row_sums, loss_part = middle(
        w, slope, x1, x2, params, targets, length
    )
    own_grad, table_grad, sums = back(
        pc,
        owners,
        ids,
        (h3, act, h2, mixed, h1, multi, phone_hot, dlogits, dffn, du, dattn),
        (qkv, do, x0, dx1, blocks, lse, segments, params, row_sums, loss_part),
        masters.shape[0],
    )
    *state, grad_norm, loss = update(
        step_count,
        sums,
        own_grad,
        masters,
        first_moment,
        second_moment,
        table_grad,
        section_table,
        table_first,
        table_second,
    )
    return (*state, grad_norm.reshape(()), loss.reshape(()))


def solution(mesh):
    return jax.shard_map(
        functools.partial(per_device, Place(mesh)),
        mesh=mesh,
        in_specs=(
            P("section", "batch", None),
            P("section", "batch", None),
            P("section", "batch", None),
            P("section", None),
            P("section", None),
            P("section", None),
            P(),
            P(),
            P(("section", "batch"), None),
            P(("section", "batch"), None, None),
            P(("section", "batch"), None),
            P(("section", "batch"), None),
            P(("section", "batch"), None),
        ),
        out_specs=(
            P("section", "batch", None),
            P("section", "batch", None),
            P("section", "batch", None),
            P("section", None),
            P("section", None),
            P("section", None),
            P(),
            P(),
        ),
        check_vma=False,
    )
```

```python
import functools
import math

import jax
import jax.numpy as jnp
import numpy as np
from jax import lax
from jax.experimental import pallas as pl
from jax.experimental.pallas import tpu as pltpu
from jax.sharding import PartitionSpec as P

D = 1024
HEADS = 16
HD = 64
CODES = 1024
LEVELS = 8
PHONES = 512
SECTIONS = 8
CORES = 2

clip_limit = 0.002
learn_rate = 0.02
table_rate = 0.1
beta_one = 0.9
beta_two = 0.95
adam_eps = 1e-08
decay_rate = 0.1
norm_eps = 1e-05
pos_scale = 0.1
float_out = jnp.float32
low = jnp.bfloat16
MESH = pl.DeviceIdType.MESH
MIB = 1 << 20


class Place:
    def __init__(self, mesh):
        self.groups = mesh.shape["section"]
        self.batch = mesh.shape["batch"]
        self.ny = self.groups // CORES
        self.nx = 1 << (int(math.log2(self.batch)) // 2)
        self.nz = self.batch // self.nx
        self.panel = D // self.groups
        self.half = D // CORES

    def here(self):
        self.s = lax.axis_index("section")
        self.j = lax.axis_index("batch")
        self.y = lax.div(self.s, CORES)
        self.c = lax.rem(self.s, CORES)
        self.z = lax.div(self.j, self.nx)
        self.x = lax.rem(self.j, self.nx)
        self.sections = [lax.rem(self.s + d, self.groups) for d in range(self.groups)]
        self.xs = [lax.rem(self.x + d, self.nx) for d in range(self.nx)]
        self.ys = [lax.rem(self.y + d, self.ny) for d in range(self.ny)]
        self.zs = [lax.rem(self.z + d, self.nz) for d in range(self.nz)]
        self.x_peers = [(self.s, self.z * self.nx + x) for x in self.xs]
        self.y_peers = [(y * CORES + self.c, self.j) for y in self.ys]
        self.z_peers = [(self.s, z * self.nx + self.x) for z in self.zs]
        self.core_peer = (self.y * CORES + (1 - self.c), self.j)

    def panel_of(self, s):
        return lax.rem(s, CORES) * self.ny + lax.div(s, CORES)

    def section_peer(self, d):
        return self.sections[d]

    def x_of(self, d):
        return self.xs[d]

    def y_of(self, d):
        return self.ys[d]

    def z_of(self, d):
        return self.zs[d]

    def at_x(self, d):
        return self.x_peers[d]

    def at_y(self, d):
        return self.y_peers[d]

    def at_z(self, d):
        return self.z_peers[d]

    def at_core(self):
        return self.core_peer

    def columns(self, index, width):
        return pl.ds(pl.multiple_of(index * width, width), width)

    def near_peers(self):
        return [
            (self.sections[d], self.z * self.nx + self.xs[e])
            for d in range(self.groups)
            for e in range(self.nx)
            if d or e
        ]

    def barrier(self):
        sem = pltpu.get_barrier_semaphore()
        peers = self.near_peers() + [self.at_z(d) for d in range(1, self.nz)]
        for peer in peers:
            pl.semaphore_signal(sem, inc=1, device_id=peer, device_id_type=MESH)
        pl.semaphore_wait(sem, len(peers))

    def small_slots(self):
        return (self.groups * self.nx - 1) + (self.nz - 1)

    def table_slots(self):
        return (self.groups - 1) + (self.nx - 1) + (self.nz - 1)

    def small_stages(self, held, sent, landed, send_sem, recv_sem):
        near = self.near_peers()
        far = [self.at_z(d) for d in range(1, self.nz)]

        def stage(number, peers, first):
            copies = [
                remote(
                    sent.at[number],
                    landed.at[first + n],
                    send_sem.at[first + n],
                    recv_sem.at[first + n],
                    peer,
                )
                for n, peer in enumerate(peers)
            ]

            def start():
                sent[number] = held[...]
                for copy in copies:
                    copy.start()

            def end():
                for copy in copies:
                    copy.wait()
                total = held[...]
                for n in range(len(peers)):
                    total = total + landed[first + n]
                held[...] = total

            return start, end

        return [stage(0, near, 0), stage(1, far, len(near))]


def remote(src, dst, send_sem, recv_sem, device):
    return pltpu.make_async_remote_copy(
        src_ref=src,
        dst_ref=dst,
        send_sem=send_sem,
        recv_sem=recv_sem,
        device_id=device,
        device_id_type=MESH,
    )


ROWS_AT_ONCE = 256
BLOCKS = 29
CODE, PHONE, QKV, OUT, UP, DOWN, HEAD = 0, 2, 3, 9, 11, 19, 27
FRONT = 9
OUTWARD = (0, 1, 2, 5, 6, 7, 8, 9, 10, 11, 12, *range(13, 29), 3, 4)
HOMEWARD = (3, 4, *range(21, 29), *range(13, 21), 11, 12, 5, 6, 7, 8, 9, 10, 0, 1, 2)


def begin(copies):
    for copy in copies:
        copy.start()


def landed_all(copies):
    for copy in copies:
        copy.wait_recv()


def gone(copies):
    for copy in copies:
        copy.wait_send()


LONG_EVERY = 7
LONG_OUT, LONG_HOME = 3, 1
LONGS = len(range(LONG_HOME, BLOCKS, LONG_EVERY))
NEARS = BLOCKS - LONGS


def place_among(b):
    return b - lax.div(b + (LONG_EVERY - 1 - LONG_HOME), LONG_EVERY)


def by_kind(b, at, near=None, far=None):
    long = lax.rem(b, LONG_EVERY) == at
    if near is not None:
        pl.when(jnp.logical_not(long))(near)
    if far is not None:
        pl.when(long)(far)


def rank_cuts(per_group):
    return sorted({0, min(2, per_group), min(4, per_group), per_group})


def rank_keys(owners_ref, order, per_group, groups):
    seen = [jnp.int32(0)] * groups
    keys = []
    for b in order:
        section = jnp.clip(lax.div(owners_ref[b], per_group), 0, groups - 1)
        rank = jnp.int32(0)
        for g in range(groups):
            rank = jnp.where(section == g, seen[g], rank)
            seen[g] = seen[g] + jnp.where(section == g, 1, 0)
        keys.append(section * per_group + jnp.minimum(rank, per_group - 1))
    return keys


def within(value, count):
    return (value >= 0) & (value < count)


def times(a, b):
    return lax.dot_general(a, b, (((1,), (0,)), ((), ())), preferred_element_type=float_out)


def times_t(a, b):
    return lax.dot_general(a, b, (((1,), (1,)), ((), ())), preferred_element_type=float_out)


def turned_times(a, b):
    return lax.dot_general(a, b, (((0,), (0,)), ((), ())), preferred_element_type=float_out)


def normalize(stream):
    centred = stream - jnp.mean(stream, axis=-1, keepdims=True)
    scale = lax.rsqrt(jnp.mean(centred * centred, axis=-1, keepdims=True) + norm_eps)
    return (centred * scale, scale)


def norm_back(grad, normed, scale, gain):
    inner = grad * (1.0 + gain)
    result = scale * (
        inner
        - jnp.mean(inner, axis=-1, keepdims=True)
        - normed * jnp.mean(inner * normed, axis=-1, keepdims=True)
    )
    return (
        result,
        jnp.sum(grad * normed, axis=0, keepdims=True),
        jnp.sum(grad, axis=0, keepdims=True),
    )


def rates():
    column = np.arange(D)
    return column, np.exp(-(2 * (column // 2)) * (math.log(10000.0) / D))


def index_waves(length):
    column, rate = rates()
    angle = np.arange(length)[:, None] * rate
    sine, cosine = np.sin(angle), np.cos(angle)
    even = column % 2 == 0
    same = pos_scale * np.where(even, sine, cosine)
    other = pos_scale * np.where(even, cosine, sine)
    return jnp.asarray(same, jnp.float32), jnp.asarray(other, jnp.float32)


def column_of(row):
    wide = jnp.broadcast_to(row.astype(float_out), (128, row.shape[1]))
    return wide.T[:, :1].astype(jnp.int32)


def masks():
    lane = lax.broadcasted_iota(jnp.int32, (1, 2 * HD), 1)
    return [(lane // HD == h).astype(low) for h in range(2)]


def in_turn(items, first, middle, last):
    ahead, behind = first(*items[0]), None
    for n, item in enumerate(items):
        now = ahead
        if n + 1 < len(items):
            ahead = first(*items[n + 1])
        made = middle(*item, *now)
        if behind is not None:
            last(*behind)
        behind = (*item, *made)
    last(*behind)


def attend_pairs(same, heads):
    turned = [v.astype(float_out).T.astype(low) for _, _, v in heads]
    outs = [[] for _ in heads]
    stats = [[] for _ in heads]
    scaled = [mask * HD ** (-0.5) for mask in masks()]

    def first(n, h):
        q, k, _ = heads[n]
        return (times_t(k, q * scaled[h]),)

    def middle(n, h, scores):
        scores = jnp.where(same, scores, -1000000000.0)
        top = jnp.max(scores, axis=0, keepdims=True)
        powers = jnp.exp(scores - top)
        total = jnp.sum(powers, axis=0, keepdims=True)
        stats[n].append(top + jnp.log(total))
        return ((powers * (1.0 / total)).astype(low),)

    def last(n, h, probs):
        outs[n].append(times(turned[n][h * HD : (h + 1) * HD], probs))

    in_turn([(n, h) for n in range(len(heads)) for h in range(2)], first, middle, last)
    return [jnp.concatenate(out, axis=0).T.astype(low) for out in outs], stats


def attend_pair_back(same, q, k, v, do, stats):
    k_turned = (k.astype(float_out) * HD ** (-0.5)).T.astype(low)
    width = q.shape[0] // 2
    q_of = [q * (mask * HD ** (-0.5)) for mask in masks()]
    do_of = [do * mask for mask in masks()]
    dq = [[], []]
    sums = [0.0, 0.0]

    def part(c):
        return slice(c * width, (c + 1) * width)

    def first(c, h):
        return times_t(k, q_of[h][part(c)]), times_t(v, do_of[h][part(c)])

    def middle(c, h, scores, grad):
        scores = jnp.where(same[:, part(c)], scores, -1000000000.0)
        probs = jnp.exp(scores - stats[h][:, part(c)])
        level = jnp.sum(probs * grad, axis=0, keepdims=True)
        return probs.astype(low), (probs * (grad - level)).astype(low)

    def last(c, h, probs, back):
        sums[0] = sums[0] + times(back, q_of[h][part(c)])
        sums[1] = sums[1] + times(probs, do_of[h][part(c)])
        dq[h].append(times(k_turned[h * HD : (h + 1) * HD], back))

    in_turn([(c, h) for c in range(2) for h in range(2)], first, middle, last)
    turned = jnp.concatenate([jnp.concatenate(parts, axis=1) for parts in dq], axis=0)
    return turned.T.astype(low), sums[0].astype(low), sums[1].astype(low)


def front_kernel(
    pc,
    owners_ref,
    ids_ref,
    masters_ref,
    raw_table,
    codes_ref,
    phones_ref,
    segs_ref,
    rate_ref,
    same_ref,
    other_ref,
    w_ref,
    params_ref,
    multi_out,
    hot_out,
    x_out,
    h_out,
    qkv_out,
    mixed_out,
    lse_ref,
    x1_out,
    h2_out,
    act_out,
    slope_out,
    x2_out,
    table_ref,
    seg_col,
    phone_col,
    code_cols,
    starts_ref,
    waves,
    rounded,
    ordered,
    counts_ref,
    *rest,
):
    parts = len(rank_cuts(ordered.shape[0])) - 1
    slots = rest[:parts]
    (
        pieces,
        table_all,
        wf,
        multi,
        hot,
        x0,
        h1,
        pool,
        wo,
        h2,
        act,
        slope,
        sent,
        landed,
        key_ref,
        in_sem,
        a_send,
        a_recv,
        t_send,
        t_recv,
        own_sem,
        z_send,
        z_recv,
        e_send,
        e_recv,
        f_send,
        f_recv,
        c_send,
        c_recv,
        m_send,
        m_recv,
        w_sem,
        out_sem,
        qkv_sem,
        mix_sem,
        o_sem,
        u_sem,
        d_sem,
        x1_sem,
        act_sem,
        x2_sem,
    ) = rest[parts:]
    pc.here()
    blocks = BLOCKS
    per_group, piece = rounded.shape[:2]
    own_sections = table_ref.shape[0]
    rows, length = segs_ref.shape
    steps = length // ROWS_AT_ONCE
    pairs = HEADS // 2
    mine = pc.columns(pc.panel_of(pc.s), pc.panel)
    core_half = pc.columns(pc.c, pc.half)
    loads = [
        pltpu.make_async_copy(
            masters_ref, x0.at[pl.ds(0, per_group * piece)], in_sem.at[0]
        ),
        pltpu.make_async_copy(same_ref, waves.at[0], in_sem.at[1]),
        pltpu.make_async_copy(other_ref, waves.at[1], in_sem.at[2]),
    ]
    begin(loads)
    keys = rank_keys(owners_ref, OUTWARD, per_group, pc.groups)
    for p in range(blocks):
        key_ref[p] = keys[p]
    base = pc.s * per_group
    slot_of = []
    for k in range(per_group):
        slot = jnp.int32(0)
        for p in range(blocks):
            slot = jnp.where(keys[p] == base + k, owners_ref[OUTWARD[p]] - base, slot)
        slot_of.append(slot)
    table_ref[...] = jnp.zeros_like(table_ref)
    for k in range(6):
        for n in range(own_sections):
            table_ref[n, k : k + 1] = raw_table[n : n + 1, k * D : (k + 1) * D]
    pc.barrier()
    loads[0].wait()
    rounded[...] = x0[: per_group * piece].astype(low).reshape(rounded.shape)
    for k in range(per_group):
        ordered[k] = rounded[jnp.clip(slot_of[k], 0, per_group - 1)]
    cuts = rank_cuts(per_group)
    for m, place in enumerate(slots):
        for k in range(cuts[m], cuts[m + 1]):
            place[pc.s, k - cuts[m]] = ordered[k, :, mine]

    def exchange(m):
        first, count = cuts[m], cuts[m + 1] - cuts[m]
        return [
            remote(
                ordered.at[
                    pl.ds(first, count),
                    :,
                    pc.columns(pc.panel_of(pc.section_peer(d)), pc.panel),
                ],
                slots[m].at[pc.s],
                a_send.at[m, d - 1],
                a_recv.at[m, d - 1],
                (pc.section_peer(d), pc.j),
            )
            for d in range(1, pc.groups)
        ]

    def table_exchange():
        return [
            remote(
                table_ref,
                table_all.at[pl.ds(pc.s * own_sections, own_sections)],
                t_send.at[d - 1],
                t_recv.at[d - 1],
                (pc.section_peer(d), pc.j),
            )
            for d in range(1, pc.groups)
        ]

    for m in range(len(cuts) - 1):
        begin(exchange(m))
    begin(table_exchange())
    table_all[pl.ds(pc.s * own_sections, own_sections)] = table_ref[...]
    section = lax.broadcasted_iota(jnp.int32, (SECTIONS, 128), 0)
    counts = jnp.zeros((SECTIONS, 128), jnp.float32)
    for r in range(rows):
        counts = counts + jnp.where(section == ids_ref[0, r], float(length), 0.0)
    counts_ref[...] = counts
    small = pc.small_stages(counts_ref, sent, landed, m_send, m_recv)

    def take_pieces(m):
        for copy in exchange(m):
            copy.wait()
        until = cuts[m + 1] if m + 2 < len(cuts) else blocks
        for p in range(cuts[m], until):
            key = jnp.clip(key_ref[p], 0, per_group * pc.groups - 1)
            section, rank = lax.div(key, per_group), lax.rem(key, per_group)
            found = slots[0][section, jnp.minimum(rank, cuts[1] - 1)]
            for n in range(1, m + 1):
                last = cuts[n + 1] - cuts[n] - 1
                here = slots[n][section, jnp.clip(rank - cuts[n], 0, last)]
                found = jnp.where(rank >= cuts[n], here, found)
            pieces[p] = found

    def set_params():
        for copy in table_exchange():
            copy.wait()
        line = lax.broadcasted_iota(jnp.int32, (8, D), 0)
        for r in range(rows):
            held = jnp.sum(
                jnp.where(section == ids_ref[0, r], counts_ref[...], 0.0), axis=0, keepdims=True
            )
            weight = 1.0 / (SECTIONS * jnp.concatenate([held] * (D // 128), axis=1))
            params_ref[r] = jnp.where(line == 6, weight, table_all[ids_ref[0, r]])

    def own(p):
        return pltpu.make_async_copy(
            pieces.at[p], w_ref.at[p, pc.z, pc.x, :, mine], own_sem.at[p]
        )

    def along_z(p):
        return [
            remote(
                pieces.at[p],
                w_ref.at[p, pc.z, pc.x, :, mine],
                z_send.at[p, d - 1],
                z_recv.at[p, d - 1],
                pc.at_z(d),
            )
            for d in range(1, pc.nz)
        ]

    def spread(p, part, send_sem, recv_sem, count, target, source=None, first=0):
        source = part if source is None else source
        return [
            remote(
                source,
                part,
                send_sem.at[p, first + d - 1],
                recv_sem.at[p, first + d - 1],
                target(d),
            )
            for d in range(1, count)
        ]

    middle_z = pc.nz // 2
    lower, upper = pl.ds(0, middle_z), pl.ds(middle_z, pc.nz - middle_z)

    def first_x(p):
        part = w_ref.at[p, lower, pc.x, :, mine]
        return spread(p, part, e_send, e_recv, pc.nx, pc.at_x)

    def first_y(p):
        part = w_ref.at[p, upper, pc.x, :, mine]
        return spread(p, part, e_send, e_recv, pc.ny, pc.at_y, first=pc.nx - 1)

    def then_y(p):
        part = w_ref.at[p, lower, :, :, mine]
        return spread(p, part, f_send, f_recv, pc.ny, pc.at_y)

    def then_x(p):
        part = w_ref.at[p, upper, pc.x, :, core_half]
        return spread(p, part, f_send, f_recv, pc.nx, pc.at_x, first=pc.ny - 1)

    def far_x(p):
        part = w_ref.at[p, pc.z, pc.x, :, mine]
        return spread(p, part, e_send, e_recv, pc.nx, pc.at_x, pieces.at[p])

    def far_y(p):
        part = w_ref.at[p, pc.z, :, :, mine]
        return spread(p, part, f_send, f_recv, pc.ny, pc.at_y)

    def ring(p, k):
        part = w_ref.at[p, pc.z_of((pc.nz - k + 1) % pc.nz), :, :, core_half]
        return [remote(part, part, z_send.at[p, k - 1], z_recv.at[p, k - 1], pc.at_z(1))]

    def to_core(p):
        part = w_ref.at[p, :, :, :, core_half]
        return [remote(part, part, c_send.at[p], c_recv.at[p], pc.at_core())]

    def into_vmem(p):
        return pltpu.make_async_copy(w_ref.at[p], wf.at[p], w_sem.at[p])

    for r in range(rows):
        at = pl.ds(r * length, length)
        tall = jnp.concatenate(
            [codes_ref[r].astype(float_out), jnp.zeros((128 - LEVELS, length), float_out)], axis=0
        )
        code_cols[at] = tall.T.astype(jnp.int32)
        seg_col[pl.ds(r * length, length)] = column_of(segs_ref[r : r + 1])
        phone_col[pl.ds(r * length, length)] = column_of(phones_ref[r : r + 1])
        starts = [
            jnp.sum(jnp.where(segs_ref[r : r + 1] < k, 1.0, 0.0), axis=1, keepdims=True)
            for k in (0, 1, 2)
        ]
        angle = jnp.concatenate(starts, axis=0) * rate_ref[...]
        odd = lax.broadcasted_iota(jnp.int32, angle.shape, 1) % 2
        starts_ref[r, 0:3] = jnp.cos(angle)
        starts_ref[r, 3:6] = jnp.where(odd == 1, 1.0, -1.0) * jnp.sin(angle)

    def chunk(i):
        return pl.ds(i * ROWS_AT_ONCE, ROWS_AT_ONCE)

    def embed_out(i):
        made = ((multi, multi_out), (hot, hot_out), (x0, x_out), (h1, h_out))
        return [
            pltpu.make_async_copy(a.at[chunk(i)], b.at[chunk(i)], out_sem.at[i, n])
            for n, (a, b) in enumerate(made)
        ]

    def qkv_copy(n):
        return pltpu.make_async_copy(pool.at[n], qkv_out.at[n], qkv_sem.at[n])

    def weight(first, count=2):
        return wf[first : first + count].reshape(count * D // 2, D)

    def prepare_step(i):
        at = chunk(i)
        r, local = i // steps, pl.ds((i % steps) * ROWS_AT_ONCE, ROWS_AT_ONCE)
        vocab = lax.broadcasted_iota(jnp.int32, (ROWS_AT_ONCE, CODES), 1)
        count = jnp.zeros((ROWS_AT_ONCE, CODES), jnp.float32)
        for level in range(LEVELS):
            code = code_cols[at, level : level + 1]
            code = jnp.where(ids_ref[0, r] >= level, code, -1)
            count = count + jnp.where(code == vocab, 1.0, 0.0)
        multi[at] = count.astype(low)
        names = lax.broadcasted_iota(jnp.int32, (ROWS_AT_ONCE, PHONES), 1)
        hot[at] = jnp.where(phone_col[at] == names, 1.0, 0.0).astype(low)
        segs = seg_col[at]
        cosine, sine = (
            jnp.where(
                segs == 0,
                starts_ref[r, k : k + 1],
                jnp.where(segs == 1, starts_ref[r, k + 1 : k + 2], starts_ref[r, k + 2 : k + 3]),
            )
            for k in (0, 3)
        )
        x0[at] = waves[0, local] * cosine + waves[1, local] * sine

    def embed_step(i):
        at, r = chunk(i), i // steps
        stream = times(multi[at], weight(CODE)) + times(hot[at], weight(PHONE, 1)) + x0[at]
        x0[at] = stream
        normed, _ = normalize(stream)
        h1[at] = (normed * (1.0 + params_ref[r, 0:1]) + params_ref[r, 1:2]).astype(low)
        begin(embed_out(i))

    def project_step(k):
        for r in range(rows):
            made = times(h1[r * length : (r + 1) * length], wf[pl.ds(QKV + 2 * k, 2)].reshape(D, D))
            pool[rows * k + r] = made.astype(low).reshape(pool.shape[1:])
            qkv_copy(rows * k + r).start()

    def row(r):
        return pl.ds(r * length, length)

    def mixed_copy(r):
        return pltpu.make_async_copy(pool.at[3 * rows + r], mixed_out.at[r], mix_sem.at[r])

    def attend_step(n):
        r, h = lax.div(2 * n, pairs), lax.rem(2 * n, pairs)
        same = seg_col[row(r)] == segs_ref[pl.ds(r, 1)]
        at = [pc.columns(h + e, 2 * HD) for e in range(2)]
        outs, stats = attend_pairs(
            same,
            [
                [
                    pool[rows * k + r, :, :, :, columns].reshape(length, 2 * HD)
                    for k in range(3)
                ]
                for columns in at
            ],
        )
        for e in range(2):
            pool[3 * rows + r, :, :, :, at[e]] = outs[e].reshape(*pool.shape[1:4], 2 * HD)
            for k, lse in enumerate(stats[e]):
                lse_ref[r, h + e, k : k + 1] = lse

        @pl.when(h + 2 == pairs)
        def _():
            mixed_copy(r).start()

    def out_weight():
        return pltpu.make_async_copy(w_ref.at[pl.ds(OUT, 2)], wo, o_sem)

    def up_weight():
        return pltpu.make_async_copy(w_ref.at[pl.ds(UP, 8)], wf.at[pl.ds(0, 8)], u_sem)

    def down_weight(p):
        return pltpu.make_async_copy(w_ref.at[p], pool.at[p - DOWN], d_sem.at[p - DOWN])

    def stream_copies(i):
        return [
            pltpu.make_async_copy(x0.at[chunk(i)], x1_out.at[chunk(i)], x1_sem.at[i, 0]),
            pltpu.make_async_copy(h2.at[chunk(i)], h2_out.at[chunk(i)], x1_sem.at[i, 1]),
        ]

    def act_copy(i):
        return pltpu.make_async_copy(
            act.at[:, chunk(i)], act_out.at[:, chunk(i)], act_sem.at[i, 0]
        )

    def slope_copy(i):
        return pltpu.make_async_copy(
            slope.at[i % 2], slope_out.at[:, chunk(i)], act_sem.at[i, 1]
        )

    def out_step(i):
        at, r = chunk(i), i // steps
        for copy in embed_out(i):
            copy.wait()
        depth = pc.nz // steps
        mixed = pool[3 * rows + r, pl.ds(i % steps * depth, depth)].reshape(ROWS_AT_ONCE, D)
        stream = x0[at] + times(mixed, wo[...].reshape(D, D))
        x0[at] = stream
        normed, _ = normalize(stream)
        h2[at] = (normed * (1.0 + params_ref[r, 2:3]) + params_ref[r, 3:4]).astype(low)
        begin(stream_copies(i))

    def up_step(i):
        at = chunk(i)

        @pl.when(i >= 2)
        def _():
            slope_copy(i - 2).wait()

        for g in range(4):
            u = times(h2[at], weight(2 * g))
            cdf = 0.5 + 0.5 * lax.erf(u * math.sqrt(0.5))
            density = jnp.exp(-0.5 * (u * u)) * (1.0 / math.sqrt(2.0 * math.pi))
            act[g, at] = (u * cdf).astype(low)
            slope[i % 2, g] = (cdf + u * density).astype(low)
        begin([act_copy(i), slope_copy(i)])

    def x2_copy(r):
        return pltpu.make_async_copy(x0.at[row(r)], x2_out.at[row(r)], x2_sem.at[r])

    def down_step(g):
        down_weight(DOWN + 2 * g).wait()
        down_weight(DOWN + 2 * g + 1).wait()
        for r in range(rows):
            at = row(r)
            x0[at] = x0[at] + times(act[g, at], pool[2 * g : 2 * g + 2].reshape(D, D))
            if g == 3:
                x2_copy(r).start()

    ahead = 4
    hops = pc.nz - 1
    embed_steps = rows * steps
    lands = [
        p + (2 * hops + 1 if p % LONG_EVERY == LONG_OUT else 6) for p in range(blocks)
    ]
    embed_from = max(lands[:QKV]) + 1
    project_from = max(
        embed_from + embed_steps,
        *(max(lands[QKV + 2 * k : QKV + 2 * k + 2]) + 1 - k for k in range(3)),
    )
    attend_from = project_from + 3
    out_from = max(attend_from + rows * pairs // 2, max(lands[OUT:UP]) + 2)
    out_ticks = embed_steps // 2
    up_fetch = max(max(lands[UP:DOWN]) + 1, attend_from)
    up_from = max(out_from + out_ticks, up_fetch + 1)
    free_at = out_from + out_ticks
    direct = max([p + 1 for p in range(DOWN, HEAD) if lands[p] < free_at], default=DOWN)
    copied = {p: max(lands[p], free_at if p < direct else 0) for p in range(DOWN, HEAD)}
    down_at = []
    for g in range(4):
        landed_by = max(copied[DOWN + 2 * g], copied[DOWN + 2 * g + 1]) + 1
        after = down_at[-1] + 1 if down_at else up_from + embed_steps
        down_at.append(max(landed_by, after))

    def step(p, body):
        pl.when(within(p, blocks))(lambda: body(p))

    def launch(p):
        own(p).start()
        by_kind(p, LONG_OUT, lambda: begin(along_z(p)), lambda: begin(far_x(p)))

    def far_second(p):
        def far():
            own(p).wait()
            landed_all(far_x(p))
            begin(far_y(p))

        by_kind(p, LONG_OUT, far=far)

    def first(p):
        def near():
            own(p).wait()
            landed_all(along_z(p))
            begin(first_x(p) + first_y(p))

        def far():
            landed_all(far_y(p))
            begin(ring(p, 1))

        by_kind(p, LONG_OUT, near, far)

    def ring_on(k):
        def body(p):
            def far():
                landed_all(ring(p, k - 1))
                begin(ring(p, k))

            by_kind(p, LONG_OUT, far=far)

        return body

    def then(p):
        def near():
            landed_all(first_x(p))
            begin(then_y(p))
            landed_all(first_y(p))
            begin(then_x(p))

        by_kind(p, LONG_OUT, near)

    def core_near(p):
        def near():
            landed_all(then_y(p) + then_x(p))
            begin(to_core(p))

        by_kind(p, LONG_OUT, near)

    def core_far(p):
        def far():
            landed_all(ring(p, hops))
            begin(to_core(p))

        by_kind(p, LONG_OUT, far=far)

    def arrived(p):
        landed_all(to_core(p))

        @pl.when(p < FRONT)
        def _():
            into_vmem(p).start()

        @pl.when((p >= direct) & (p < HEAD))
        def _():
            down_weight(p).start()

    sent_after = 2 * hops + 4

    def sent_off(p):
        gone(to_core(p))

        def near():
            gone(along_z(p) + first_x(p) + first_y(p) + then_y(p) + then_x(p))

        def far():
            gone(far_x(p) + far_y(p))
            for k in range(1, pc.nz):
                gone(ring(p, k))

        by_kind(p, LONG_OUT, near, far)

    def tick(turn, carry):
        t = turn - ahead
        for m in range(len(cuts) - 1):
            pl.when(turn == cuts[m])(functools.partial(take_pieces, m))
        step(turn, launch)
        step(t + 2, far_second)
        step(t, first)
        step(t - 2, then)
        for k in range(2, pc.nz):
            step(t - 2 * (k - 1), ring_on(k))
        step(t - 5, core_near)
        step(t - 2 * hops, core_far)
        step(t - 6, lambda p: by_kind(p, LONG_OUT, lambda: arrived(p)))
        step(t - 2 * hops - 1, lambda p: by_kind(p, LONG_OUT, far=lambda: arrived(p)))
        for p in range(DOWN, direct):
            pl.when(t == copied[p])(down_weight(p).start)

        for stage, (start, end) in enumerate(small):
            pl.when(turn == ahead + 1 + 2 * stage)(start)
            pl.when(turn == ahead + 2 + 2 * stage)(end)
        pl.when(turn == ahead + 7)(set_params)

        @pl.when(t == 0)
        def _():
            loads[1].wait()
            loads[2].wait()

        @pl.when(within(t, embed_steps))
        def _():
            prepare_step(t)

        @pl.when(t == embed_from)
        def _():
            for p in range(QKV):
                into_vmem(p).wait()

        @pl.when(within(t - embed_from, embed_steps))
        def _():
            embed_step(t - embed_from)

        @pl.when(within(t - project_from, 3))
        def _():
            k = t - project_from
            into_vmem(QKV + 2 * k).wait()
            into_vmem(QKV + 2 * k + 1).wait()
            project_step(k)

        @pl.when(within(t - attend_from, rows * pairs // 2))
        def _():
            attend_step(t - attend_from)

        @pl.when(t == out_from - 1)
        def _():
            out_weight().start()

        @pl.when(t == up_fetch)
        def _():
            up_weight().start()

        @pl.when(t == out_from)
        def _():
            out_weight().wait()
            for n in range(3 * rows):
                qkv_copy(n).wait()

        @pl.when(within(t - out_from, out_ticks))
        def _():
            out_step(2 * (t - out_from))
            out_step(2 * (t - out_from) + 1)

        @pl.when(t == out_from + out_ticks - 1)
        def _():
            for r in range(rows):
                mixed_copy(r).wait()

        @pl.when(t == up_from)
        def _():
            up_weight().wait()

        @pl.when(within(t - up_from, embed_steps))
        def _():
            up_step(t - up_from)

        for g in range(4):

            @pl.when(t == down_at[g])
            def _(g=g):
                if g == 0:
                    for i in range(embed_steps):
                        for copy in stream_copies(i):
                            copy.wait()
                down_step(g)

        step(t - sent_after, sent_off)
        return carry

    last = max(blocks + 6, blocks + 2 * hops, down_at[-1] + 1)
    lax.fori_loop(0, last + ahead, tick, 0)

    def finish(p, carry):
        sent_off(p)
        return carry

    lax.fori_loop(last - sent_after, blocks, finish, 0)
    for i in range(embed_steps):
        act_copy(i).wait()
    for i in range(embed_steps - 2, embed_steps):
        slope_copy(i).wait()
    for r in range(rows):
        x2_copy(r).wait()


def like(shape, dtype=low):
    return jax.ShapeDtypeStruct(shape, dtype)


def front(pc, owners, ids, masters, table, codes, phones, segments):
    per_group, piece, _ = masters.shape
    rows, length = segments.shape
    total = rows * length
    rate = jnp.asarray(rates()[1][None], jnp.float32)
    own_sections = table.shape[0]
    hops = pc.nx - 1 + pc.ny - 1
    same, other = index_waves(length)
    small = pc.small_slots()
    embed_steps = total // ROWS_AT_ONCE
    cuts = rank_cuts(per_group)
    dma = pltpu.SemaphoreType.DMA
    vmem = pl.BlockSpec(memory_space=pltpu.VMEM)
    smem = pl.BlockSpec(memory_space=pltpu.SMEM)
    far = pl.BlockSpec(memory_space=pl.ANY)
    return pl.pallas_call(
        functools.partial(front_kernel, pc),
        out_shape=(
            like((BLOCKS, pc.nz, pc.nx, piece, D)),
            like((rows, 8, D), float_out),
            like((total, CODES)),
            like((total, PHONES)),
            like((total, D), float_out),
            like((total, D)),
            like((3 * rows, pc.nz, pc.nx, piece, D)),
            like((rows, pc.nz, pc.nx, piece, D)),
            like((rows, HEADS // 2, 2, length), float_out),
            like((total, D), float_out),
            like((total, D)),
            like((4, total, D)),
            like((4, total, D)),
            like((total, D), float_out),
        ),
        in_specs=[smem, smem, far] + [vmem] * 5 + [far, far],
        out_specs=(far, vmem, far, far, far, far, far, far, vmem, far, far, far, far, far),
        scratch_shapes=[
            pltpu.VMEM((own_sections, 8, D), float_out),
            pltpu.VMEM((total, 1), jnp.int32),
            pltpu.VMEM((total, 1), jnp.int32),
            pltpu.VMEM((total, 128), jnp.int32),
            pltpu.VMEM((rows, 8, D), float_out),
            pltpu.VMEM((2, length, D), float_out),
            pltpu.VMEM((per_group, piece, D), low),
            pltpu.VMEM((per_group, piece, D), low),
            pltpu.VMEM((SECTIONS, 128), float_out),
            *(
                pltpu.VMEM((pc.groups, b - a, piece, pc.panel), low)
                for a, b in zip(cuts[:-1], cuts[1:], strict=True)
            ),
            pltpu.VMEM((BLOCKS, piece, pc.panel), low),
            pltpu.VMEM((own_sections * pc.groups, 8, D), float_out),
            pltpu.VMEM((FRONT, pc.nz, pc.nx, piece, D), low),
            pltpu.VMEM((total, CODES), low),
            pltpu.VMEM((total, PHONES), low),
            pltpu.VMEM((total, D), float_out),
            pltpu.VMEM((total, D), low),
            pltpu.VMEM((max(4 * rows, 8), pc.nz, pc.nx, piece, D), low),
            pltpu.VMEM((2, pc.nz, pc.nx, piece, D), low),
            pltpu.VMEM((total, D), low),
            pltpu.VMEM((4, total, D), low),
            pltpu.VMEM((2, 4, ROWS_AT_ONCE, D), low),
            pltpu.VMEM((2, 8, 128), float_out),
            pltpu.VMEM((small, 8, 128), float_out),
            pltpu.SMEM((BLOCKS,), jnp.int32),
            dma((3,)),
            dma((3, pc.groups - 1)),
            dma((3, pc.groups - 1)),
            dma((pc.groups - 1,)),
            dma((pc.groups - 1,)),
            dma((BLOCKS,)),
            dma((BLOCKS, pc.nz - 1)),
            dma((BLOCKS, pc.nz - 1)),
            dma((BLOCKS, hops)),
            dma((BLOCKS, hops)),
            dma((BLOCKS, hops)),
            dma((BLOCKS, hops)),
            dma((BLOCKS,)),
            dma((BLOCKS,)),
            dma((small,)),
            dma((small,)),
            dma((FRONT,)),
            dma((embed_steps, 4)),
            dma((3 * rows,)),
            dma((rows,)),
            dma,
            dma,
            dma((8,)),
            dma((embed_steps, 2)),
            dma((embed_steps, 2)),
            dma((rows,)),
        ],
        name="front",
        compiler_params=pltpu.CompilerParams(
            collective_id=0, has_side_effects=True, vmem_limit_bytes=62 * MIB
        ),
    )(owners, ids, masters.reshape(-1, D), table, codes, phones, segments, rate, same, other)


FAR = ("h3", "act", "h2", "mixed", "h1", "multi", "hot", "dlogits", "dffn", "du", "dattn")


HOME = (
    (0, 2, "h3", "dlogits"),
    (2, 8, "act", "dffn"),
    (10, 8, "h2", "du"),
    (18, 2, "mixed", "dattn"),
    (20, 6, "h1", "dqkv"),
    (26, 2, "multi", "demb"),
    (28, 1, "hot", "demb"),
)


def back_kernel(pc, *refs):
    held = dict(zip(FAR, refs[2 : 2 + len(FAR)], strict=True))
    owners_ref, ids_ref = refs[:2]
    (
        qkv_ref,
        do_ref,
        x0_ref,
        dx_ref,
        w_ref,
        lse_ref,
        segs_ref,
        params_ref,
        rows_ref,
        loss_ref,
        out_ref,
        table_out,
        sums_out,
        seg_col,
        block_of_ref,
        key_ref,
        rank_ref,
        arrived,
        sums_ref,
        x_buf,
        y_buf,
        own_half,
        send_half,
        core_in,
        first_a,
        first_b,
        then_in,
        z_in,
        far_z,
        far_yx,
        far_in,
        final,
        by_slot,
        square,
        heads,
        dqkv,
        demb,
        qkv_w,
        chunks,
        row_sums,
        table_mine,
        table_in,
        table_mid,
        sent,
        landed,
        in_sem,
        head_sem,
        chunk_sem,
        w_sem,
        free_sem,
        c_send,
        c_recv,
        e_send,
        e_recv,
        f_send,
        f_recv,
        z_send,
        z_recv,
        a_send,
        a_recv,
        t_send,
        t_recv,
        m_send,
        m_recv,
    ) = refs[2 + len(FAR) :]
    held["dqkv"], held["demb"] = dqkv, demb
    pc.here()
    blocks = BLOCKS
    per_group = out_ref.shape[0]
    own_sections = table_out.shape[0]
    rows, length = segs_ref.shape
    pairs = HEADS // 2
    steps = length // ROWS_AT_ONCE
    attend_steps, embed_steps = rows * pairs, rows * steps
    width = x_buf.shape[2]
    keep = pc.columns(pc.c, pc.half)
    away = pc.columns(1 - pc.c, pc.half)
    core_slots = core_in.shape[0]
    hops = pc.nz - 1
    release = 2 * pc.nz - 1

    def fetch(t):
        for from_, count, xs, ys in HOME:
            u = t - from_

            @pl.when(within(u, count))
            def _(xs=xs, ys=ys, u=u):
                slot = lax.rem(t, 2)
                x_ref, y_ref = held[xs], held[ys]
                columns = pc.columns(lax.rem(u, 2), width)
                x_src = x_ref.at[lax.div(u, 2), :, columns] if len(x_ref.shape) == 3 else x_ref.at[:, columns]
                y_src = y_ref.at[lax.div(u, 2)] if len(y_ref.shape) == 3 else y_ref
                pltpu.make_async_copy(x_src, x_buf.at[slot], in_sem.at[slot, 0]).start()
                pltpu.make_async_copy(y_src, y_buf.at[slot], in_sem.at[slot, 1]).start()

    def fetched(slot):
        for n, buf in enumerate((x_buf, y_buf)):
            pltpu.make_async_copy(buf.at[slot], buf.at[slot], in_sem.at[slot, n]).wait()

    def head_copies(n):
        r, h, slot = n // pairs, n % pairs, n % 2
        at, columns = pl.ds(r * length, length), pc.columns(h, 2 * HD)
        copies = [
            pltpu.make_async_copy(
                qkv_ref.at[k, at, columns], heads.at[slot, k], head_sem.at[slot, k]
            )
            for k in range(3)
        ]
        copies.append(
            pltpu.make_async_copy(do_ref.at[at, columns], heads.at[slot, 3], head_sem.at[slot, 3])
        )
        return copies

    def chunk(i):
        return pl.ds(i * ROWS_AT_ONCE, ROWS_AT_ONCE)

    def chunk_copies(i):
        slot = i % 2
        return [
            pltpu.make_async_copy(x0_ref.at[chunk(i)], chunks.at[slot, 0], chunk_sem.at[slot, 0]),
            pltpu.make_async_copy(dx_ref.at[chunk(i)], chunks.at[slot, 1], chunk_sem.at[slot, 1]),
        ]

    weight_copy = pltpu.make_async_copy(w_ref.at[pl.ds(QKV, 6)], qkv_w, w_sem)

    def attend_back_step(n):
        r, h, slot = n // pairs, n % pairs, n % 2
        at, columns = pl.ds(r * length, length), pc.columns(h, 2 * HD)
        same = seg_col[at] == segs_ref[pl.ds(r, 1)]
        stats = [lse_ref[r, h, k : k + 1] for k in range(2)]
        made = attend_pair_back(same, *(heads[slot, k] for k in range(4)), stats)
        for k in range(3):
            dqkv[k, at, columns] = made[k]

    def embed_back_step(i):
        for copy in chunk_copies(i):
            copy.wait()
        r, slot = i // steps, i % 2
        dh = 0.0
        for k in range(3):
            dh = dh + times_t(
                dqkv[k, chunk(i)], qkv_w[2 * k : 2 * k + 2].reshape(D, D)
            )
        normed, scale = normalize(chunks[slot, 0])
        dx, gain, shift = norm_back(dh, normed, scale, params_ref[r, 0:1])
        demb[chunk(i)] = (chunks[slot, 1] + dx).astype(low)
        row_sums[r, 0:2] += jnp.concatenate([gain, shift], axis=0)

    def to_core(b):
        return [
            remote(
                send_half.at[lax.rem(b, 4)],
                core_in.at[lax.rem(b, core_slots)],
                c_send.at[b],
                c_recv.at[b],
                pc.at_core(),
            )
        ]

    middle_z = pc.nz // 2
    lower, upper = slice(0, middle_z), slice(middle_z, pc.nz)
    lower_at, upper_at = pl.ds(0, middle_z), pl.ds(middle_z, pc.nz - middle_z)

    def first_x(b):
        return [
            remote(
                core_in.at[lax.rem(b, core_slots), lower_at, pc.x_of(d)],
                first_a.at[place_among(b), d - 1],
                e_send.at[b, d - 1],
                e_recv.at[b, d - 1],
                pc.at_x(d),
            )
            for d in range(1, pc.nx)
        ]

    def first_y(b):
        return [
            remote(
                core_in.at[
                    lax.rem(b, core_slots), upper_at, :, :, pc.columns(pc.y_of(d), pc.panel)
                ],
                first_b.at[place_among(b), d - 1],
                e_send.at[b, pc.nx - 1 + d - 1],
                e_recv.at[b, pc.nx - 1 + d - 1],
                pc.at_y(d),
            )
            for d in range(1, pc.ny)
        ]

    def then_y(b):
        return [
            remote(
                first_a.at[place_among(b), 0, :, :, pc.columns(pc.y_of(d), pc.panel)],
                then_in.at[place_among(b), d - 1, lower_at],
                f_send.at[b, d - 1],
                f_recv.at[b, d - 1],
                pc.at_y(d),
            )
            for d in range(1, pc.ny)
        ]

    def then_x(b):
        return [
            remote(
                first_b.at[place_among(b), 0, :, pc.x_of(d)],
                then_in.at[place_among(b), d - 1, upper_at],
                f_send.at[b, pc.ny - 1 + d - 1],
                f_recv.at[b, pc.ny - 1 + d - 1],
                pc.at_x(d),
            )
            for d in range(1, pc.nx)
        ]

    def along_z(b):
        return [
            remote(
                then_in.at[place_among(b), 0, pc.z_of(d)],
                z_in.at[place_among(b), d - 1],
                z_send.at[b, d - 1],
                z_recv.at[b, d - 1],
                pc.at_z(d),
            )
            for d in range(1, pc.nz)
        ]

    def ring(b, k):
        n = lax.div(b, LONG_EVERY)
        source = (
            core_in.at[lax.rem(b, core_slots), pc.z_of(hops)] if k == 1 else far_z.at[n, k - 2]
        )
        return [
            remote(source, far_z.at[n, k - 1], z_send.at[b, k - 1], z_recv.at[b, k - 1], pc.at_z(1))
        ]

    def far_y(b):
        n = lax.div(b, LONG_EVERY)
        return [
            remote(
                far_z.at[n, hops - 1, :, :, pc.columns(pc.y_of(d), pc.panel)],
                far_yx.at[n, d - 1],
                f_send.at[b, d - 1],
                f_recv.at[b, d - 1],
                pc.at_y(d),
            )
            for d in range(1, pc.ny)
        ]

    def far_x(b):
        n = lax.div(b, LONG_EVERY)
        return [
            remote(
                far_yx.at[n, 0, pc.x_of(d)],
                far_in.at[n, d - 1],
                e_send.at[b, d - 1],
                e_recv.at[b, d - 1],
                pc.at_x(d),
            )
            for d in range(1, pc.nx)
        ]

    def summed(own, landed_ref, index, count):
        total = own.astype(float_out)
        for d in range(count - 1):
            total = total + landed_ref[index, d].astype(float_out)
        return total

    def table_stage():
        return [
            remote(
                table_mine.at[pl.ds(pc.section_peer(d) * own_sections, own_sections)],
                table_in.at[d - 1],
                t_send.at[d - 1],
                t_recv.at[d - 1],
                (pc.section_peer(d), pc.j),
            )
            for d in range(1, pc.groups)
        ]

    def table_hop(stage):
        count, target = ((pc.nx, pc.at_x), (pc.nz, pc.at_z))[stage]
        first = pc.groups - 1 + stage * (pc.nx - 1)
        return [
            remote(
                table_mid.at[stage],
                table_in.at[first + d - 1],
                t_send.at[first + d - 1],
                t_recv.at[first + d - 1],
                target(d),
            )
            for d in range(1, count)
        ]

    def table_landed(copies, own, first):
        for copy in copies:
            copy.wait()
        total = own
        for n in range(len(copies)):
            total = total + table_in[first + n]
        return total

    def table_after_section():
        own = table_mine[pl.ds(pc.s * own_sections, own_sections)]
        table_mid[0] = table_landed(table_stage(), own, 0)
        begin(table_hop(0))

    def table_after_x():
        table_mid[1] = table_landed(table_hop(0), table_mid[0], pc.groups - 1)
        begin(table_hop(1))

    def table_after_z():
        first = pc.groups - 1 + pc.nx - 1
        table_out[...] = table_landed(table_hop(1), table_mid[1], first)

    fetch(0)
    begin(head_copies(0))
    weight_copy.start()
    pc.barrier()
    square[...] = jnp.zeros_like(square)
    final[blocks] = jnp.zeros(final.shape[1:], low)
    row_sums[...] = rows_ref[...]
    for r in range(rows):
        seg_col[pl.ds(r * length, length)] = column_of(segs_ref[r : r + 1])

    base = pc.s * per_group

    def rank_blocks():
        keys = rank_keys(owners_ref, HOMEWARD[::-1], per_group, pc.groups)[::-1]
        for b in range(blocks):
            key_ref[b] = keys[b]
        for i in range(per_group):
            rank = jnp.int32(per_group)
            for b in range(blocks):
                rank = jnp.where(owners_ref[HOMEWARD[b]] == base + i, keys[b] - base, rank)
            rank_ref[i] = rank

        def find(i, carry):
            where = jnp.int32(blocks)
            for b in range(blocks):
                where = jnp.where(key_ref[b] == i, b, where)
            block_of_ref[i] = where
            return carry

        lax.fori_loop(0, per_group * pc.groups, find, 0)

    arrived[:, per_group] = jnp.zeros((pc.groups, *arrived.shape[2:]), low)
    early = per_group // 4
    panel = pc.panel_of(pc.s)

    def exchange(m):
        ranks = pl.ds(early, per_group - early) if m == 0 else pl.ds(0, early)
        return [
            remote(
                by_slot.at[pc.section_peer(d), ranks],
                arrived.at[panel, ranks],
                a_send.at[m, d - 1],
                a_recv.at[m, d - 1],
                (pc.section_peer(d), pc.j),
            )
            for d in range(1, pc.groups)
        ]

    def send_ranks(m):
        for k in range(early, per_group) if m == 0 else range(early):
            for g in range(pc.groups):
                where = jnp.clip(block_of_ref[g * per_group + k], 0, blocks)
                by_slot[g, k] = final[where]
            arrived[panel, k] = by_slot[pc.s, k]
        begin(exchange(m))

    def step(b, body):
        pl.when(within(b, blocks))(lambda: body(b))

    def first(b):
        landed_all(to_core(b))
        at = lax.rem(b, core_slots)
        core_in[at] = (
            core_in[at].astype(float_out) + own_half[lax.rem(b, 2)].reshape(core_in.shape[1:])
        ).astype(low)
        by_kind(
            b,
            LONG_HOME,
            lambda: begin(first_x(b) + first_y(b)),
            lambda: begin(ring(b, 1)),
        )

    def then(b):
        at, n = lax.rem(b, core_slots), place_among(b)

        def near():
            landed_all(first_x(b))
            first_a[n, 0] = summed(core_in[at, lower, pc.x], first_a, n, pc.nx).astype(low)
            begin(then_y(b))
            landed_all(first_y(b))
            mine = pc.columns(pc.y, pc.panel)
            first_b[n, 0] = summed(
                core_in[at, upper, :, :, mine], first_b, n, pc.ny
            ).astype(low)
            begin(then_x(b))

        by_kind(b, LONG_HOME, near)

    def ring_on(k):
        def body(b):
            def far():
                landed_all(ring(b, k))
                n, held_for = lax.div(b, LONG_EVERY), pc.z_of((2 * pc.nz - 1 - k) % pc.nz)
                far_z[n, k - 1] = (
                    far_z[n, k - 1].astype(float_out)
                    + core_in[lax.rem(b, core_slots), held_for].astype(float_out)
                ).astype(low)
                begin(ring(b, k + 1) if k < hops else far_y(b))

            by_kind(b, LONG_HOME, far=far)

        return body

    def third(b):
        n = place_among(b)

        def near():
            landed_all(then_y(b))
            total = first_a[n, 0, :, :, pc.columns(pc.y, pc.panel)].astype(float_out)
            for d in range(pc.ny - 1):
                total = total + then_in[n, d, lower].astype(float_out)
            then_in[n, 0, lower] = total.astype(low)
            landed_all(then_x(b))
            total = first_b[n, 0, :, pc.x].astype(float_out)
            for d in range(pc.nx - 1):
                total = total + then_in[n, d, upper].astype(float_out)
            then_in[n, 0, upper] = total.astype(low)
            begin(along_z(b))

        by_kind(b, LONG_HOME, near)

    def far_third(b):
        def far():
            landed_all(far_y(b))
            n, mine = lax.div(b, LONG_EVERY), pc.columns(pc.y, pc.panel)
            far_yx[n, 0] = summed(far_z[n, hops - 1, :, :, mine], far_yx, n, pc.ny).astype(low)
            begin(far_x(b))

        by_kind(b, LONG_HOME, far=far)

    def let_go(b):
        by_kind(
            b,
            LONG_HOME,
            lambda: gone(first_x(b) + first_y(b)),
            lambda: gone(ring(b, 1)),
        )

        @pl.when(b < blocks - core_slots)
        def _():
            pl.semaphore_signal(free_sem, inc=1, device_id=pc.at_core(), device_id_type=MESH)

    def settle(b, total):
        rounded = total.astype(low)
        final[b] = rounded
        wide = rounded.astype(float_out)
        square[...] += jnp.sum(wide * wide, axis=0, keepdims=True)

    def close(b):
        n = place_among(b)

        def near():
            landed_all(along_z(b))
            settle(b, summed(then_in[n, 0, pc.z], z_in, n, pc.nz))

        by_kind(b, LONG_HOME, near)

    def far_close(b):
        def far():
            landed_all(far_x(b))
            n = lax.div(b, LONG_EVERY)
            settle(b, summed(far_yx[n, 0, pc.x], far_in, n, pc.nx))

        by_kind(b, LONG_HOME, far=far)

    def sent_off(b):
        def far():
            for k in range(2, pc.nz):
                gone(ring(b, k))
            gone(far_y(b) + far_x(b))

        by_kind(
            b,
            LONG_HOME,
            lambda: gone(then_y(b) + then_x(b) + along_z(b)),
            far,
        )

    early_at = 1 + max(
        b + (release + 4 if b % LONG_EVERY == LONG_HOME else 7) for b in range(blocks - early)
    )

    def weigh(t):
        slot = lax.rem(t, 2)
        send_half[lax.rem(t, 4)] = (
            turned_times(x_buf[slot], y_buf[slot, :, away])
            .astype(low)
            .reshape(send_half.shape[1:])
        )
        own_half[slot] = turned_times(x_buf[slot], y_buf[slot, :, keep])

    def make_ready(t):
        fetched(lax.rem(t, 2))

        @pl.when(t >= 4)
        def _():
            gone(to_core(t - 4))

    def leave(t):
        @pl.when(t >= core_slots)
        def _():
            pl.semaphore_wait(free_sem, 1)

        begin(to_core(t))

    def serve(t):
        step(t - 1, first)
        step(t - 3, then)
        for k in range(1, pc.nz):
            step(t - 2 * k - 1, ring_on(k))
        step(t - 5, third)
        step(t - release, let_go)
        step(t - release - 2, far_third)
        step(t - 7, close)
        step(t - release - 4, far_close)

    def attending(t, carry):
        fetch(t + 1)

        @pl.when(t + 1 < attend_steps)
        def _():
            begin(head_copies(t + 1))

        for copy in head_copies(t):
            copy.wait()
        make_ready(t)
        weigh(t)
        attend_back_step(t)
        leave(t)
        serve(t)
        return carry

    def later(t, carry):
        pl.when(t + 1 < blocks)(lambda: fetch(t + 1))
        i = lax.div(t - attend_steps, 2)
        odd = lax.rem(t - attend_steps, 2)

        @pl.when((t < attend_steps + 2 * embed_steps) & (odd == 0))
        def _():
            begin(chunk_copies(i))

        @pl.when(t < blocks)
        def _():
            make_ready(t)
            weigh(t)
            leave(t)

        serve(t)
        pl.when(t == blocks - 2)(rank_blocks)
        pl.when(t == early_at)(lambda: send_ranks(0))

        @pl.when((t < attend_steps + 2 * embed_steps) & (odd == 1))
        def _():
            @pl.when(t == attend_steps + 1)
            def _():
                weight_copy.wait()

            embed_back_step(i)

        table_at = attend_steps + 2 * embed_steps

        @pl.when(t == table_at)
        def _():
            for section in range(own_sections * pc.groups):
                total = jnp.zeros(row_sums.shape[1:], float_out)
                for r in range(rows):
                    total = total + jnp.where(ids_ref[0, r] == section, row_sums[r], 0.0)
                table_mine[section] = total
            begin(table_stage())

        pl.when(t == table_at + 4)(table_after_section)
        pl.when(t == table_at + 8)(table_after_x)
        for k in range(2):
            b = 2 * (t - table_at) + k
            pl.when((t >= table_at) & (b < sent_in_loop))(functools.partial(sent_off, b))

        return carry

    last_long = LONG_HOME + (LONGS - 1) * LONG_EVERY
    last_tick = attend_steps + 2 * embed_steps + 8
    ticks = max(
        last_tick + 1, blocks + 7, blocks + release, last_long + release + 5, early_at + 1
    )
    sent_in_loop = min(blocks - 7, 2 * (ticks - attend_steps - 2 * embed_steps))
    lax.fori_loop(0, attend_steps, attending, 0)
    lax.fori_loop(attend_steps, ticks, later, 0)

    send_ranks(1)

    table_after_z()
    total = table_out[...]
    table_square = jnp.sum(total * total) / pc.batch
    lane = lax.broadcasted_iota(jnp.int32, (8, 128), 1)
    part = jnp.where(lane == 0, jnp.sum(square[...]) + table_square, loss_ref[...])
    sums_ref[...] = part
    for start, end in pc.small_stages(sums_ref, sent, landed, m_send, m_recv):
        start()
        end()
    sums_out[...] = sums_ref[...]
    for copy in exchange(0) + exchange(1):
        copy.wait()
    for i in range(per_group):
        for q in range(pc.groups):
            rank = jnp.clip(rank_ref[i], 0, per_group)
            out_ref[i, :, q * pc.panel : (q + 1) * pc.panel] = arrived[q, rank]

    for b in range(blocks - 4, blocks):
        gone(to_core(b))

    def finish(b, carry):
        sent_off(b)
        return carry

    lax.fori_loop(sent_in_loop, blocks, finish, 0)


def back(pc, owners, ids, arrays, near, per_group):
    total = arrays[0].shape[0]
    rows, length = near[6].shape
    width = D // 2
    piece = width // pc.batch
    own_sections = SECTIONS // pc.groups
    hops = pc.nx - 1 + pc.ny - 1
    blocks = BLOCKS
    steps, small = pc.table_slots(), pc.small_slots()
    dma = pltpu.SemaphoreType.DMA
    vmem = pl.BlockSpec(memory_space=pltpu.VMEM)
    smem = pl.BlockSpec(memory_space=pltpu.SMEM)
    far = pl.BlockSpec(memory_space=pl.ANY)
    nz, nx, ny, half, panel = pc.nz, pc.nx, pc.ny, pc.half, pc.panel
    return pl.pallas_call(
        functools.partial(back_kernel, pc),
        out_shape=(
            like((per_group, piece, D)),
            like((own_sections, 8, D), float_out),
            like((8, 128), float_out),
        ),
        in_specs=[smem, smem] + [far] * len(arrays) + [far] * 5 + [vmem] * 5,
        out_specs=(vmem, vmem, vmem),
        scratch_shapes=[
            pltpu.VMEM((total, 1), jnp.int32),
            pltpu.SMEM((per_group * pc.groups,), jnp.int32),
            pltpu.SMEM((BLOCKS,), jnp.int32),
            pltpu.SMEM((per_group,), jnp.int32),
            pltpu.VMEM((pc.groups, per_group + 1, piece, panel), low),
            pltpu.VMEM((8, 128), float_out),
            pltpu.VMEM((2, total, width), low),
            pltpu.VMEM((2, total, D), low),
            pltpu.VMEM((2, width, half), float_out),
            pltpu.VMEM((4, nz, nx, piece, half), low),
            pltpu.VMEM((2 * nz + 4, nz, nx, piece, half), low),
            pltpu.VMEM((NEARS, nx - 1, nz // 2, piece, half), low),
            pltpu.VMEM((NEARS, ny - 1, nz - nz // 2, nx, piece, panel), low),
            pltpu.VMEM((NEARS, max(nx, ny) - 1, nz, piece, panel), low),
            pltpu.VMEM((NEARS, nz - 1, piece, panel), low),
            pltpu.VMEM((LONGS, nz - 1, nx, piece, half), low),
            pltpu.VMEM((LONGS, ny - 1, nx, piece, panel), low),
            pltpu.VMEM((LONGS, nx - 1, piece, panel), low),
            pltpu.VMEM((blocks + 1, piece, panel), low),
            pltpu.VMEM((pc.groups, per_group, piece, panel), low),
            pltpu.VMEM((1, panel), float_out),
            pltpu.VMEM((2, 4, length, 2 * HD), low),
            pltpu.VMEM((3, total, D), low),
            pltpu.VMEM((total, D), low),
            pltpu.VMEM((6, nz, nx, piece, D), low),
            pltpu.VMEM((2, 2, ROWS_AT_ONCE, D), float_out),
            pltpu.VMEM((rows, 8, D), float_out),
            pltpu.VMEM((own_sections * pc.groups, 8, D), float_out),
            pltpu.VMEM((steps, own_sections, 8, D), float_out),
            pltpu.VMEM((2, own_sections, 8, D), float_out),
            pltpu.VMEM((2, 8, 128), float_out),
            pltpu.VMEM((small, 8, 128), float_out),
            dma((2, 2)),
            dma((2, 4)),
            dma((2, 2)),
            dma,
            pltpu.SemaphoreType.REGULAR,
            dma((blocks,)),
            dma((blocks,)),
            dma((blocks, hops)),
            dma((blocks, hops)),
            dma((blocks, hops)),
            dma((blocks, hops)),
            dma((blocks, nz - 1)),
            dma((blocks, nz - 1)),
            dma((2, pc.groups - 1)),
            dma((2, pc.groups - 1)),
            dma((steps,)),
            dma((steps,)),
            dma((small,)),
            dma((small,)),
        ],
        name="back",
        compiler_params=pltpu.CompilerParams(
            collective_id=1, has_side_effects=True, vmem_limit_bytes=62 * MIB
        ),
    )(owners, ids, *arrays, *near)


def matrix(ref, first, count=2):
    return ref[first : first + count].reshape(count * ref.shape[1], ref.shape[2])


def row_block(width, count=ROWS_AT_ONCE):
    return pl.BlockSpec((count, width), lambda i: (i, 0))


def plane_block(planes, width=D, count=ROWS_AT_ONCE):
    return pl.BlockSpec((planes, count, width), lambda i: (0, i, 0))


def per_row(steps, height=8):
    return pl.BlockSpec((1, height, D), lambda i: (i // steps, 0, 0))


def compiler(mib):
    return pltpu.CompilerParams(vmem_limit_bytes=mib * MIB)


def cost(flops, reach, deep=0):
    return pl.CostEstimate(flops=flops, bytes_accessed=reach, transcendentals=deep)


def middle_kernel(
    steps,
    slope_ref,
    x1_ref,
    x2_ref,
    params_ref,
    targets_ref,
    w_ref,
    h3_ref,
    dlogits_ref,
    dffn_ref,
    du_ref,
    dattn_ref,
    do_ref,
    dx_ref,
    rows_ref,
    loss_ref,
    out_w,
    up_w,
    down_w,
    head_w,
    sems,
):
    step = pl.program_id(0)
    parts = [(HEAD, head_w, 0)]
    for g in range(4):
        parts += [(DOWN + 2 * g, down_w, 2 * g), (UP + 2 * g, up_w, 2 * g)]
    parts.append((OUT, out_w, 0))
    loads = [
        pltpu.make_async_copy(w_ref.at[pl.ds(first, 2)], dst.at[pl.ds(at, 2)], sems.at[n])
        for n, (first, dst, at) in enumerate(parts)
    ]

    def ready(*numbers):
        @pl.when(step == 0)
        def _():
            for n in numbers:
                loads[n].wait()

    pl.when(step == 0)(lambda: begin(loads))
    par = [params_ref[0, k : k + 1] for k in range(7)]
    n3, scale3 = normalize(x2_ref[...])
    h3 = (n3 * (1.0 + par[4]) + par[5]).astype(low)
    h3_ref[...] = h3
    ready(0)
    logits = times(h3, matrix(head_w, 0))
    top = jnp.max(logits, axis=-1, keepdims=True)
    lse = top + jnp.log(jnp.sum(jnp.exp(logits - top), axis=-1, keepdims=True))
    vocab = lax.broadcasted_iota(jnp.int32, logits.shape, 1)
    wanted = targets_ref[
        pl.ds(step // steps, 1),
        pl.ds(pl.multiple_of(step % steps * ROWS_AT_ONCE, ROWS_AT_ONCE), ROWS_AT_ONCE),
    ]
    picked = column_of(wanted) == vocab
    losses = lse - jnp.sum(jnp.where(picked, logits, 0.0), axis=-1, keepdims=True)
    weight = par[6]
    dlogits = ((jnp.exp(logits - lse) - jnp.where(picked, 1.0, 0.0)) * weight).astype(low)
    dlogits_ref[...] = dlogits
    dh3 = times_t(dlogits, matrix(head_w, 0))
    dx2, gain3, shift3 = norm_back(dh3, n3, scale3, par[4])
    dffn = dx2.astype(low)
    dffn_ref[...] = dffn
    dh2 = 0.0
    for g in range(4):
        ready(1 + 2 * g, 2 + 2 * g)
        du = (times_t(dffn, matrix(down_w, 2 * g)) * slope_ref[g].astype(float_out)).astype(low)
        du_ref[g] = du
        dh2 = dh2 + times_t(du, matrix(up_w, 2 * g))
    n2, scale2 = normalize(x1_ref[...])
    dx1, gain2, shift2 = norm_back(dh2, n2, scale2, par[2])
    dx1 = dx1 + dx2
    dx_ref[...] = dx1
    dattn = dx1.astype(low)
    dattn_ref[...] = dattn
    ready(9)
    do_ref[...] = times_t(dattn, matrix(out_w, 0)).astype(low)
    grads = jnp.concatenate([gain2, shift2, gain3, shift3], axis=0)

    @pl.when(step == 0)
    def _():
        loss_ref[...] = jnp.zeros_like(loss_ref)

    @pl.when(step % steps == 0)
    def _():
        rows_ref[...] = jnp.zeros_like(rows_ref)

    rows_ref[0, 2:6] += grads
    loss_ref[...] += jnp.sum(losses) * weight[:, :128]


def middle(w, slope, x1, x2, params, targets, length):
    total = x1.shape[0]
    steps = length // ROWS_AT_ONCE
    rows = total // length
    return pl.pallas_call(
        functools.partial(middle_kernel, steps),
        grid=(total // ROWS_AT_ONCE,),
        out_shape=(
            like((total, D)),
            like((total, CODES)),
            like((total, D)),
            like((4, total, D)),
            like((total, D)),
            like((total, D)),
            like((total, D), float_out),
            like((rows, 8, D), float_out),
            like((8, 128), float_out),
        ),
        in_specs=[
            plane_block(4),
            row_block(D),
            row_block(D),
            per_row(steps),
            pl.BlockSpec(targets.shape, lambda i: (0, 0)),
            pl.BlockSpec(memory_space=pl.ANY),
        ],
        out_specs=(
            row_block(D),
            row_block(CODES),
            row_block(D),
            plane_block(4),
            row_block(D),
            row_block(D),
            row_block(D),
            per_row(steps),
            pl.BlockSpec((8, 128), lambda i: (0, 0)),
        ),
        scratch_shapes=[
            *(pltpu.VMEM((count, D // 2, D), low) for count in (2, 8, 8, 2)),
            pltpu.SemaphoreType.DMA((10,)),
        ],
        name="middle",
        compiler_params=compiler(62),
        cost_estimate=cost(22 * total * D * D, 60 * MIB, 2 * total * D),
    )(slope, x1, x2, params, targets, w)


def adam(weight, first, second, grad, rate, fixes):
    new_first = beta_one * first + (1.0 - beta_one) * grad
    new_second = beta_two * second + (1.0 - beta_two) * grad * grad
    update = new_first * fixes[0] / (jnp.sqrt(new_second * fixes[1]) + adam_eps)
    return (weight - rate * (update + decay_rate * weight), new_first, new_second)


SLOTS_AT_ONCE = 2


def update_kernel(
    step_ref,
    sums_ref,
    table_grad_ref,
    table_ref,
    table_first_ref,
    table_second_ref,
    grad_ref,
    masters_ref,
    first_ref,
    second_ref,
    new_masters,
    new_first,
    new_second,
    new_table,
    new_table_first,
    new_table_second,
    norm_ref,
    loss_ref,
    grad,
    state,
    made,
    in_sem,
    out_sem,
):
    turns = masters_ref.shape[0] // SLOTS_AT_ONCE

    def part(i):
        return pl.ds(i * SLOTS_AT_ONCE, SLOTS_AT_ONCE)

    def loads(i):
        copies = [pltpu.make_async_copy(grad_ref.at[part(i)], grad.at[part(i)], in_sem.at[i, 3])]
        for n, ref in enumerate((masters_ref, first_ref, second_ref)):
            copies.append(
                pltpu.make_async_copy(ref.at[part(i)], state.at[n, part(i)], in_sem.at[i, n])
            )
        return copies

    def stores(i):
        return [
            pltpu.make_async_copy(made.at[n, part(i)], ref.at[part(i)], out_sem.at[i, n])
            for n, ref in enumerate((new_masters, new_first, new_second))
        ]

    for i in range(turns):
        begin(loads(i))
    step = jnp.full((1, 128), step_ref[0]).astype(float_out)
    fixes = [
        1.0 / (1.0 - jnp.exp(step * math.log(beta)))[:, :1] for beta in (beta_one, beta_two)
    ]
    norm = jnp.sqrt(sums_ref[0:1, 0:1])
    clip = jnp.minimum(1.0, clip_limit / norm)
    norm_ref[...] = norm
    loss_ref[...] = sums_ref[0:1, 1:2]
    for n in range(table_ref.shape[0]):
        for k in range(6):
            at = (slice(n, n + 1), slice(k * D, (k + 1) * D))
            new_table[at], new_table_first[at], new_table_second[at] = adam(
                table_ref[at],
                table_first_ref[at],
                table_second_ref[at],
                table_grad_ref[n, k : k + 1] * clip,
                table_rate,
                fixes,
            )

    def one(i, carry):
        for copy in loads(i):
            copy.wait()
        results = adam(
            state[0, part(i)],
            state[1, part(i)],
            state[2, part(i)],
            grad[part(i)].astype(float_out) * clip,
            learn_rate,
            fixes,
        )
        for n, value in enumerate(results):
            made[n, part(i)] = value
        begin(stores(i))
        return carry

    lax.fori_loop(0, turns, one, 0)
    for i in range(turns):
        for copy in stores(i):
            copy.wait()


def update(step, sums, grad, masters, first, second, table_grad, table, table_first, table_second):
    turns = masters.shape[0] // SLOTS_AT_ONCE
    vmem = pl.BlockSpec(memory_space=pltpu.VMEM)
    far = pl.BlockSpec(memory_space=pl.ANY)
    dma = pltpu.SemaphoreType.DMA
    return pl.pallas_call(
        update_kernel,
        out_shape=(
            *(like(masters.shape, float_out) for _ in range(3)),
            *(like(table.shape, float_out) for _ in range(3)),
            like((1, 1), float_out),
            like((1, 1), float_out),
        ),
        in_specs=[pl.BlockSpec(memory_space=pltpu.SMEM)] + [vmem] * 5 + [far] * 4,
        out_specs=(far, far, far, vmem, vmem, vmem, vmem, vmem),
        scratch_shapes=[
            pltpu.VMEM(grad.shape, low),
            pltpu.VMEM((3, *masters.shape), float_out),
            pltpu.VMEM((3, *masters.shape), float_out),
            dma((turns, 4)),
            dma((turns, 3)),
        ],
        name="update",
        compiler_params=compiler(62),
        cost_estimate=cost(20 * masters.size, 28 * masters.size),
    )(step, sums, table_grad, table, table_first, table_second, grad, masters, first, second)


def per_device(
    pc,
    masters,
    first_moment,
    second_moment,
    section_table,
    table_first,
    table_second,
    owners,
    step_count,
    phones,
    codes,
    segments,
    sections,
    targets,
):
    row_count, length = segments.shape
    ids = sections.reshape(1, row_count)
    blocks, params, multi, phone_hot, x0, h1, qkv, mixed, lse, x1, h2, act, slope, x2 = front(
        pc, owners, ids, masters, section_table, codes.swapaxes(1, 2), phones, segments
    )
    w = blocks.reshape(BLOCKS, D // 2, D)
    qkv = qkv.reshape(3, row_count * length, D)
    mixed = mixed.reshape(row_count * length, D)
    h3, dlogits, dffn, du, dattn, do, dx1, row_sums, loss_part = middle(
        w, slope, x1, x2, params, targets, length
    )
    own_grad, table_grad, sums = back(
        pc,
        owners,
        ids,
        (h3, act, h2, mixed, h1, multi, phone_hot, dlogits, dffn, du, dattn),
        (qkv, do, x0, dx1, blocks, lse, segments, params, row_sums, loss_part),
        masters.shape[0],
    )
    *state, grad_norm, loss = update(
        step_count,
        sums,
        own_grad,
        masters,
        first_moment,
        second_moment,
        table_grad,
        section_table,
        table_first,
        table_second,
    )
    return (*state, grad_norm.reshape(()), loss.reshape(()))


def solution(mesh):
    return jax.shard_map(
        functools.partial(per_device, Place(mesh)),
        mesh=mesh,
        in_specs=(
            P("section", "batch", None),
            P("section", "batch", None),
            P("section", "batch", None),
            P("section", None),
            P("section", None),
            P("section", None),
            P(),
            P(),
            P(("section", "batch"), None),
            P(("section", "batch"), None, None),
            P(("section", "batch"), None),
            P(("section", "batch"), None),
            P(("section", "batch"), None),
        ),
        out_specs=(
            P("section", "batch", None),
            P("section", "batch", None),
            P("section", "batch", None),
            P("section", None),
            P("section", None),
            P("section", None),
            P(),
            P(),
        ),
        check_vma=False,
    )
```
